32 devices in a mesh: ctx: 4 (over y, core), ch: 8 (over z, x).
Axes of the slice: x: 2, y: 2, z: 4, core: 2. Of those that a mesh axis runs over, the one named last changes fastest.
Arguments:
- q_branch: bfloat16 [1, 2048, 8192], P(None, 'ctx', 'ch'), may hold values from -6 to 6
- k_branch: bfloat16 [1, 2048, 8192], P(None, 'ctx', 'ch'), may hold values from -6 to 6
- out_gate: bfloat16 [1, 2048, 8192], P(None, 'ctx', 'ch'), may hold values from -6 to 6
- filters: bfloat16 [512, 2048], P('ch'), may hold values from -1.1 to 1.1
- grad_out: bfloat16 [1, 2048, 8192], P(None, 'ctx', 'ch'), may hold values from -6 to 6
Outputs:
- grad_q: bfloat16 [1, 2048, 8192], P(None, 'ctx', 'ch')
- grad_k: bfloat16 [1, 2048, 8192], P(None, 'ctx', 'ch')
- grad_filters: float32 [512, 2048], P('ch', 'ctx')
The draws below stay inside these ranges and needn't reach their ends.
All inputs are finite; a program needn't handle non-finite values.
Results may differ from the reference program's by a relative error of at most 0.005.
Values may be sent and summed in bfloat16 or wider, within the bound.
No kernel may reach another device: no remote copies, remote signals or barrier semaphores. Data moves between devices by JAX's collectives and lax.ppermute only.
A program may use at most 128 MiB of HBM per device.

```python
import math
import jax
import jax.numpy as jnp
from jax import lax

WIDTH = 8192
GROUP = 16
FILTERS = 512
SEQS = 1
LEN = 2048


def draw_filters(key, part):
    rate_key, noise_key = jax.random.split(jax.random.fold_in(key, 11))
    low_rate = 0.25 / LEN
    high_rate = 1.0 / 32.0
    spread = jax.random.uniform(rate_key, (FILTERS, 1), jnp.float32)
    rates = jnp.exp(jnp.log(low_rate) + spread * (jnp.log(high_rate) - jnp.log(low_rate)))
    noise = jnp.clip(jax.random.normal(noise_key, (FILTERS, LEN), jnp.float32), -4.0, 4.0)
    lag_pos = jnp.arange(LEN, dtype=jnp.float32)[None, :]
    amplitude = jnp.sqrt(2.0 * rates + 1.0 / LEN)
    return (noise * jnp.exp(-rates * lag_pos) * amplitude).astype(jnp.bfloat16)


def block_scale(rng, extent, cuts, least, high):
    def one(dim, shards_of):
        heights = jax.random.uniform(jax.random.fold_in(jax.random.fold_in(rng, 6), dim), (shards_of,), jnp.float32, least / len(cuts), high / len(cuts))
        return jnp.repeat(jnp.exp(heights), extent[dim] // shards_of).reshape((-1,) + (1,) * (len(extent) - dim - 1))

    factor_of = one(*cuts[0])
    for cut in cuts[1:]:
        factor_of = factor_of * one(*cut)
    return factor_of


def gaussian(stream_key, dims, deviation, limit, cuts=(), kind=jnp.bfloat16):
    loudness = block_scale(stream_key, dims, cuts, -0.22, 0.18) if cuts else 1.0
    values = jax.random.normal(stream_key, dims, jnp.float32) * deviation * loudness
    return jnp.minimum(jnp.maximum(values, -limit), limit).astype(kind)


def setup_inputs(seed: int = 0) -> dict:
    arg_keys = jax.random.split(jax.random.key(seed), 6)
    q_branch = gaussian(arg_keys[0], (SEQS, LEN, WIDTH), 1.0, 6.0, ((1, 4), (2, 8)))
    k_branch = gaussian(arg_keys[1], (SEQS, LEN, WIDTH), 1.0, 6.0, ((1, 4), (2, 8)))
    out_gate = gaussian(arg_keys[2], (SEQS, LEN, WIDTH), 1.0, 6.0, ((1, 4), (2, 8)))
    filters = draw_filters(jax.random.fold_in(arg_keys[5], 71), 0)
    grad_out = gaussian(arg_keys[4], (SEQS, LEN, WIDTH), 1.0, 6.0, ((1, 4), (2, 8)))
    return {"q_branch": q_branch, "k_branch": k_branch, "out_gate": out_gate, "filters": filters, "grad_out": grad_out}


def group_terms(pieces):
    grad_g, prod_g, taps = pieces
    grad_g = grad_g.astype(jnp.float32)
    prod_g = prod_g.astype(jnp.float32)
    taps = taps.astype(jnp.float32)
    span = 2 * LEN
    grad_f = jnp.fft.rfft(grad_g, n=span, axis=1)
    prod_f = jnp.fft.rfft(prod_g, n=span, axis=1)
    taps_f = jnp.fft.rfft(taps, n=span)
    grad_v = jnp.fft.irfft(jnp.conj(taps_f)[None, :, None] * grad_f, n=span, axis=1)[:, :LEN]
    lag_f = lax.optimization_barrier(jnp.sum(jnp.conj(prod_f) * grad_f, axis=(0, 2)))
    lag_grad = jnp.fft.irfft(lag_f, n=span)[:LEN]
    return (grad_v.astype(jnp.float32), lag_grad.astype(jnp.float32))

def reference(q_branch, k_branch, out_gate, filters, grad_out):
    gated_grad = (grad_out.astype(jnp.float32) * out_gate.astype(jnp.float32)).astype(jnp.bfloat16)
    prod = (q_branch.astype(jnp.float32) * k_branch.astype(jnp.float32)).astype(jnp.bfloat16)

    def by_group(values):
        return jnp.transpose(values.reshape(SEQS, LEN, FILTERS, GROUP), (2, 0, 1, 3))
    grad_v, lag_grad = lax.map(group_terms, (by_group(gated_grad), by_group(prod), filters))
    grad_prod = jnp.transpose(grad_v, (1, 2, 0, 3)).reshape(SEQS, LEN, WIDTH)
    grad_q = (grad_prod * k_branch.astype(jnp.float32)).astype(jnp.bfloat16)
    grad_k = (grad_prod * q_branch.astype(jnp.float32)).astype(jnp.bfloat16)
    raw = lag_grad * (4.0 / math.sqrt(SEQS * GROUP))
    squares = jnp.sum(raw * raw)
    factor = jnp.minimum(1.0, math.sqrt(FILTERS * LEN) / jnp.sqrt(squares + 1e-06))
    return (grad_q, grad_k, raw * factor)
```

```python
import functools
import math

import jax
import jax.numpy as jnp
from jax import lax
from jax.experimental import pallas as pl
from jax.experimental.pallas import tpu as pltpu
from jax.sharding import PartitionSpec as P

WIDTH = 8192
GROUP = 16
LANES = 128
NT = (((1,), (1,)), ((), ()))


def gate_kernel(q_ref, k_ref, gate_ref, grad_ref, out_ref):
    groups = out_ref.shape[0]
    pairs = ((grad_ref, gate_ref), (q_ref, k_ref))
    for slot, (left, right) in enumerate(pairs):
        value = left[0].astype(jnp.float32) * right[0].astype(jnp.float32)
        value = value.T.astype(jnp.bfloat16)
        out_ref[:, slot, 0, 0] = value.reshape(groups, GROUP, LANES)


def ungate_kernel(grad_ref, q_ref, k_ref, gq_ref, gk_ref):
    groups = grad_ref.shape[0]
    grad = grad_ref[:, 0, 0].reshape(groups * GROUP, LANES).astype(jnp.float32).T
    gq_ref[0] = (grad * k_ref[0].astype(jnp.float32)).astype(jnp.bfloat16)
    gk_ref[0] = (grad * q_ref[0].astype(jnp.float32)).astype(jnp.bfloat16)


def group_kernel(
    pos_ref, data_ref, filt_ref, grad_ref, raw_ref, sq_ref, toep_ref, pad_ref, *, scale
):
    step = pl.program_id(0)
    per_device = pl.num_programs(0)
    blocks = raw_ref.shape[0] * raw_ref.shape[2]
    rows = data_ref.shape[0] * data_ref.shape[4] * GROUP
    row_id = lax.broadcasted_iota(jnp.int32, (LANES, LANES), 0)
    col_id = lax.broadcasted_iota(jnp.int32, (LANES, LANES), 1)

    @pl.when(step == 0)
    def _():
        toep_ref[:, :LANES] = jnp.zeros((LANES, LANES), jnp.bfloat16)
        pad_ref[:, rows:] = jnp.zeros((2, rows, LANES), jnp.bfloat16)
        sq_ref[...] = jnp.zeros_like(sq_ref)

    for half in range(2):
        pad_ref[half, :rows] = data_ref[:, 0, 0, half].reshape(rows, LANES)
    row = pos_ref[0] * per_device + step
    pick = lax.broadcasted_iota(jnp.int32, (8, filt_ref.shape[0]), 1) == row
    picked = jnp.dot(pick.astype(jnp.bfloat16), filt_ref[...], preferred_element_type=jnp.float32)
    upper = col_id >= row_id
    before = jnp.zeros((LANES, LANES), jnp.float32)
    for block in range(blocks):
        taps = jnp.concatenate([picked[:, block * LANES : (block + 1) * LANES]] * (LANES // 8), axis=0)
        rolled = pltpu.roll(taps, 0, 1, stride=1, stride_axis=0)
        toep_ref[:, (block + 1) * LANES : (block + 2) * LANES] = jnp.where(
            upper, rolled, before
        ).astype(jnp.bfloat16)
        before = rolled

    acc = jnp.zeros((rows, 2 * LANES), jnp.float32)
    for pair in range(blocks // 2):
        start = pair * GROUP
        left = jnp.concatenate([pad_ref[half, start:rows] for half in range(2)], axis=1)
        at = 2 * pair * LANES
        right = jnp.concatenate(
            [toep_ref[:, at + LANES : at + 3 * LANES], toep_ref[:, at : at + 2 * LANES]], axis=0
        )
        part = lax.dot_general(left, right, NT, preferred_element_type=jnp.float32)
        if start:
            part = jnp.concatenate([part, jnp.zeros((start, 2 * LANES), jnp.float32)], axis=0)
        acc = acc + part
    for half in range(2):
        value = acc[:, half * LANES : (half + 1) * LANES].astype(jnp.bfloat16)
        grad_ref[:, 0, half] = value.reshape(grad_ref.shape[0], grad_ref.shape[3], GROUP, LANES)

    flip = (row_id + col_id == LANES - 1).astype(jnp.bfloat16)
    prod = jnp.concatenate(
        [
            lax.dot_general(
                flip, data_ref[:, 0, 1, half].reshape(rows, LANES), NT, preferred_element_type=jnp.float32
            )
            for half in range(2)
        ],
        axis=1,
    ).astype(jnp.bfloat16)
    wraps = col_id <= row_id
    after = jnp.zeros((LANES, LANES), jnp.float32)
    per_owner = raw_ref.shape[2]
    squares = jnp.zeros((1, LANES), jnp.float32)
    for pair in reversed(range(blocks // 2)):
        start = pair * GROUP
        even = jnp.concatenate([pad_ref[0, start : start + rows], pad_ref[1, start : start + rows]], axis=0)
        odd = jnp.concatenate(
            [pad_ref[1, start : start + rows], pad_ref[0, start + GROUP : start + GROUP + rows]], axis=0
        )
        right = jnp.concatenate([even, odd], axis=1)
        both = jnp.dot(prod, right, preferred_element_type=jnp.float32)
        for half in (1, 0):
            block = 2 * pair + half
            rolled = pltpu.roll(both[:, half * LANES : (half + 1) * LANES], 1, 1, stride=1, stride_axis=0)
            lags = jnp.sum(jnp.where(wraps, rolled, after), axis=0, keepdims=True) * scale
            after = rolled
            raw_ref[block // per_owner, 0, block % per_owner : block % per_owner + 1] = lags
            squares = squares + lags * lags
    sq_ref[...] += jnp.broadcast_to(squares, sq_ref.shape)


def on_device(q_branch, k_branch, out_gate, filters, grad_out):
    seqs, block_len, chans = q_branch.shape
    owners = lax.axis_size("ctx")
    groups = chans // GROUP
    per_device = groups // owners
    local = block_len // LANES
    length = owners * block_len
    blocks = length // LANES
    wide = min(256, chans)
    scale = 4.0 / math.sqrt(seqs * GROUP)
    bf16, f32 = jnp.bfloat16, jnp.float32

    plain = pl.BlockSpec((1, LANES, wide), lambda i, j: (0, i, j))
    sent = pl.pallas_call(
        gate_kernel,
        grid=(local, chans // wide),
        in_specs=[plain] * 4,
        out_specs=pl.BlockSpec(
            (wide // GROUP, 2, 1, 1, GROUP, LANES), lambda i, j: (j, 0, i % 2, i // 2, 0, 0)
        ),
        out_shape=jax.ShapeDtypeStruct((groups, 2, 2, local // 2, GROUP, LANES), bf16),
        name="gate",
    )(q_branch, k_branch, out_gate, grad_out)
    got = lax.all_to_all(sent, "ctx", 0, 0, tiled=True)
    got = got.reshape(owners, per_device, 2, 2, local // 2, GROUP, LANES)
    rows = length * GROUP // (2 * LANES)
    pos = lax.axis_index("ctx").astype(jnp.int32).reshape(1)
    grad, raw, squares = pl.pallas_call(
        functools.partial(group_kernel, scale=scale),
        grid_spec=pltpu.PrefetchScalarGridSpec(
            num_scalar_prefetch=1,
            grid=(per_device,),
            in_specs=[
                pl.BlockSpec(
                    (owners, 1, 2, 2, local // 2, GROUP, LANES), lambda f, p: (0, f, 0, 0, 0, 0, 0)
                ),
                pl.BlockSpec((groups, length), lambda f, p: (0, 0)),
            ],
            out_specs=[
                pl.BlockSpec((owners, 1, 2, local // 2, GROUP, LANES), lambda f, p: (0, f, 0, 0, 0, 0)),
                pl.BlockSpec((owners, 1, blocks // owners, LANES), lambda f, p: (0, f, 0, 0)),
                pl.BlockSpec((8, LANES), lambda f, p: (0, 0)),
            ],
            scratch_shapes=[
                pltpu.VMEM((LANES, length + LANES), bf16),
                pltpu.VMEM((2, 2 * rows, LANES), bf16),
            ],
        ),
        out_shape=[
            jax.ShapeDtypeStruct((owners, per_device, 2, local // 2, GROUP, LANES), bf16),
            jax.ShapeDtypeStruct((owners, per_device, blocks // owners, LANES), f32),
            jax.ShapeDtypeStruct((8, LANES), f32),
        ],
        name="groups",
    )(pos, got, filters)

    back = lax.all_to_all(grad.reshape(groups, 2, local // 2, GROUP, LANES), "ctx", 0, 0, tiled=True)
    raw = lax.all_to_all(raw, "ctx", 0, 0, tiled=True).reshape(groups, length // owners)
    both = ("ctx", "ch")
    count = lax.axis_size(both)
    spread = jnp.broadcast_to(squares[:1], (count, LANES))
    total = jnp.sum(lax.all_to_all(spread, both, 0, 0, tiled=True))
    threshold = math.sqrt(WIDTH // GROUP * length)
    factor = jnp.minimum(1.0, threshold / jnp.sqrt(total + 1e-06))
    grad_q, grad_k = pl.pallas_call(
        ungate_kernel,
        grid=(local, chans // wide),
        in_specs=[
            pl.BlockSpec((wide // GROUP, 1, 1, GROUP, LANES), lambda i, j: (j, i % 2, i // 2, 0, 0)),
            plain,
            plain,
        ],
        out_specs=[plain] * 2,
        out_shape=[jax.ShapeDtypeStruct(q_branch.shape, bf16)] * 2,
        name="ungate",
    )(back, q_branch, k_branch)
    return (grad_q, grad_k, raw * factor)


def solution(mesh):
    return jax.shard_map(
        on_device,
        mesh=mesh,
        in_specs=(
            P(None, "ctx", "ch"),
            P(None, "ctx", "ch"),
            P(None, "ctx", "ch"),
            P("ch", None),
            P(None, "ctx", "ch"),
        ),
        out_specs=(P(None, "ctx", "ch"), P(None, "ctx", "ch"), P("ch", "ctx")),
        check_vma=False,
    )
```

```python
import functools
import math

import jax
import jax.numpy as jnp
from jax import lax
from jax.experimental import pallas as pl
from jax.experimental.pallas import tpu as pltpu
from jax.sharding import PartitionSpec as P

WIDTH = 8192
GROUP = 16
LANES = 128
NT = (((1,), (1,)), ((), ()))
BF16, F32 = jnp.bfloat16, jnp.float32


def gate_kernel(pos_ref, left_ref, right_ref, *refs):
    *outs, left, right, out, in_sem, out_sem = refs
    local = left.shape[0] // LANES
    per_device = outs[0].shape[0]
    copies = []
    for i in range(local):
        here = pl.ds(i * LANES, LANES)
        copies.append(
            (
                pltpu.make_async_copy(left_ref.at[0, here], left.at[here], in_sem.at[i, 0]),
                pltpu.make_async_copy(right_ref.at[0, here], right.at[here], in_sem.at[i, 1]),
            )
        )
    for pair in copies:
        for copy in pair:
            copy.start()
    sends = []
    for i in range(local):
        for copy in copies[i]:
            copy.wait()
        rows = slice(i * LANES, (i + 1) * LANES)
        value = (left[rows].astype(F32) * right[rows].astype(F32)).astype(BF16).T
        out[i % 2, i // 2] = value.reshape(out.shape[2:])
        for k, target in enumerate(outs):
            first = jnp.bitwise_xor(pos_ref[0], k) * per_device
            send = pltpu.make_async_copy(
                out.at[i % 2, i // 2, pl.ds(first, per_device)],
                target.at[:, i % 2, i // 2],
                out_sem.at[i, k],
            )
            send.start()
            sends.append(send)
    for send in sends:
        send.wait()


def ungate_kernel(pos_ref, q_ref, k_ref, *refs):
    *grads, gq_ref, gk_ref, grad, q_in, k_in, gq, gk, in_sem, out_sem = refs
    local = q_in.shape[0] // LANES
    per_device = grads[0].shape[0]
    owners = len(grads)
    copies, sends = [], []
    for i in range(local):
        here = pl.ds(i * LANES, LANES)
        row = [
            pltpu.make_async_copy(q_ref.at[0, here], q_in.at[here], in_sem.at[i, owners]),
            pltpu.make_async_copy(k_ref.at[0, here], k_in.at[here], in_sem.at[i, owners + 1]),
        ]
        for k, source in enumerate(grads):
            first = jnp.bitwise_xor(pos_ref[0], k) * per_device
            row.append(
                pltpu.make_async_copy(
                    source.at[:, i % 2, i // 2], grad.at[i, pl.ds(first, per_device)], in_sem.at[i, k]
                )
            )
        copies.append(row)
    for row in copies:
        for copy in row:
            copy.start()
    for i in range(local):
        for copy in copies[i]:
            copy.wait()
        here = pl.ds(i * LANES, LANES)
        rows = slice(i * LANES, (i + 1) * LANES)
        value = grad[i].reshape(q_in.shape[1], LANES).T.astype(F32)
        gq[rows] = (value * k_in[rows].astype(F32)).astype(BF16)
        gk[rows] = (value * q_in[rows].astype(F32)).astype(BF16)
        for n, (source, target) in enumerate(((gq, gq_ref), (gk, gk_ref))):
            send = pltpu.make_async_copy(source.at[here], target.at[0, here], out_sem.at[i, n])
            send.start()
            sends.append(send)
    for send in sends:
        send.wait()


def clip_kernel(pos_ref, total_ref, *refs, threshold):
    *parts, _, out_ref, stage = refs
    per_device, each = stage.shape[1:3]
    for k, part in enumerate(parts):
        stage[jnp.bitwise_xor(pos_ref[0], k)] = part[...]
    total = jnp.sum(total_ref[...], axis=(0, 1, 2), keepdims=True)[0]
    factor = jnp.minimum(1.0, threshold / jnp.sqrt(total + 1e-06))
    for owner in range(stage.shape[0]):
        for n in range(each):
            rows = slice(owner * per_device, (owner + 1) * per_device)
            out_ref[rows, n * LANES : (n + 1) * LANES] = stage[owner, :, n] * factor


def fetch(pos_ref, sources, target, sem, *at):
    return [
        pltpu.make_async_copy(source, target.at[jnp.bitwise_xor(pos_ref[0], k)], sem.at[(k,) + at])
        for k, source in enumerate(sources)
    ]


def store(pos_ref, source, targets, sem, *at):
    return [
        pltpu.make_async_copy(source.at[jnp.bitwise_xor(pos_ref[0], k)], target, sem.at[(k,) + at])
        for k, target in enumerate(targets)
    ]


def conv_kernel(pos_ref, filt_ref, *refs):
    *refs, grad_v, out_v, taps, toep, pad, sem = refs
    ins, outs = refs[: len(refs) // 2], refs[len(refs) // 2 :]
    per_device, blocks = taps.shape[0], taps.shape[1] - 1
    owners, half_blocks = grad_v.shape[0], grad_v.shape[3]
    rows = pad.shape[1]
    copies = fetch(pos_ref, ins, grad_v, sem)
    for copy in copies:
        copy.start()
    groups = filt_ref.shape[0]
    picks = max(per_device, 8)
    row_id = lax.broadcasted_iota(jnp.int32, (picks, groups), 0)
    col_id = lax.broadcasted_iota(jnp.int32, (picks, groups), 1)
    pick = (col_id == row_id + pos_ref[0] * per_device).astype(BF16)
    mine = jnp.dot(pick, filt_ref[...], preferred_element_type=F32).astype(BF16)
    empty = jnp.zeros((picks, LANES), BF16)
    mine = jnp.concatenate([empty, mine, empty], axis=1)
    row_id = lax.broadcasted_iota(jnp.int32, (2 * LANES, LANES), 0)
    col_id = lax.broadcasted_iota(jnp.int32, (2 * LANES, LANES), 1)
    flip = (row_id + col_id == LANES).astype(BF16)
    for block in range(blocks + 1):
        near = mine[:, block * LANES : (block + 2) * LANES]
        back = jnp.dot(near, flip, preferred_element_type=F32)
        for f in range(per_device):
            taps[f, block] = back[f : f + 1]
    toep[0] = jnp.zeros((LANES, LANES), BF16)
    row_id = lax.broadcasted_iota(jnp.int32, (LANES, LANES), 0)
    col_id = lax.broadcasted_iota(jnp.int32, (LANES, LANES), 1)
    upper = col_id >= row_id

    def one(f, carry):
        for half in range(2):
            pad[half] = grad_v[:, f, half].reshape(rows, LANES)
        before = None
        for block in range(blocks + 1):
            tap = jnp.broadcast_to(taps[f, block], (LANES, LANES))
            rolled = pltpu.roll(tap, 0, 1, stride=1, stride_axis=0)
            if block:
                toep[block] = jnp.where(upper, before, rolled).astype(BF16)
            before = rolled
        acc = jnp.zeros((rows, 2 * LANES), F32)
        for pair in range(blocks // 2):
            start = pair * GROUP
            left = jnp.concatenate([pad[0, start:], pad[1, start:]], axis=1)
            at = 2 * pair + 1
            top = jnp.concatenate([toep[at], toep[at - 1]], axis=1)
            low = jnp.concatenate([toep[at + 1], toep[at]], axis=1)
            right = jnp.concatenate([top, low], axis=0)
            part = jnp.dot(left, right, preferred_element_type=F32)
            if start:
                part = jnp.concatenate([part, jnp.zeros((start, 2 * LANES), F32)], axis=0)
            acc = acc + part
        for half in range(2):
            value = acc[:, half * LANES : (half + 1) * LANES].astype(BF16)
            out_v[:, f, half] = value.reshape(owners, half_blocks, GROUP, LANES)
        return carry

    for copy in copies:
        copy.wait()
    lax.fori_loop(0, per_device, one, 0)
    sends = store(pos_ref, out_v, outs, sem)
    for send in sends:
        send.start()
    for send in sends:
        send.wait()


def lag_kernel(pos_ref, *refs, scale):
    *refs, sq_ref, grad_v, prod_v, raw_v, pad, sem = refs
    owners, per_device, per_owner = raw_v.shape[:3]
    blocks = owners * per_owner
    grads, prods, raws = refs[:owners], refs[owners : 2 * owners], refs[-owners:]
    rows = pad.shape[1] // 2
    copies = fetch(pos_ref, grads, grad_v, sem, 0) + fetch(pos_ref, prods, prod_v, sem, 1)
    for copy in copies:
        copy.start()
    pad[:, rows:] = jnp.zeros((2, rows, LANES), BF16)
    sq_ref[...] = jnp.zeros_like(sq_ref)
    row_id = lax.broadcasted_iota(jnp.int32, (LANES, LANES), 0)
    col_id = lax.broadcasted_iota(jnp.int32, (LANES, LANES), 1)
    flip = (row_id + col_id == LANES - 1).astype(BF16)
    wraps = col_id <= row_id

    def one(f, carry):
        for half in range(2):
            pad[half, :rows] = grad_v[:, f, half].reshape(rows, LANES)
        prod = jnp.concatenate(
            [
                lax.dot_general(
                    flip, prod_v[:, f, half].reshape(rows, LANES), NT, preferred_element_type=F32
                )
                for half in range(2)
            ],
            axis=1,
        ).astype(BF16)
        after = jnp.zeros((LANES, LANES), F32)
        squares = jnp.zeros((1, LANES), F32)
        for pair in reversed(range(blocks // 2)):
            start = pair * GROUP
            here, later = slice(start, start + rows), slice(start + GROUP, start + GROUP + rows)
            even = jnp.concatenate([pad[0, here], pad[1, here]], axis=0)
            odd = jnp.concatenate([pad[1, here], pad[0, later]], axis=0)
            both = jnp.dot(
                prod, jnp.concatenate([even, odd], axis=1), preferred_element_type=F32
            )
            for half in (1, 0):
                block = 2 * pair + half
                rolled = pltpu.roll(
                    both[:, half * LANES : (half + 1) * LANES], 1, 1, stride=1, stride_axis=0
                )
                lags = jnp.sum(jnp.where(wraps, rolled, after), axis=0, keepdims=True) * scale
                after = rolled
                raw_v[block // per_owner, f, block % per_owner : block % per_owner + 1] = lags
                squares = squares + lags * lags
        sq_ref[...] += jnp.broadcast_to(squares, sq_ref.shape)
        return carry

    for copy in copies:
        copy.wait()
    lax.fori_loop(0, per_device, one, 0)
    sends = store(pos_ref, raw_v, raws, sem, 0)
    for send in sends:
        send.start()
    for send in sends:
        send.wait()


def cost(flops, moved):
    return pl.CostEstimate(flops=int(flops), bytes_accessed=int(moved), transcendentals=0)


def on_device(q_branch, k_branch, out_gate, filters, grad_out):
    seqs, block_len, chans = q_branch.shape
    owners = lax.axis_size("ctx")
    groups = chans // GROUP
    per_device = groups // owners
    local = block_len // LANES
    length = owners * block_len
    blocks = length // LANES
    rows = length * GROUP // (2 * LANES)
    scale = 4.0 / math.sqrt(seqs * GROUP)
    size = block_len * chans * 2
    anywhere = pl.BlockSpec(memory_space=pl.ANY)
    vmem = pl.BlockSpec(memory_space=pltpu.VMEM)
    smem = pl.BlockSpec(memory_space=pltpu.SMEM)
    tail = (2, local // 2, GROUP, LANES)
    whole = (owners, per_device) + tail
    pos = lax.axis_index("ctx").astype(jnp.int32).reshape(1)
    piece = jax.ShapeDtypeStruct((per_device,) + tail, BF16)
    lag_piece = jax.ShapeDtypeStruct((per_device, blocks // owners, LANES), F32)

    def gate(left, right, limit, name):
        return pl.pallas_call(
            gate_kernel,
            in_specs=[smem] + [pl.BlockSpec(memory_space=pltpu.HBM)] * 2,
            out_specs=[anywhere] * owners,
            out_shape=[piece] * owners,
            scratch_shapes=[
                pltpu.VMEM((block_len, chans), BF16),
                pltpu.VMEM((block_len, chans), BF16),
                pltpu.VMEM((2, local // 2, groups, GROUP, LANES), BF16),
                pltpu.SemaphoreType.DMA((local, 2)),
                pltpu.SemaphoreType.DMA((local, owners)),
            ],
            cost_estimate=cost(block_len * chans, 3 * size),
            compiler_params=pltpu.CompilerParams(vmem_limit_bytes=limit << 20),
            name=name,
        )(pos, left, right)

    def swap(values):
        out = [values[0]]
        for k in range(1, owners):
            out.append(lax.ppermute(values[k], "ctx", [(i, i ^ k) for i in range(owners)]))
        return out

    grad_got = swap(gate(grad_out, out_gate, 56, "gate_grad"))
    prod_got = swap(gate(q_branch, k_branch, 12, "gate_prod"))
    conv = pl.pallas_call(
        conv_kernel,
        in_specs=[smem, vmem] + [anywhere] * owners,
        out_specs=[anywhere] * owners,
        out_shape=[piece] * owners,
        scratch_shapes=[
            pltpu.VMEM(whole, BF16),
            pltpu.VMEM(whole, BF16),
            pltpu.VMEM((per_device, blocks + 1, 1, LANES), F32),
            pltpu.VMEM((blocks + 1, LANES, LANES), BF16),
            pltpu.VMEM((2, rows, LANES), BF16),
            pltpu.SemaphoreType.DMA((owners,)),
        ],
        cost_estimate=cost(per_device * rows * length * 4096, 2 * size + groups * length * 2),
        compiler_params=pltpu.CompilerParams(vmem_limit_bytes=16 << 20),
        name="conv",
    )(pos, filters, *grad_got)
    back = swap(conv)
    *raw, squares = pl.pallas_call(
        functools.partial(lag_kernel, scale=scale),
        in_specs=[smem] + [anywhere] * (2 * owners + 1),
        out_specs=[anywhere] * owners + [vmem],
        out_shape=[lag_piece] * owners + [jax.ShapeDtypeStruct((8, LANES), F32)],
        scratch_shapes=[
            pltpu.VMEM(whole, BF16),
            pltpu.VMEM(whole, BF16),
            pltpu.VMEM((owners, per_device, blocks // owners, LANES), F32),
            pltpu.VMEM((2, 2 * rows, LANES), BF16),
            pltpu.SemaphoreType.DMA((owners, 2)),
        ],
        cost_estimate=cost(per_device * 2 * rows * length * 2048, 2 * size + per_device * length * 4),
        compiler_params=pltpu.CompilerParams(vmem_limit_bytes=16 << 20),
        name="lags",
    )(pos, *grad_got, *prod_got, conv[0])

    raw = swap(raw)
    both = ("ctx", "ch")
    count = lax.axis_size(both)
    spread = jnp.broadcast_to(squares[:1], (count, 1, LANES))
    total = lax.all_to_all(spread, both, 0, 0, tiled=True)
    threshold = math.sqrt(WIDTH // GROUP * length)
    grad_q, grad_k = pl.pallas_call(
        ungate_kernel,
        in_specs=[smem] + [anywhere] * (2 + owners),
        out_specs=[anywhere] * 2,
        out_shape=[jax.ShapeDtypeStruct(q_branch.shape, BF16)] * 2,
        scratch_shapes=[
            pltpu.VMEM((local, groups, GROUP, LANES), BF16),
            pltpu.VMEM((block_len, chans), BF16),
            pltpu.VMEM((block_len, chans), BF16),
            pltpu.VMEM((block_len, chans), BF16),
            pltpu.VMEM((block_len, chans), BF16),
            pltpu.SemaphoreType.DMA((local, owners + 2)),
            pltpu.SemaphoreType.DMA((local, 2)),
        ],
        cost_estimate=cost(2 * block_len * chans, 5 * size),
        compiler_params=pltpu.CompilerParams(vmem_limit_bytes=16 << 20),
        name="ungate",
    )(pos, q_branch, k_branch, *back)
    grad_filters = pl.pallas_call(
        functools.partial(clip_kernel, threshold=threshold),
        in_specs=[smem] + [vmem] * (1 + owners) + [anywhere],
        out_specs=vmem,
        out_shape=jax.ShapeDtypeStruct((groups, length // owners), F32),
        scratch_shapes=[pltpu.VMEM((owners, per_device, blocks // owners, LANES), F32)],
        cost_estimate=cost(groups * length, groups * length * 4),
        compiler_params=pltpu.CompilerParams(vmem_limit_bytes=60 << 20),
        name="clip",
    )(pos, total, *raw, grad_q)
    return (grad_q, grad_k, grad_filters)


def solution(mesh):
    return jax.shard_map(
        on_device,
        mesh=mesh,
        in_specs=(
            P(None, "ctx", "ch"),
            P(None, "ctx", "ch"),
            P(None, "ctx", "ch"),
            P("ch", None),
            P(None, "ctx", "ch"),
        ),
        out_specs=(P(None, "ctx", "ch"), P(None, "ctx", "ch"), P("ch", "ctx")),
        check_vma=False,
    )
```

```python
import functools
import math

import jax
import jax.numpy as jnp
from jax import lax
from jax.experimental import pallas as pl
from jax.experimental.pallas import tpu as pltpu
from jax.sharding import PartitionSpec as P

WIDTH = 8192
GROUP = 16
LANES = 128
NT = (((1,), (1,)), ((), ()))
BF16, F32 = jnp.bfloat16, jnp.float32


def gate_kernel(pos_ref, left_ref, right_ref, *refs, reverse):
    *outs, left, right, out, in_sem, out_sem = refs
    local = left.shape[0] // LANES
    per_device = outs[0].shape[0]
    copies = []
    for i in range(local):
        here = pl.ds(i * LANES, LANES)
        copies.append(
            (
                pltpu.make_async_copy(left_ref.at[0, here], left.at[here], in_sem.at[i, 0]),
                pltpu.make_async_copy(right_ref.at[0, here], right.at[here], in_sem.at[i, 1]),
            )
        )
    for pair in copies:
        for copy in pair:
            copy.start()
    sends = []
    for i in range(local):
        for copy in copies[i]:
            copy.wait()
        rows = slice(i * LANES, (i + 1) * LANES)
        value = (left[rows].astype(F32) * right[rows].astype(F32)).astype(BF16)
        if reverse:
            row_id = lax.broadcasted_iota(jnp.int32, (LANES, LANES), 0)
            col_id = lax.broadcasted_iota(jnp.int32, (LANES, LANES), 1)
            flip = (row_id + col_id == LANES - 1).astype(BF16)
            value = jnp.dot(flip, value, preferred_element_type=F32).astype(BF16)
        value = value.T
        out[i % 2, i // 2] = value.reshape(out.shape[2:])
        for k, target in enumerate(outs):
            first = jnp.bitwise_xor(pos_ref[0], k) * per_device
            send = pltpu.make_async_copy(
                out.at[i % 2, i // 2, pl.ds(first, per_device)],
                target.at[:, i % 2, i // 2],
                out_sem.at[i, k],
            )
            send.start()
            sends.append(send)
    for send in sends:
        send.wait()


def ungate_kernel(pos_ref, q_ref, k_ref, *refs):
    *grads, gq_ref, gk_ref, mark_ref, grad, q_in, k_in, gq, gk, in_sem, out_sem = refs
    local = q_in.shape[0] // LANES
    per_device = grads[0].shape[0]
    owners = len(grads)
    mark_ref[...] = jnp.zeros_like(mark_ref)
    copies, sends = [], []
    for i in range(local):
        here = pl.ds(i * LANES, LANES)
        row = [
            pltpu.make_async_copy(q_ref.at[0, here], q_in.at[here], in_sem.at[i, owners]),
            pltpu.make_async_copy(k_ref.at[0, here], k_in.at[here], in_sem.at[i, owners + 1]),
        ]
        for k, source in enumerate(grads):
            first = jnp.bitwise_xor(pos_ref[0], k) * per_device
            row.append(
                pltpu.make_async_copy(
                    source.at[:, i % 2, i // 2], grad.at[i, pl.ds(first, per_device)], in_sem.at[i, k]
                )
            )
        copies.append(row)
    for row in copies:
        for copy in row:
            copy.start()
    for i in range(local):
        for copy in copies[i]:
            copy.wait()
        here = pl.ds(i * LANES, LANES)
        rows = slice(i * LANES, (i + 1) * LANES)
        value = grad[i].reshape(q_in.shape[1], LANES).T.astype(F32)
        gq[rows] = (value * k_in[rows].astype(F32)).astype(BF16)
        gk[rows] = (value * q_in[rows].astype(F32)).astype(BF16)
        for n, (source, target) in enumerate(((gq, gq_ref), (gk, gk_ref))):
            send = pltpu.make_async_copy(source.at[here], target.at[0, here], out_sem.at[i, n])
            send.start()
            sends.append(send)
    for send in sends:
        send.wait()


def clip_kernel(pos_ref, total_ref, *refs, threshold):
    *parts, _, out_ref, stage = refs
    per_device, each = stage.shape[1:3]
    for k, part in enumerate(parts):
        stage[jnp.bitwise_xor(pos_ref[0], k)] = part[...]
    total = jnp.sum(total_ref[...], axis=(0, 1, 2), keepdims=True)[0]
    factor = jnp.minimum(1.0, threshold / jnp.sqrt(total + 1e-06))
    for owner in range(stage.shape[0]):
        for n in range(each):
            rows = slice(owner * per_device, (owner + 1) * per_device)
            out_ref[rows, n * LANES : (n + 1) * LANES] = stage[owner, :, n] * factor


def spread_rows(pos_ref, sources, f, target):
    for k, source in enumerate(sources):
        count = source.shape[2] * GROUP
        at = pl.multiple_of(jnp.bitwise_xor(pos_ref[0], k) * count, count)
        for half in range(2):
            target[half, pl.ds(at, count)] = source[f, half].reshape(count, LANES)


def conv_kernel(pos_ref, filt_ref, *refs, owners, unroll):
    ins, outs, refs = refs[:owners], refs[owners : 2 * owners], refs[2 * owners :]
    taps, refs = refs[0], refs[1:]
    toeps, pads, accs = refs[:unroll], refs[unroll : 2 * unroll], refs[2 * unroll :]
    per_device, blocks = taps.shape[0], taps.shape[1] - 1
    rows = pads[0].shape[1]
    groups = filt_ref.shape[0]
    picks = max(per_device, 8)
    row_id = lax.broadcasted_iota(jnp.int32, (picks, groups), 0)
    col_id = lax.broadcasted_iota(jnp.int32, (picks, groups), 1)
    pick = (col_id == row_id + pos_ref[0] * per_device).astype(BF16)
    mine = jnp.dot(pick, filt_ref[...], preferred_element_type=F32).astype(BF16)
    empty = jnp.zeros((picks, LANES), BF16)
    mine = jnp.concatenate([empty, mine, empty], axis=1)
    row_id = lax.broadcasted_iota(jnp.int32, (2 * LANES, LANES), 0)
    col_id = lax.broadcasted_iota(jnp.int32, (2 * LANES, LANES), 1)
    flip = (row_id + col_id == LANES).astype(BF16)
    for block in range(blocks + 1):
        near = mine[:, block * LANES : (block + 2) * LANES]
        back = jnp.dot(near, flip, preferred_element_type=F32)
        for f in range(per_device):
            taps[f, block] = back[f : f + 1]
    for toep in toeps:
        toep[0] = jnp.zeros((LANES, LANES), BF16)
    row_id = lax.broadcasted_iota(jnp.int32, (LANES, LANES), 0)
    col_id = lax.broadcasted_iota(jnp.int32, (LANES, LANES), 1)
    upper = col_id >= row_id

    def one(f, toep, pad, out):
        before = None
        for block in range(blocks + 1):
            tap = jnp.broadcast_to(taps[f, block], (LANES, LANES))
            rolled = pltpu.roll(tap, 0, 1, stride=1, stride_axis=0)
            if block:
                toep[block] = jnp.where(upper, before, rolled).astype(BF16)
            before = rolled
        acc = jnp.zeros((rows, 2 * LANES), F32)
        for pair in range(blocks // 2):
            start = pair * GROUP
            left = jnp.concatenate([pad[0, start:], pad[1, start:]], axis=1)
            at = 2 * pair + 1
            top = jnp.concatenate([toep[at], toep[at - 1]], axis=1)
            low = jnp.concatenate([toep[at + 1], toep[at]], axis=1)
            right = jnp.concatenate([top, low], axis=0)
            part = jnp.dot(left, right, preferred_element_type=F32)
            if start:
                part = jnp.concatenate([part, jnp.zeros((start, 2 * LANES), F32)], axis=0)
            acc = acc + part
        for half in range(2):
            out[half] = acc[:, half * LANES : (half + 1) * LANES].astype(BF16)

    def some(i, carry):
        for u in range(unroll):
            spread_rows(pos_ref, ins, i * unroll + u, pads[u])
        for u in range(unroll):
            one(i * unroll + u, toeps[u], pads[u], accs[u])
        for u in range(unroll):
            for k, target in enumerate(outs):
                count = target.shape[2] * GROUP
                at = pl.multiple_of(jnp.bitwise_xor(pos_ref[0], k) * count, count)
                for half in range(2):
                    value = accs[u][half, pl.ds(at, count)]
                    target[i * unroll + u, half] = value.reshape(target.shape[2:])
        return carry

    lax.fori_loop(0, per_device // unroll, some, 0)


def lag_kernel(pos_ref, *refs, owners, unroll, scale):
    grads, prods, refs = refs[:owners], refs[owners : 2 * owners], refs[2 * owners + 1 :]
    raws, sum_ref, refs = refs[:owners], refs[owners], refs[owners + 1 :]
    pads, flips, lags_v, sq_v = refs[:unroll], refs[unroll : 2 * unroll], refs[-2], refs[-1]
    per_device, per_owner = raws[0].shape[:2]
    blocks = owners * per_owner
    rows = flips[0].shape[1]
    for pad in pads:
        pad[:, rows:] = jnp.zeros((2, rows, LANES), BF16)
    sq_v[...] = jnp.zeros_like(sq_v)
    row_id = lax.broadcasted_iota(jnp.int32, (LANES, LANES), 0)
    col_id = lax.broadcasted_iota(jnp.int32, (LANES, LANES), 1)
    wraps = col_id <= row_id

    def one(slot, pad, flipped):
        prod = jnp.concatenate([flipped[half].T for half in range(2)], axis=1)
        after = jnp.zeros((LANES, LANES), F32)
        sums = {}
        for pair in reversed(range(blocks // 2)):
            start = pair * GROUP
            here, later = slice(start, start + rows), slice(start + GROUP, start + GROUP + rows)
            even = jnp.concatenate([pad[0, here], pad[1, here]], axis=0)
            odd = jnp.concatenate([pad[1, here], pad[0, later]], axis=0)
            both = jnp.dot(
                prod, jnp.concatenate([even, odd], axis=1), preferred_element_type=F32
            )
            for half in (1, 0):
                rolled = pltpu.roll(
                    both[:, half * LANES : (half + 1) * LANES], 1, 1, stride=1, stride_axis=0
                )
                part = jnp.where(wraps, rolled, after)
                sums[2 * pair + half] = jnp.sum(part, axis=0, keepdims=True)
                after = rolled
        for owner in range(owners):
            lags = jnp.concatenate(
                [sums[owner * per_owner + n] for n in range(per_owner)], axis=0
            ) * scale
            lags_v[slot, owner] = lags
            sq_v[...] += lags * lags

    def some(i, carry):
        for u in range(unroll):
            spread_rows(pos_ref, grads, i * unroll + u, pads[u])
            spread_rows(pos_ref, prods, i * unroll + u, flips[u])
        for u in range(unroll):
            one(u, pads[u], flips[u])
        for u in range(unroll):
            for k, target in enumerate(raws):
                target[i * unroll + u] = lags_v[u, jnp.bitwise_xor(pos_ref[0], k)]
        return carry

    lax.fori_loop(0, per_device // unroll, some, 0)
    squares = jnp.sum(sq_v[...], axis=0, keepdims=True)
    sum_ref[...] = jnp.broadcast_to(squares[None], sum_ref.shape)


def cost(flops, moved):
    return pl.CostEstimate(flops=int(flops), bytes_accessed=int(moved), transcendentals=0)


def on_device(q_branch, k_branch, out_gate, filters, grad_out):
    seqs, block_len, chans = q_branch.shape
    owners = lax.axis_size("ctx")
    groups = chans // GROUP
    per_device = groups // owners
    local = block_len // LANES
    length = owners * block_len
    blocks = length // LANES
    rows = length * GROUP // (2 * LANES)
    scale = 4.0 / math.sqrt(seqs * GROUP)
    size = block_len * chans * 2
    anywhere = pl.BlockSpec(memory_space=pl.ANY)
    vmem = pl.BlockSpec(memory_space=pltpu.VMEM)
    smem = pl.BlockSpec(memory_space=pltpu.SMEM)
    tail = (2, local // 2, GROUP, LANES)
    whole = (owners, per_device) + tail
    pos = lax.axis_index("ctx").astype(jnp.int32).reshape(1)
    piece = jax.ShapeDtypeStruct((per_device,) + tail, BF16)
    lag_piece = jax.ShapeDtypeStruct((per_device, blocks // owners, LANES), F32)

    def gate(left, right, reverse, limit, name):
        return pl.pallas_call(
            functools.partial(gate_kernel, reverse=reverse),
            in_specs=[smem] + [pl.BlockSpec(memory_space=pltpu.HBM)] * 2,
            out_specs=[anywhere] * owners,
            out_shape=[piece] * owners,
            scratch_shapes=[
                pltpu.VMEM((block_len, chans), BF16),
                pltpu.VMEM((block_len, chans), BF16),
                pltpu.VMEM((2, local // 2, groups, GROUP, LANES), BF16),
                pltpu.SemaphoreType.DMA((local, 2)),
                pltpu.SemaphoreType.DMA((local, owners)),
            ],
            cost_estimate=cost(block_len * chans, 3 * size),
            compiler_params=pltpu.CompilerParams(vmem_limit_bytes=limit << 20),
            name=name,
        )(pos, left, right)

    def swap(values):
        out = [values[0]]
        for k in range(1, owners):
            out.append(lax.ppermute(values[k], "ctx", [(i, i ^ k) for i in range(owners)]))
        return out

    grad_got = swap(gate(grad_out, out_gate, False, 56, "gate_grad"))
    prod_got = swap(gate(q_branch, k_branch, True, 12, "gate_prod"))
    unroll = math.gcd(4, per_device)
    conv = pl.pallas_call(
        functools.partial(conv_kernel, owners=owners, unroll=unroll),
        in_specs=[smem] + [vmem] * (1 + owners),
        out_specs=[vmem] * owners,
        out_shape=[piece] * owners,
        scratch_shapes=[pltpu.VMEM((per_device, blocks + 1, 1, LANES), F32)]
        + [pltpu.VMEM((blocks + 1, LANES, LANES), BF16)] * unroll
        + [pltpu.VMEM((2, rows, LANES), BF16)] * (2 * unroll),
        cost_estimate=cost(per_device * rows * length * 4096, 2 * size + groups * length * 2),
        compiler_params=pltpu.CompilerParams(vmem_limit_bytes=16 << 20),
        name="conv",
    )(pos, filters, *grad_got)
    back = swap(conv)
    both = ("ctx", "ch")
    count = lax.axis_size(both)
    unroll = math.gcd(8, per_device)
    *raw, spread = pl.pallas_call(
        functools.partial(lag_kernel, owners=owners, unroll=unroll, scale=scale),
        in_specs=[smem] + [vmem] * (2 * owners) + [anywhere],
        out_specs=[vmem] * (owners + 1),
        out_shape=[lag_piece] * owners + [jax.ShapeDtypeStruct((count, 1, LANES), F32)],
        scratch_shapes=[pltpu.VMEM((2, 2 * rows, LANES), BF16)] * unroll
        + [pltpu.VMEM((2, rows, LANES), BF16)] * unroll
        + [
            pltpu.VMEM((unroll, owners, blocks // owners, LANES), F32),
            pltpu.VMEM((blocks // owners, LANES), F32),
        ],
        cost_estimate=cost(per_device * 2 * rows * length * 2048, 2 * size + per_device * length * 4),
        compiler_params=pltpu.CompilerParams(vmem_limit_bytes=16 << 20),
        name="lags",
    )(pos, *grad_got, *prod_got, conv[0])
    total = lax.all_to_all(spread, both, 0, 0, tiled=True)
    threshold = math.sqrt(WIDTH // GROUP * length)
    grad_q, grad_k, mark = pl.pallas_call(
        ungate_kernel,
        in_specs=[smem] + [anywhere] * (2 + owners),
        out_specs=[anywhere] * 2 + [vmem],
        out_shape=[jax.ShapeDtypeStruct(q_branch.shape, BF16)] * 2
        + [jax.ShapeDtypeStruct((8, LANES), F32)],
        scratch_shapes=[
            pltpu.VMEM((local, groups, GROUP, LANES), BF16),
            pltpu.VMEM((block_len, chans), BF16),
            pltpu.VMEM((block_len, chans), BF16),
            pltpu.VMEM((block_len, chans), BF16),
            pltpu.VMEM((block_len, chans), BF16),
            pltpu.SemaphoreType.DMA((local, owners + 2)),
            pltpu.SemaphoreType.DMA((local, 2)),
        ],
        cost_estimate=cost(2 * block_len * chans, 5 * size),
        compiler_params=pltpu.CompilerParams(vmem_limit_bytes=16 << 20),
        name="ungate",
    )(pos, q_branch, k_branch, *back)
    raw, mark = lax.optimization_barrier((raw, mark))
    raw = swap(raw)
    grad_filters = pl.pallas_call(
        functools.partial(clip_kernel, threshold=threshold),
        in_specs=[smem] + [vmem] * (2 + owners),
        out_specs=vmem,
        out_shape=jax.ShapeDtypeStruct((groups, length // owners), F32),
        scratch_shapes=[pltpu.VMEM((owners, per_device, blocks // owners, LANES), F32)],
        cost_estimate=cost(groups * length, groups * length * 4),
        compiler_params=pltpu.CompilerParams(vmem_limit_bytes=8 << 20),
        name="clip",
    )(pos, total, *raw, mark)
    return (grad_q, grad_k, grad_filters)


def solution(mesh):
    return jax.shard_map(
        on_device,
        mesh=mesh,
        in_specs=(
            P(None, "ctx", "ch"),
            P(None, "ctx", "ch"),
            P(None, "ctx", "ch"),
            P("ch", None),
            P(None, "ctx", "ch"),
        ),
        out_specs=(P(None, "ctx", "ch"), P(None, "ctx", "ch"), P("ch", "ctx")),
        check_vma=False,
    )
```

```python
import functools
import math

import jax
import jax.numpy as jnp
from jax import lax
from jax.experimental import pallas as pl
from jax.experimental.pallas import tpu as pltpu
from jax.sharding import PartitionSpec as P

WIDTH = 8192
GROUP = 16
LANES = 128
NT = (((1,), (1,)), ((), ()))
BF16, F32 = jnp.bfloat16, jnp.float32


def gate_kernel(pos_ref, left_ref, right_ref, *refs, reverse):
    *outs, left, right, out, in_sem, out_sem = refs
    local = left.shape[0] // LANES
    per_device = outs[0].shape[0]
    copies = []
    for i in range(local):
        here = pl.ds(i * LANES, LANES)
        copies.append(
            (
                pltpu.make_async_copy(left_ref.at[0, here], left.at[here], in_sem.at[i, 0]),
                pltpu.make_async_copy(right_ref.at[0, here], right.at[here], in_sem.at[i, 1]),
            )
        )
    for pair in copies:
        for copy in pair:
            copy.start()
    sends = []
    for i in range(local):
        for copy in copies[i]:
            copy.wait()
        rows = slice(i * LANES, (i + 1) * LANES)
        value = (left[rows].astype(F32) * right[rows].astype(F32)).astype(BF16)
        if reverse:
            row_id = lax.broadcasted_iota(jnp.int32, (LANES, LANES), 0)
            col_id = lax.broadcasted_iota(jnp.int32, (LANES, LANES), 1)
            flip = (row_id + col_id == LANES - 1).astype(BF16)
            value = jnp.dot(flip, value, preferred_element_type=F32).astype(BF16)
        value = value.T
        out[i % 2, i // 2] = value.reshape(out.shape[2:])
        for k, target in enumerate(outs):
            first = jnp.bitwise_xor(pos_ref[0], k) * per_device
            send = pltpu.make_async_copy(
                out.at[i % 2, i // 2, pl.ds(first, per_device)],
                target.at[:, i % 2, i // 2],
                out_sem.at[i, k],
            )
            send.start()
            sends.append(send)
    for send in sends:
        send.wait()


def ungate_kernel(pos_ref, q_ref, k_ref, *refs):
    *grads, gq_ref, gk_ref, mark_ref, grad, q_in, k_in, gq, gk, in_sem, out_sem = refs
    local = q_in.shape[0] // LANES
    per_device = grads[0].shape[0]
    owners = len(grads)
    mark_ref[...] = jnp.zeros_like(mark_ref)
    copies, sends = [], []
    for i in range(local):
        here = pl.ds(i * LANES, LANES)
        row = [
            pltpu.make_async_copy(q_ref.at[0, here], q_in.at[here], in_sem.at[i, owners]),
            pltpu.make_async_copy(k_ref.at[0, here], k_in.at[here], in_sem.at[i, owners + 1]),
        ]
        for k, source in enumerate(grads):
            first = jnp.bitwise_xor(pos_ref[0], k) * per_device
            row.append(
                pltpu.make_async_copy(
                    source.at[:, i % 2, i // 2], grad.at[i, pl.ds(first, per_device)], in_sem.at[i, k]
                )
            )
        copies.append(row)
    for row in copies:
        for copy in row:
            copy.start()
    for i in range(local):
        for copy in copies[i]:
            copy.wait()
        here = pl.ds(i * LANES, LANES)
        rows = slice(i * LANES, (i + 1) * LANES)
        value = grad[i].reshape(q_in.shape[1], LANES).T.astype(F32)
        gq[rows] = (value * k_in[rows].astype(F32)).astype(BF16)
        gk[rows] = (value * q_in[rows].astype(F32)).astype(BF16)
        for n, (source, target) in enumerate(((gq, gq_ref), (gk, gk_ref))):
            send = pltpu.make_async_copy(source.at[here], target.at[0, here], out_sem.at[i, n])
            send.start()
            sends.append(send)
    for send in sends:
        send.wait()


def clip_kernel(pos_ref, total_ref, *refs, threshold):
    *parts, _, out_ref, stage = refs
    per_device, each = stage.shape[1:3]
    for k, part in enumerate(parts):
        stage[jnp.bitwise_xor(pos_ref[0], k)] = part[...]
    total = jnp.sum(total_ref[...], axis=(0, 1, 2), keepdims=True)[0]
    factor = jnp.minimum(1.0, threshold / jnp.sqrt(total + 1e-06))
    for owner in range(stage.shape[0]):
        for n in range(each):
            rows = slice(owner * per_device, (owner + 1) * per_device)
            out_ref[rows, n * LANES : (n + 1) * LANES] = stage[owner, :, n] * factor


def spread_rows(pos_ref, sources, f, target):
    for k, source in enumerate(sources):
        count = source.shape[2] * GROUP
        at = pl.multiple_of(jnp.bitwise_xor(pos_ref[0], k) * count, count)
        for half in range(2):
            target[half, pl.ds(at, count)] = source[f, half].reshape(count, LANES)


def conv_kernel(pos_ref, filt_ref, *refs, owners, unroll):
    ins, outs, refs = refs[:owners], refs[owners : 2 * owners], refs[2 * owners :]
    taps, refs = refs[0], refs[1:]
    toeps, pads, accs = refs[:unroll], refs[unroll : 2 * unroll], refs[2 * unroll :]
    per_device, blocks = taps.shape[0], taps.shape[1] - 1
    rows = pads[0].shape[1]
    groups = filt_ref.shape[0]
    picks = max(per_device, 8)
    row_id = lax.broadcasted_iota(jnp.int32, (picks, groups), 0)
    col_id = lax.broadcasted_iota(jnp.int32, (picks, groups), 1)
    pick = (col_id == row_id + pos_ref[0] * per_device).astype(BF16)
    mine = jnp.dot(pick, filt_ref[...], preferred_element_type=F32).astype(BF16)
    empty = jnp.zeros((picks, LANES), BF16)
    mine = jnp.concatenate([empty, mine, empty], axis=1)
    row_id = lax.broadcasted_iota(jnp.int32, (2 * LANES, LANES), 0)
    col_id = lax.broadcasted_iota(jnp.int32, (2 * LANES, LANES), 1)
    flip = (row_id + col_id == LANES).astype(BF16)
    for block in range(blocks + 1):
        near = mine[:, block * LANES : (block + 2) * LANES]
        back = jnp.dot(near, flip, preferred_element_type=F32)
        for f in range(per_device):
            taps[f, block] = back[f : f + 1]
    for toep in toeps:
        toep[0] = jnp.zeros((LANES, LANES), BF16)
    row_id = lax.broadcasted_iota(jnp.int32, (LANES, LANES), 0)
    col_id = lax.broadcasted_iota(jnp.int32, (LANES, LANES), 1)
    upper = col_id >= row_id

    def one(f, toep, pad, out):
        before = None
        for block in range(blocks + 1):
            tap = jnp.broadcast_to(taps[f, block], (LANES, LANES))
            rolled = pltpu.roll(tap, 0, 1, stride=1, stride_axis=0)
            if block:
                toep[block] = jnp.where(upper, before, rolled).astype(BF16)
            before = rolled
        acc = jnp.zeros((rows, 2 * LANES), F32)
        for pair in range(blocks // 2):
            start = pair * GROUP
            left = jnp.concatenate([pad[0, start:], pad[1, start:]], axis=1)
            at = 2 * pair + 1
            top = jnp.concatenate([toep[at], toep[at - 1]], axis=1)
            low = jnp.concatenate([toep[at + 1], toep[at]], axis=1)
            right = jnp.concatenate([top, low], axis=0)
            part = jnp.dot(left, right, preferred_element_type=F32)
            if start:
                part = jnp.concatenate([part, jnp.zeros((start, 2 * LANES), F32)], axis=0)
            acc = acc + part
        for half in range(2):
            out[half] = acc[:, half * LANES : (half + 1) * LANES].astype(BF16)

    def some(i, carry):
        for u in range(unroll):
            spread_rows(pos_ref, ins, i * unroll + u, pads[u])
        for u in range(unroll):
            one(i * unroll + u, toeps[u], pads[u], accs[u])
        for u in range(unroll):
            for k, target in enumerate(outs):
                count = target.shape[2] * GROUP
                at = pl.multiple_of(jnp.bitwise_xor(pos_ref[0], k) * count, count)
                for half in range(2):
                    value = accs[u][half, pl.ds(at, count)]
                    target[i * unroll + u, half] = value.reshape(target.shape[2:])
        return carry

    lax.fori_loop(0, per_device // unroll, some, 0)


def lag_kernel(pos_ref, *refs, owners, unroll, scale):
    grads, prods, refs = refs[:owners], refs[owners : 2 * owners], refs[2 * owners + 1 :]
    raws, sum_ref, refs = refs[:owners], refs[owners], refs[owners + 1 :]
    pads, flips, lags_v, sq_v = refs[:unroll], refs[unroll : 2 * unroll], refs[-2], refs[-1]
    per_device, per_owner = raws[0].shape[:2]
    blocks = owners * per_owner
    rows = flips[0].shape[1]
    for pad in pads:
        pad[:, rows:] = jnp.zeros((2, rows, LANES), BF16)
    sq_v[...] = jnp.zeros_like(sq_v)
    row_id = lax.broadcasted_iota(jnp.int32, (LANES, LANES), 0)
    col_id = lax.broadcasted_iota(jnp.int32, (LANES, LANES), 1)
    wraps = col_id <= row_id

    def one(slot, pad, flipped):
        prod = jnp.concatenate([flipped[half].T for half in range(2)], axis=1)
        after = jnp.zeros((LANES, LANES), F32)
        sums = {}
        for pair in reversed(range(blocks // 2)):
            start = pair * GROUP
            here, later = slice(start, start + rows), slice(start + GROUP, start + GROUP + rows)
            even = jnp.concatenate([pad[0, here], pad[1, here]], axis=0)
            odd = jnp.concatenate([pad[1, here], pad[0, later]], axis=0)
            both = jnp.dot(
                prod, jnp.concatenate([even, odd], axis=1), preferred_element_type=F32
            )
            for half in (1, 0):
                rolled = pltpu.roll(
                    both[:, half * LANES : (half + 1) * LANES], 1, 1, stride=1, stride_axis=0
                )
                part = jnp.where(wraps, rolled, after)
                sums[2 * pair + half] = jnp.sum(part, axis=0, keepdims=True)
                after = rolled
        for owner in range(owners):
            lags = jnp.concatenate(
                [sums[owner * per_owner + n] for n in range(per_owner)], axis=0
            ) * scale
            lags_v[slot, owner] = lags
            sq_v[...] += lags * lags

    def some(i, carry):
        for u in range(unroll):
            spread_rows(pos_ref, grads, i * unroll + u, pads[u])
            spread_rows(pos_ref, prods, i * unroll + u, flips[u])
        for u in range(unroll):
            one(u, pads[u], flips[u])
        for u in range(unroll):
            for k, target in enumerate(raws):
                target[i * unroll + u] = lags_v[u, jnp.bitwise_xor(pos_ref[0], k)]
        return carry

    lax.fori_loop(0, per_device // unroll, some, 0)
    squares = jnp.sum(sq_v[...], axis=0, keepdims=True)
    sum_ref[...] = jnp.broadcast_to(squares[None], sum_ref.shape)


def cost(flops, moved):
    return pl.CostEstimate(flops=int(flops), bytes_accessed=int(moved), transcendentals=0)


def on_device(q_branch, k_branch, out_gate, filters, grad_out):
    seqs, block_len, chans = q_branch.shape
    owners = lax.axis_size("ctx")
    groups = chans // GROUP
    per_device = groups // owners
    local = block_len // LANES
    length = owners * block_len
    blocks = length // LANES
    rows = length * GROUP // (2 * LANES)
    scale = 4.0 / math.sqrt(seqs * GROUP)
    size = block_len * chans * 2
    anywhere = pl.BlockSpec(memory_space=pl.ANY)
    vmem = pl.BlockSpec(memory_space=pltpu.VMEM)
    smem = pl.BlockSpec(memory_space=pltpu.SMEM)
    tail = (2, local // 2, GROUP, LANES)
    whole = (owners, per_device) + tail
    pos = lax.axis_index("ctx").astype(jnp.int32).reshape(1)
    piece = jax.ShapeDtypeStruct((per_device,) + tail, BF16)
    lag_piece = jax.ShapeDtypeStruct((per_device, blocks // owners, LANES), F32)

    def gate(left, right, reverse, limit, name):
        return pl.pallas_call(
            functools.partial(gate_kernel, reverse=reverse),
            in_specs=[smem] + [pl.BlockSpec(memory_space=pltpu.HBM)] * 2,
            out_specs=[anywhere] * owners,
            out_shape=[piece] * owners,
            scratch_shapes=[
                pltpu.VMEM((block_len, chans), BF16),
                pltpu.VMEM((block_len, chans), BF16),
                pltpu.VMEM((2, local // 2, groups, GROUP, LANES), BF16),
                pltpu.SemaphoreType.DMA((local, 2)),
                pltpu.SemaphoreType.DMA((local, owners)),
            ],
            cost_estimate=cost(block_len * chans, 3 * size),
            compiler_params=pltpu.CompilerParams(vmem_limit_bytes=limit << 20),
            name=name,
        )(pos, left, right)

    def swap(values):
        out = [values[0]]
        for k in range(1, owners):
            out.append(lax.ppermute(values[k], "ctx", [(i, i ^ k) for i in range(owners)]))
        return out

    grad_got = swap(gate(grad_out, out_gate, False, 56, "gate_grad"))
    prod_got = swap(gate(q_branch, k_branch, True, 12, "gate_prod"))
    unroll = math.gcd(4, per_device)
    conv = pl.pallas_call(
        functools.partial(conv_kernel, owners=owners, unroll=unroll),
        in_specs=[smem] + [vmem] * (1 + owners),
        out_specs=[vmem] * owners,
        out_shape=[piece] * owners,
        scratch_shapes=[pltpu.VMEM((per_device, blocks + 1, 1, LANES), F32)]
        + [pltpu.VMEM((blocks + 1, LANES, LANES), BF16)] * unroll
        + [pltpu.VMEM((2, rows, LANES), BF16)] * (2 * unroll),
        cost_estimate=cost(per_device * rows * length * 4096, 2 * size + groups * length * 2),
        compiler_params=pltpu.CompilerParams(vmem_limit_bytes=16 << 20),
        name="conv",
    )(pos, filters, *grad_got)
    back = swap(conv)
    both = ("ctx", "ch")
    count = lax.axis_size(both)
    unroll = math.gcd(8, per_device)
    *raw, spread = pl.pallas_call(
        functools.partial(lag_kernel, owners=owners, unroll=unroll, scale=scale),
        in_specs=[smem] + [vmem] * (2 * owners) + [anywhere],
        out_specs=[vmem] * (owners + 1),
        out_shape=[lag_piece] * owners + [jax.ShapeDtypeStruct((count, 1, LANES), F32)],
        scratch_shapes=[pltpu.VMEM((2, 2 * rows, LANES), BF16)] * unroll
        + [pltpu.VMEM((2, rows, LANES), BF16)] * unroll
        + [
            pltpu.VMEM((unroll, owners, blocks // owners, LANES), F32),
            pltpu.VMEM((blocks // owners, LANES), F32),
        ],
        cost_estimate=cost(per_device * 2 * rows * length * 2048, 2 * size + per_device * length * 4),
        compiler_params=pltpu.CompilerParams(vmem_limit_bytes=16 << 20),
        name="lags",
    )(pos, *grad_got, *prod_got, conv[0])
    total = lax.all_to_all(spread, both, 0, 0, tiled=True)
    raw = swap(raw)
    threshold = math.sqrt(WIDTH // GROUP * length)
    grad_q, grad_k, mark = pl.pallas_call(
        ungate_kernel,
        in_specs=[smem] + [anywhere] * (2 + owners),
        out_specs=[anywhere] * 2 + [vmem],
        out_shape=[jax.ShapeDtypeStruct(q_branch.shape, BF16)] * 2
        + [jax.ShapeDtypeStruct((8, LANES), F32)],
        scratch_shapes=[
            pltpu.VMEM((local, groups, GROUP, LANES), BF16),
            pltpu.VMEM((block_len, chans), BF16),
            pltpu.VMEM((block_len, chans), BF16),
            pltpu.VMEM((block_len, chans), BF16),
            pltpu.VMEM((block_len, chans), BF16),
            pltpu.SemaphoreType.DMA((local, owners + 2)),
            pltpu.SemaphoreType.DMA((local, 2)),
        ],
        cost_estimate=cost(2 * block_len * chans, 5 * size),
        compiler_params=pltpu.CompilerParams(vmem_limit_bytes=16 << 20),
        name="ungate",
    )(pos, q_branch, k_branch, *back)
    grad_filters = pl.pallas_call(
        functools.partial(clip_kernel, threshold=threshold),
        in_specs=[smem] + [vmem] * (2 + owners),
        out_specs=vmem,
        out_shape=jax.ShapeDtypeStruct((groups, length // owners), F32),
        scratch_shapes=[pltpu.VMEM((owners, per_device, blocks // owners, LANES), F32)],
        cost_estimate=cost(groups * length, groups * length * 4),
        compiler_params=pltpu.CompilerParams(vmem_limit_bytes=8 << 20),
        name="clip",
    )(pos, total, *raw, mark)
    return (grad_q, grad_k, grad_filters)


def solution(mesh):
    return jax.shard_map(
        on_device,
        mesh=mesh,
        in_specs=(
            P(None, "ctx", "ch"),
            P(None, "ctx", "ch"),
            P(None, "ctx", "ch"),
            P("ch", None),
            P(None, "ctx", "ch"),
        ),
        out_specs=(P(None, "ctx", "ch"), P(None, "ctx", "ch"), P("ch", "ctx")),
        check_vma=False,
    )
```

```python
import functools
import math

import jax
import jax.numpy as jnp
from jax import lax
from jax.experimental import pallas as pl
from jax.experimental.pallas import tpu as pltpu
from jax.sharding import PartitionSpec as P

WIDTH = 8192
GROUP = 16
LANES = 128
NT = (((1,), (1,)), ((), ()))
BF16, F32 = jnp.bfloat16, jnp.float32


def gate_kernel(pos_ref, left_ref, right_ref, *refs, reverse, chunks):
    *outs, left, right, out, in_sem, out_sem = refs
    local = left.shape[0] // LANES
    each = outs[0].shape[0]
    copies = []
    for i in range(local):
        here = pl.ds(i * LANES, LANES)
        copies.append(
            (
                pltpu.make_async_copy(left_ref.at[0, here], left.at[here], in_sem.at[i, 0]),
                pltpu.make_async_copy(right_ref.at[0, here], right.at[here], in_sem.at[i, 1]),
            )
        )
    for pair in copies:
        for copy in pair:
            copy.start()
    sends = []
    for i in range(local):
        for copy in copies[i]:
            copy.wait()
        rows = slice(i * LANES, (i + 1) * LANES)
        value = (left[rows].astype(F32) * right[rows].astype(F32)).astype(BF16)
        if reverse:
            row_id = lax.broadcasted_iota(jnp.int32, (LANES, LANES), 0)
            col_id = lax.broadcasted_iota(jnp.int32, (LANES, LANES), 1)
            flip = (row_id + col_id == LANES - 1).astype(BF16)
            value = jnp.dot(flip, value, preferred_element_type=F32).astype(BF16)
        value = value.T
        out[i % 2, i // 2] = value.reshape(out.shape[2:])
        for n, target in enumerate(outs):
            first = (jnp.bitwise_xor(pos_ref[0], n // chunks) * chunks + n % chunks) * each
            send = pltpu.make_async_copy(
                out.at[i % 2, i // 2, pl.ds(first, each)],
                target.at[:, i % 2, i // 2],
                out_sem.at[i, n],
            )
            send.start()
            sends.append(send)
    for send in sends:
        send.wait()


def ungate_kernel(pos_ref, q_ref, k_ref, *refs):
    *grads, gq_ref, gk_ref, mark_ref, grad, q_in, k_in, gq, gk, in_sem, out_sem = refs
    local = q_in.shape[0] // LANES
    per_device = grads[0].shape[0]
    owners = len(grads)
    mark_ref[...] = jnp.zeros_like(mark_ref)
    copies, sends = [], []
    for i in range(local):
        here = pl.ds(i * LANES, LANES)
        row = [
            pltpu.make_async_copy(q_ref.at[0, here], q_in.at[here], in_sem.at[i, owners]),
            pltpu.make_async_copy(k_ref.at[0, here], k_in.at[here], in_sem.at[i, owners + 1]),
        ]
        for k, source in enumerate(grads):
            first = jnp.bitwise_xor(pos_ref[0], k) * per_device
            row.append(
                pltpu.make_async_copy(
                    source.at[:, i % 2, i // 2], grad.at[i, pl.ds(first, per_device)], in_sem.at[i, k]
                )
            )
        copies.append(row)
    for row in copies:
        for copy in row:
            copy.start()
    for i in range(local):
        for copy in copies[i]:
            copy.wait()
        here = pl.ds(i * LANES, LANES)
        rows = slice(i * LANES, (i + 1) * LANES)
        value = grad[i].reshape(q_in.shape[1], LANES).T.astype(F32)
        gq[rows] = (value * k_in[rows].astype(F32)).astype(BF16)
        gk[rows] = (value * q_in[rows].astype(F32)).astype(BF16)
        for n, (source, target) in enumerate(((gq, gq_ref), (gk, gk_ref))):
            send = pltpu.make_async_copy(source.at[here], target.at[0, here], out_sem.at[i, n])
            send.start()
            sends.append(send)
    for send in sends:
        send.wait()


def clip_kernel(pos_ref, total_ref, *refs, threshold):
    *parts, _, out_ref, stage = refs
    per_device, each = stage.shape[1:3]
    for k, part in enumerate(parts):
        stage[jnp.bitwise_xor(pos_ref[0], k)] = part[...]
    total = jnp.sum(total_ref[...], axis=(0, 1, 2), keepdims=True)[0]
    factor = jnp.minimum(1.0, threshold / jnp.sqrt(total + 1e-06))
    for owner in range(stage.shape[0]):
        for n in range(each):
            rows = slice(owner * per_device, (owner + 1) * per_device)
            out_ref[rows, n * LANES : (n + 1) * LANES] = stage[owner, :, n] * factor


def spread_rows(pos_ref, sources, f, target):
    for k, source in enumerate(sources):
        count = source.shape[2] * GROUP
        at = pl.multiple_of(jnp.bitwise_xor(pos_ref[0], k) * count, count)
        for half in range(2):
            target[half, pl.ds(at, count)] = source[f, half].reshape(count, LANES)


def reverse_taps(owner, filt_ref, taps):
    per_device, blocks = taps.shape[0], taps.shape[1] - 1
    groups = filt_ref.shape[0]
    picks = max(per_device, 8)
    row_id = lax.broadcasted_iota(jnp.int32, (picks, groups), 0)
    col_id = lax.broadcasted_iota(jnp.int32, (picks, groups), 1)
    pick = (col_id == row_id + owner * per_device).astype(BF16)
    width = min((blocks + 1) * LANES, filt_ref.shape[1])
    mine = jnp.dot(pick, filt_ref[:, :width], preferred_element_type=F32).astype(BF16)
    empty = jnp.zeros((picks, LANES), BF16)
    mine = jnp.concatenate([empty, mine, empty], axis=1)
    row_id = lax.broadcasted_iota(jnp.int32, (2 * LANES, LANES), 0)
    col_id = lax.broadcasted_iota(jnp.int32, (2 * LANES, LANES), 1)
    flip = (row_id + col_id == LANES).astype(BF16)
    for block in range(blocks + 1):
        near = mine[:, block * LANES : (block + 2) * LANES]
        back = jnp.dot(near, flip, preferred_element_type=F32)
        for f in range(per_device):
            taps[f, block] = back[f : f + 1]


def build_blocks(taps, f, toep):
    row_id = lax.broadcasted_iota(jnp.int32, (LANES, LANES), 0)
    col_id = lax.broadcasted_iota(jnp.int32, (LANES, LANES), 1)
    upper = col_id >= row_id
    before = None
    for block in range(taps.shape[1]):
        tap = jnp.broadcast_to(taps[f, block], (LANES, LANES))
        rolled = pltpu.roll(tap, 0, 1, stride=1, stride_axis=0)
        if block:
            toep[block] = jnp.where(upper, before, rolled).astype(BF16)
        before = rolled


def weights(toep, pair):
    at = 2 * pair + 1
    top = jnp.concatenate([toep[at], toep[at - 1]], axis=1)
    low = jnp.concatenate([toep[at + 1], toep[at]], axis=1)
    return jnp.concatenate([top, low], axis=0)


def conv_kernel(pos_ref, filt_ref, *refs, owners, unroll):
    ins, outs, refs = refs[:owners], refs[owners : 2 * owners], refs[2 * owners :]
    taps, refs = refs[0], refs[1:]
    toeps, pads, accs = refs[:unroll], refs[unroll : 2 * unroll], refs[2 * unroll :]
    per_device, blocks = taps.shape[0], taps.shape[1] - 1
    rows = pads[0].shape[1]
    reverse_taps(pos_ref[0], filt_ref, taps)
    for toep in toeps:
        toep[0] = jnp.zeros((LANES, LANES), BF16)

    def one(f, toep, pad, out):
        build_blocks(taps, f, toep)
        acc = jnp.zeros((rows, 2 * LANES), F32)
        for pair in range(blocks // 2):
            start = pair * GROUP
            left = jnp.concatenate([pad[0, start:], pad[1, start:]], axis=1)
            part = jnp.dot(left, weights(toep, pair), preferred_element_type=F32)
            if start:
                part = jnp.concatenate([part, jnp.zeros((start, 2 * LANES), F32)], axis=0)
            acc = acc + part
        for half in range(2):
            out[half] = acc[:, half * LANES : (half + 1) * LANES].astype(BF16)

    def some(i, carry):
        for u in range(unroll):
            spread_rows(pos_ref, ins, i * unroll + u, pads[u])
        for u in range(unroll):
            one(i * unroll + u, toeps[u], pads[u], accs[u])
        for u in range(unroll):
            for k, target in enumerate(outs):
                count = target.shape[2] * GROUP
                at = pl.multiple_of(jnp.bitwise_xor(pos_ref[0], k) * count, count)
                for half in range(2):
                    value = accs[u][half, pl.ds(at, count)]
                    target[i * unroll + u, half] = value.reshape(target.shape[2:])
        return carry

    lax.fori_loop(0, per_device // unroll, some, 0)


def lag_sums(pad, flipped, rows, blocks):
    row_id = lax.broadcasted_iota(jnp.int32, (LANES, LANES), 0)
    col_id = lax.broadcasted_iota(jnp.int32, (LANES, LANES), 1)
    wraps = col_id <= row_id
    prod = jnp.concatenate([flipped[half, :rows].T for half in range(2)], axis=1)
    after = jnp.zeros((LANES, LANES), F32)
    sums = {}
    for pair in reversed(range(blocks // 2)):
        start = pair * GROUP
        here, later = slice(start, start + rows), slice(start + GROUP, start + GROUP + rows)
        even = jnp.concatenate([pad[0, here], pad[1, here]], axis=0)
        odd = jnp.concatenate([pad[1, here], pad[0, later]], axis=0)
        both = jnp.dot(prod, jnp.concatenate([even, odd], axis=1), preferred_element_type=F32)
        for half in (1, 0):
            rolled = pltpu.roll(
                both[:, half * LANES : (half + 1) * LANES], 1, 1, stride=1, stride_axis=0
            )
            part = jnp.where(wraps, rolled, after)
            sums[2 * pair + half] = jnp.sum(part, axis=0, keepdims=True)
            after = rolled
    return sums


def lag_kernel(pos_ref, *refs, owners, unroll, scale, first, last):
    grads, prods, refs = refs[:owners], refs[owners : 2 * owners], refs[2 * owners :]
    olds, refs = (refs[: owners + 1], refs[owners + 1 :]) if first else ([], refs[1:])
    raws, sum_ref, refs = refs[:owners], refs[owners], refs[owners + 1 :]
    pads, flips, lags_v, sq_v = refs[:unroll], refs[unroll : 2 * unroll], refs[-2], refs[-1]
    per_owner = raws[0].shape[1]
    blocks = owners * per_owner
    rows = flips[0].shape[1]
    for pad in pads:
        pad[:, rows:] = jnp.zeros((2, rows, LANES), BF16)
    sq_v[...] = olds[-1][...] if olds else jnp.zeros_like(sq_v)
    for old, target in zip(olds, raws):
        target[:first] = old[...]

    def one(slot, pad, flipped):
        sums = lag_sums(pad, flipped, rows, blocks)
        for owner in range(owners):
            lags = jnp.concatenate(
                [sums[owner * per_owner + n] for n in range(per_owner)], axis=0
            ) * scale
            lags_v[slot, owner] = lags
            sq_v[...] += lags * lags

    def some(i, carry):
        for u in range(unroll):
            spread_rows(pos_ref, grads, first + i * unroll + u, pads[u])
            spread_rows(pos_ref, prods, i * unroll + u, flips[u])
        for u in range(unroll):
            one(u, pads[u], flips[u])
        for u in range(unroll):
            for k, target in enumerate(raws):
                target[first + i * unroll + u] = lags_v[u, jnp.bitwise_xor(pos_ref[0], k)]
        return carry

    lax.fori_loop(0, prods[0].shape[0] // unroll, some, 0)
    if not last:
        sum_ref[...] = sq_v[...]
        return
    squares = jnp.sum(sq_v[...], axis=0, keepdims=True)
    sum_ref[...] = jnp.zeros_like(sum_ref)
    sum_ref[:, :1] = jnp.broadcast_to(squares[None], (sum_ref.shape[0], 1, LANES))


def cost(flops, moved):
    return pl.CostEstimate(flops=int(flops), bytes_accessed=int(moved), transcendentals=0)


def on_device(q_branch, k_branch, out_gate, filters, grad_out):
    seqs, block_len, chans = q_branch.shape
    owners = lax.axis_size("ctx")
    groups = chans // GROUP
    per_device = groups // owners
    local = block_len // LANES
    length = owners * block_len
    blocks = length // LANES
    rows = length * GROUP // (2 * LANES)
    scale = 4.0 / math.sqrt(seqs * GROUP)
    size = block_len * chans * 2
    anywhere = pl.BlockSpec(memory_space=pl.ANY)
    vmem = pl.BlockSpec(memory_space=pltpu.VMEM)
    smem = pl.BlockSpec(memory_space=pltpu.SMEM)
    tail = (2, local // 2, GROUP, LANES)
    whole = (owners, per_device) + tail
    pos = lax.axis_index("ctx").astype(jnp.int32).reshape(1)
    piece = jax.ShapeDtypeStruct((per_device,) + tail, BF16)
    lag_piece = jax.ShapeDtypeStruct((per_device, blocks // owners, LANES), F32)

    def gate(left, right, reverse, chunks, limit, name):
        part = jax.ShapeDtypeStruct((per_device // chunks,) + tail, BF16)
        out = pl.pallas_call(
            functools.partial(gate_kernel, reverse=reverse, chunks=chunks),
            in_specs=[smem] + [pl.BlockSpec(memory_space=pltpu.HBM)] * 2,
            out_specs=[anywhere] * (owners * chunks),
            out_shape=[part] * (owners * chunks),
            scratch_shapes=[
                pltpu.VMEM((block_len, chans), BF16),
                pltpu.VMEM((block_len, chans), BF16),
                pltpu.VMEM((2, local // 2, groups, GROUP, LANES), BF16),
                pltpu.SemaphoreType.DMA((local, 2)),
                pltpu.SemaphoreType.DMA((local, owners * chunks)),
            ],
            cost_estimate=cost(block_len * chans, 3 * size),
            compiler_params=pltpu.CompilerParams(vmem_limit_bytes=limit << 20),
            name=name,
        )(pos, left, right)
        return [out[n::chunks] for n in range(chunks)]

    def swap(values):
        out = [values[0]]
        for k in range(1, owners):
            out.append(lax.ppermute(values[k], "ctx", [(i, i ^ k) for i in range(owners)]))
        return out

    chunks = 1
    (grad_send,) = gate(grad_out, out_gate, False, 1, 56, "gate_grad")
    grad_got = swap(grad_send)
    prod_got = [swap(part) for part in gate(q_branch, k_branch, True, chunks, 12, "gate_prod")]
    unroll = math.gcd(4, per_device)
    conv = pl.pallas_call(
        functools.partial(conv_kernel, owners=owners, unroll=unroll),
        in_specs=[smem] + [vmem] * (1 + owners),
        out_specs=[vmem] * owners,
        out_shape=[piece] * owners,
        scratch_shapes=[pltpu.VMEM((per_device, blocks + 1, 1, LANES), F32)]
        + [pltpu.VMEM((blocks + 1, LANES, LANES), BF16)] * unroll
        + [pltpu.VMEM((2, rows, LANES), BF16)] * (2 * unroll),
        cost_estimate=cost(per_device * rows * length * 4096, 2 * size + groups * length * 2),
        compiler_params=pltpu.CompilerParams(vmem_limit_bytes=16 << 20),
        name="conv",
    )(pos, filters, *grad_got)
    back = swap(conv)
    both = ("ctx", "ch")
    count = lax.axis_size(both)
    each = per_device // chunks
    unroll = math.gcd(8, each)
    old = [conv[0]]
    for n in range(chunks):
        last = n == chunks - 1
        done = jax.ShapeDtypeStruct(((n + 1) * each, blocks // owners, LANES), F32)
        sums = jax.ShapeDtypeStruct((count, 8, LANES) if last else (blocks // owners, LANES), F32)
        old = pl.pallas_call(
            functools.partial(
                lag_kernel, owners=owners, unroll=unroll, scale=scale, first=n * each, last=last
            ),
            in_specs=[smem] + [vmem] * (2 * owners) + ([vmem] * (owners + 1) if n else [anywhere]),
            out_specs=[vmem] * (owners + 1),
            out_shape=[done] * owners + [sums],
            scratch_shapes=[pltpu.VMEM((2, 2 * rows, LANES), BF16)] * unroll
            + [pltpu.VMEM((2, rows, LANES), BF16)] * unroll
            + [
                pltpu.VMEM((unroll, owners, blocks // owners, LANES), F32),
                pltpu.VMEM((blocks // owners, LANES), F32),
            ],
            cost_estimate=cost(each * 2 * rows * length * 2048, 2 * size),
            compiler_params=pltpu.CompilerParams(vmem_limit_bytes=16 << 20),
            name="lags",
        )(pos, *grad_got, *prod_got[n], *old)
    *raw, spread = old
    total = lax.all_to_all(spread, both, 0, 0, tiled=True)
    raw = swap(raw)
    threshold = math.sqrt(WIDTH // GROUP * length)
    grad_q, grad_k, mark = pl.pallas_call(
        ungate_kernel,
        in_specs=[smem] + [anywhere] * (2 + owners),
        out_specs=[anywhere] * 2 + [vmem],
        out_shape=[jax.ShapeDtypeStruct(q_branch.shape, BF16)] * 2
        + [jax.ShapeDtypeStruct((8, LANES), F32)],
        scratch_shapes=[
            pltpu.VMEM((local, groups, GROUP, LANES), BF16),
            pltpu.VMEM((block_len, chans), BF16),
            pltpu.VMEM((block_len, chans), BF16),
            pltpu.VMEM((block_len, chans), BF16),
            pltpu.VMEM((block_len, chans), BF16),
            pltpu.SemaphoreType.DMA((local, owners + 2)),
            pltpu.SemaphoreType.DMA((local, 2)),
        ],
        cost_estimate=cost(2 * block_len * chans, 5 * size),
        compiler_params=pltpu.CompilerParams(vmem_limit_bytes=16 << 20),
        name="ungate",
    )(pos, q_branch, k_branch, *back)
    grad_filters = pl.pallas_call(
        functools.partial(clip_kernel, threshold=threshold),
        in_specs=[smem] + [vmem] * (2 + owners),
        out_specs=vmem,
        out_shape=jax.ShapeDtypeStruct((groups, length // owners), F32),
        scratch_shapes=[pltpu.VMEM((owners, per_device, blocks // owners, LANES), F32)],
        cost_estimate=cost(groups * length, groups * length * 4),
        compiler_params=pltpu.CompilerParams(vmem_limit_bytes=8 << 20),
        name="clip",
    )(pos, total, *raw, mark)
    return (grad_q, grad_k, grad_filters)


def solution(mesh):
    return jax.shard_map(
        on_device,
        mesh=mesh,
        in_specs=(
            P(None, "ctx", "ch"),
            P(None, "ctx", "ch"),
            P(None, "ctx", "ch"),
            P("ch", None),
            P(None, "ctx", "ch"),
        ),
        out_specs=(P(None, "ctx", "ch"), P(None, "ctx", "ch"), P("ch", "ctx")),
        check_vma=False,
    )
```

```python
import functools
import math

import jax
import jax.numpy as jnp
from jax import lax
from jax.experimental import pallas as pl
from jax.experimental.pallas import tpu as pltpu
from jax.sharding import PartitionSpec as P

WIDTH = 8192
GROUP = 16
LANES = 128
NT = (((1,), (1,)), ((), ()))
BF16, F32 = jnp.bfloat16, jnp.float32


def gate_kernel(pos_ref, left_ref, right_ref, *refs, reverse, chunks):
    *outs, left, right, out, in_sem, out_sem = refs
    local = left.shape[0] // LANES
    each = outs[0].shape[0]
    copies = []
    for i in range(local):
        here = pl.ds(i * LANES, LANES)
        copies.append(
            (
                pltpu.make_async_copy(left_ref.at[0, here], left.at[here], in_sem.at[i, 0]),
                pltpu.make_async_copy(right_ref.at[0, here], right.at[here], in_sem.at[i, 1]),
            )
        )
    for pair in copies:
        for copy in pair:
            copy.start()
    sends = []
    for i in range(local):
        for copy in copies[i]:
            copy.wait()
        rows = slice(i * LANES, (i + 1) * LANES)
        value = (left[rows].astype(F32) * right[rows].astype(F32)).astype(BF16)
        if reverse:
            row_id = lax.broadcasted_iota(jnp.int32, (LANES, LANES), 0)
            col_id = lax.broadcasted_iota(jnp.int32, (LANES, LANES), 1)
            flip = (row_id + col_id == LANES - 1).astype(BF16)
            value = jnp.dot(flip, value, preferred_element_type=F32).astype(BF16)
        value = value.T
        out[i % 2, i // 2] = value.reshape(out.shape[2:])
        for n, target in enumerate(outs):
            first = (jnp.bitwise_xor(pos_ref[0], n // chunks) * chunks + n % chunks) * each
            send = pltpu.make_async_copy(
                out.at[i % 2, i // 2, pl.ds(first, each)],
                target.at[:, i % 2, i // 2],
                out_sem.at[i, n],
            )
            send.start()
            sends.append(send)
    for send in sends:
        send.wait()


def ungate_kernel(pos_ref, q_ref, k_ref, *refs):
    *grads, gq_ref, gk_ref, mark_ref, grad, q_in, k_in, gq, gk, in_sem, out_sem = refs
    local = q_in.shape[0] // LANES
    per_device = grads[0].shape[0]
    owners = len(grads)
    mark_ref[...] = jnp.zeros_like(mark_ref)
    copies, sends = [], []
    for i in range(local):
        here = pl.ds(i * LANES, LANES)
        row = [
            pltpu.make_async_copy(q_ref.at[0, here], q_in.at[here], in_sem.at[i, owners]),
            pltpu.make_async_copy(k_ref.at[0, here], k_in.at[here], in_sem.at[i, owners + 1]),
        ]
        for k, source in enumerate(grads):
            first = jnp.bitwise_xor(pos_ref[0], k) * per_device
            row.append(
                pltpu.make_async_copy(
                    source.at[:, i % 2, i // 2], grad.at[i, pl.ds(first, per_device)], in_sem.at[i, k]
                )
            )
        copies.append(row)
    for row in copies:
        for copy in row:
            copy.start()
    for i in range(local):
        for copy in copies[i]:
            copy.wait()
        here = pl.ds(i * LANES, LANES)
        rows = slice(i * LANES, (i + 1) * LANES)
        value = grad[i].reshape(q_in.shape[1], LANES).T.astype(F32)
        gq[rows] = (value * k_in[rows].astype(F32)).astype(BF16)
        gk[rows] = (value * q_in[rows].astype(F32)).astype(BF16)
        for n, (source, target) in enumerate(((gq, gq_ref), (gk, gk_ref))):
            send = pltpu.make_async_copy(source.at[here], target.at[0, here], out_sem.at[i, n])
            send.start()
            sends.append(send)
    for send in sends:
        send.wait()


def clip_kernel(pos_ref, total_ref, *refs, threshold):
    *parts, _, out_ref, stage = refs
    per_device, each = stage.shape[1:3]
    for k, part in enumerate(parts):
        stage[jnp.bitwise_xor(pos_ref[0], k)] = part[...]
    total = jnp.sum(total_ref[...], axis=(0, 1, 2), keepdims=True)[0]
    factor = jnp.minimum(1.0, threshold / jnp.sqrt(total + 1e-06))
    for owner in range(stage.shape[0]):
        for n in range(each):
            rows = slice(owner * per_device, (owner + 1) * per_device)
            out_ref[rows, n * LANES : (n + 1) * LANES] = stage[owner, :, n] * factor


def spread_rows(pos_ref, sources, f, target):
    for k, source in enumerate(sources):
        count = source.shape[2] * GROUP
        at = pl.multiple_of(jnp.bitwise_xor(pos_ref[0], k) * count, count)
        for half in range(2):
            target[half, pl.ds(at, count)] = source[f, half].reshape(count, LANES)


def reverse_taps(owner, filt_ref, taps):
    per_device, blocks = taps.shape[0], taps.shape[1] - 1
    groups = filt_ref.shape[0]
    picks = max(per_device, 8)
    row_id = lax.broadcasted_iota(jnp.int32, (picks, groups), 0)
    col_id = lax.broadcasted_iota(jnp.int32, (picks, groups), 1)
    pick = (col_id == row_id + owner * per_device).astype(BF16)
    width = min((blocks + 1) * LANES, filt_ref.shape[1])
    mine = jnp.dot(pick, filt_ref[:, :width], preferred_element_type=F32).astype(BF16)
    empty = jnp.zeros((picks, LANES), BF16)
    mine = jnp.concatenate([empty, mine, empty], axis=1)
    row_id = lax.broadcasted_iota(jnp.int32, (2 * LANES, LANES), 0)
    col_id = lax.broadcasted_iota(jnp.int32, (2 * LANES, LANES), 1)
    flip = (row_id + col_id == LANES).astype(BF16)
    for block in range(blocks + 1):
        near = mine[:, block * LANES : (block + 2) * LANES]
        back = jnp.dot(near, flip, preferred_element_type=F32)
        for f in range(per_device):
            taps[f, block] = back[f : f + 1]


def build_blocks(taps, f, toep):
    row_id = lax.broadcasted_iota(jnp.int32, (LANES, LANES), 0)
    col_id = lax.broadcasted_iota(jnp.int32, (LANES, LANES), 1)
    upper = col_id >= row_id
    before = None
    for block in range(taps.shape[1]):
        tap = jnp.broadcast_to(taps[f, block], (LANES, LANES))
        rolled = pltpu.roll(tap, 0, 1, stride=1, stride_axis=0)
        if block:
            toep[block] = jnp.where(upper, before, rolled).astype(BF16)
        before = rolled


def weights(toep, pair):
    at = 2 * pair + 1
    top = jnp.concatenate([toep[at], toep[at - 1]], axis=1)
    low = jnp.concatenate([toep[at + 1], toep[at]], axis=1)
    return jnp.concatenate([top, low], axis=0)


def conv_kernel(pos_ref, filt_ref, *refs, owners, unroll):
    ins, outs, refs = refs[:owners], refs[owners : 2 * owners], refs[2 * owners :]
    taps, refs = refs[0], refs[1:]
    toeps, pads, accs = refs[:unroll], refs[unroll : 2 * unroll], refs[2 * unroll :]
    per_device, blocks = taps.shape[0], taps.shape[1] - 1
    rows = pads[0].shape[1]
    reverse_taps(pos_ref[0], filt_ref, taps)
    for toep in toeps:
        toep[0] = jnp.zeros((LANES, LANES), BF16)

    def one(f, toep, pad, out):
        build_blocks(taps, f, toep)
        acc = jnp.zeros((rows, 2 * LANES), F32)
        for pair in range(blocks // 2):
            start = pair * GROUP
            left = jnp.concatenate([pad[0, start:], pad[1, start:]], axis=1)
            part = jnp.dot(left, weights(toep, pair), preferred_element_type=F32)
            if start:
                part = jnp.concatenate([part, jnp.zeros((start, 2 * LANES), F32)], axis=0)
            acc = acc + part
        for half in range(2):
            out[half] = acc[:, half * LANES : (half + 1) * LANES].astype(BF16)

    def some(i, carry):
        for u in range(unroll):
            spread_rows(pos_ref, ins, i * unroll + u, pads[u])
        for u in range(unroll):
            one(i * unroll + u, toeps[u], pads[u], accs[u])
        for u in range(unroll):
            for k, target in enumerate(outs):
                count = target.shape[2] * GROUP
                at = pl.multiple_of(jnp.bitwise_xor(pos_ref[0], k) * count, count)
                for half in range(2):
                    value = accs[u][half, pl.ds(at, count)]
                    target[i * unroll + u, half] = value.reshape(target.shape[2:])
        return carry

    lax.fori_loop(0, per_device // unroll, some, 0)


def lag_sums(pad, flipped, rows, blocks):
    row_id = lax.broadcasted_iota(jnp.int32, (LANES, LANES), 0)
    col_id = lax.broadcasted_iota(jnp.int32, (LANES, LANES), 1)
    wraps = col_id <= row_id
    prod = jnp.concatenate([flipped[half, :rows].T for half in range(2)], axis=1)
    after = jnp.zeros((LANES, LANES), F32)
    sums = {}
    for pair in reversed(range(blocks // 2)):
        start = pair * GROUP
        here, later = slice(start, start + rows), slice(start + GROUP, start + GROUP + rows)
        even = jnp.concatenate([pad[0, here], pad[1, here]], axis=0)
        odd = jnp.concatenate([pad[1, here], pad[0, later]], axis=0)
        both = jnp.dot(prod, jnp.concatenate([even, odd], axis=1), preferred_element_type=F32)
        for half in (1, 0):
            rolled = pltpu.roll(
                both[:, half * LANES : (half + 1) * LANES], 1, 1, stride=1, stride_axis=0
            )
            part = jnp.where(wraps, rolled, after)
            sums[2 * pair + half] = jnp.sum(part, axis=0, keepdims=True)
            after = rolled
    return sums


def lag_kernel(pos_ref, *refs, owners, unroll, scale, first, last):
    grads, prods, refs = refs[:owners], refs[owners : 2 * owners], refs[2 * owners :]
    olds, refs = (refs[: owners + 1], refs[owners + 1 :]) if first else ([], refs[1:])
    raws, sum_ref, refs = refs[:owners], refs[owners], refs[owners + 1 :]
    pads, flips, lags_v, sq_v = refs[:unroll], refs[unroll : 2 * unroll], refs[-2], refs[-1]
    per_owner = raws[0].shape[1]
    blocks = owners * per_owner
    rows = flips[0].shape[1]
    for pad in pads:
        pad[:, rows:] = jnp.zeros((2, rows, LANES), BF16)
    sq_v[...] = olds[-1][...] if olds else jnp.zeros_like(sq_v)
    for old, target in zip(olds, raws):
        target[:first] = old[...]

    def one(slot, pad, flipped):
        sums = lag_sums(pad, flipped, rows, blocks)
        for owner in range(owners):
            lags = jnp.concatenate(
                [sums[owner * per_owner + n] for n in range(per_owner)], axis=0
            ) * scale
            lags_v[slot, owner] = lags
            sq_v[...] += lags * lags

    def some(i, carry):
        for u in range(unroll):
            spread_rows(pos_ref, grads, first + i * unroll + u, pads[u])
            spread_rows(pos_ref, prods, i * unroll + u, flips[u])
        for u in range(unroll):
            one(u, pads[u], flips[u])
        for u in range(unroll):
            for k, target in enumerate(raws):
                target[first + i * unroll + u] = lags_v[u, jnp.bitwise_xor(pos_ref[0], k)]
        return carry

    lax.fori_loop(0, prods[0].shape[0] // unroll, some, 0)
    if not last:
        sum_ref[...] = sq_v[...]
        return
    squares = jnp.sum(sq_v[...], axis=0, keepdims=True)
    sum_ref[...] = jnp.zeros_like(sum_ref)
    sum_ref[:, :1] = jnp.broadcast_to(squares[None], (sum_ref.shape[0], 1, LANES))


def cost(flops, moved):
    return pl.CostEstimate(flops=int(flops), bytes_accessed=int(moved), transcendentals=0)


def on_device(q_branch, k_branch, out_gate, filters, grad_out):
    seqs, block_len, chans = q_branch.shape
    owners = lax.axis_size("ctx")
    groups = chans // GROUP
    per_device = groups // owners
    local = block_len // LANES
    length = owners * block_len
    blocks = length // LANES
    rows = length * GROUP // (2 * LANES)
    scale = 4.0 / math.sqrt(seqs * GROUP)
    size = block_len * chans * 2
    anywhere = pl.BlockSpec(memory_space=pl.ANY)
    vmem = pl.BlockSpec(memory_space=pltpu.VMEM)
    smem = pl.BlockSpec(memory_space=pltpu.SMEM)
    tail = (2, local // 2, GROUP, LANES)
    whole = (owners, per_device) + tail
    pos = lax.axis_index("ctx").astype(jnp.int32).reshape(1)
    piece = jax.ShapeDtypeStruct((per_device,) + tail, BF16)
    lag_piece = jax.ShapeDtypeStruct((per_device, blocks // owners, LANES), F32)

    def gate(left, right, reverse, chunks, limit, name):
        part = jax.ShapeDtypeStruct((per_device // chunks,) + tail, BF16)
        out = pl.pallas_call(
            functools.partial(gate_kernel, reverse=reverse, chunks=chunks),
            in_specs=[smem] + [pl.BlockSpec(memory_space=pltpu.HBM)] * 2,
            out_specs=[anywhere] * (owners * chunks),
            out_shape=[part] * (owners * chunks),
            scratch_shapes=[
                pltpu.VMEM((block_len, chans), BF16),
                pltpu.VMEM((block_len, chans), BF16),
                pltpu.VMEM((2, local // 2, groups, GROUP, LANES), BF16),
                pltpu.SemaphoreType.DMA((local, 2)),
                pltpu.SemaphoreType.DMA((local, owners * chunks)),
            ],
            cost_estimate=cost(block_len * chans, 3 * size),
            compiler_params=pltpu.CompilerParams(vmem_limit_bytes=limit << 20),
            name=name,
        )(pos, left, right)
        return [out[n::chunks] for n in range(chunks)]

    def swap(values):
        out = [values[0]]
        for k in range(1, owners):
            out.append(lax.ppermute(values[k], "ctx", [(i, i ^ k) for i in range(owners)]))
        return out

    chunks = 2 if per_device % 16 == 0 else 1
    (grad_send,) = gate(grad_out, out_gate, False, 1, 56, "gate_grad")
    grad_got = swap(grad_send)
    prod_send = gate(q_branch, k_branch, True, chunks, 12, "gate_prod")
    prod_got = []
    for part in prod_send:
        if prod_got:
            part, prod_got[-1][1] = lax.optimization_barrier((part, prod_got[-1][1]))
        prod_got.append(swap(part))
    unroll = math.gcd(4, per_device)
    conv = pl.pallas_call(
        functools.partial(conv_kernel, owners=owners, unroll=unroll),
        in_specs=[smem] + [vmem] * (1 + owners),
        out_specs=[vmem] * owners,
        out_shape=[piece] * owners,
        scratch_shapes=[pltpu.VMEM((per_device, blocks + 1, 1, LANES), F32)]
        + [pltpu.VMEM((blocks + 1, LANES, LANES), BF16)] * unroll
        + [pltpu.VMEM((2, rows, LANES), BF16)] * (2 * unroll),
        cost_estimate=cost(per_device * rows * length * 4096, 2 * size + groups * length * 2),
        compiler_params=pltpu.CompilerParams(vmem_limit_bytes=16 << 20),
        name="conv",
    )(pos, filters, *grad_got)
    back = swap(conv)
    both = ("ctx", "ch")
    count = lax.axis_size(both)
    each = per_device // chunks
    unroll = math.gcd(8, each)
    old = [conv[0]]
    for n in range(chunks):
        last = n == chunks - 1
        done = jax.ShapeDtypeStruct(((n + 1) * each, blocks // owners, LANES), F32)
        sums = jax.ShapeDtypeStruct((count, 8, LANES) if last else (blocks // owners, LANES), F32)
        old = pl.pallas_call(
            functools.partial(
                lag_kernel, owners=owners, unroll=unroll, scale=scale, first=n * each, last=last
            ),
            in_specs=[smem] + [vmem] * (2 * owners) + ([vmem] * (owners + 1) if n else [anywhere]),
            out_specs=[vmem] * (owners + 1),
            out_shape=[done] * owners + [sums],
            scratch_shapes=[pltpu.VMEM((2, 2 * rows, LANES), BF16)] * unroll
            + [pltpu.VMEM((2, rows, LANES), BF16)] * unroll
            + [
                pltpu.VMEM((unroll, owners, blocks // owners, LANES), F32),
                pltpu.VMEM((blocks // owners, LANES), F32),
            ],
            cost_estimate=cost(each * 2 * rows * length * 2048, 2 * size),
            compiler_params=pltpu.CompilerParams(vmem_limit_bytes=16 << 20),
            name="lags",
        )(pos, *grad_got, *prod_got[n], *old)
    *raw, spread = old
    total = lax.all_to_all(spread, both, 0, 0, tiled=True)
    raw = swap(raw)
    threshold = math.sqrt(WIDTH // GROUP * length)
    grad_q, grad_k, mark = pl.pallas_call(
        ungate_kernel,
        in_specs=[smem] + [anywhere] * (2 + owners),
        out_specs=[anywhere] * 2 + [vmem],
        out_shape=[jax.ShapeDtypeStruct(q_branch.shape, BF16)] * 2
        + [jax.ShapeDtypeStruct((8, LANES), F32)],
        scratch_shapes=[
            pltpu.VMEM((local, groups, GROUP, LANES), BF16),
            pltpu.VMEM((block_len, chans), BF16),
            pltpu.VMEM((block_len, chans), BF16),
            pltpu.VMEM((block_len, chans), BF16),
            pltpu.VMEM((block_len, chans), BF16),
            pltpu.SemaphoreType.DMA((local, owners + 2)),
            pltpu.SemaphoreType.DMA((local, 2)),
        ],
        cost_estimate=cost(2 * block_len * chans, 5 * size),
        compiler_params=pltpu.CompilerParams(vmem_limit_bytes=16 << 20),
        name="ungate",
    )(pos, q_branch, k_branch, *back)
    grad_filters = pl.pallas_call(
        functools.partial(clip_kernel, threshold=threshold),
        in_specs=[smem] + [vmem] * (2 + owners),
        out_specs=vmem,
        out_shape=jax.ShapeDtypeStruct((groups, length // owners), F32),
        scratch_shapes=[pltpu.VMEM((owners, per_device, blocks // owners, LANES), F32)],
        cost_estimate=cost(groups * length, groups * length * 4),
        compiler_params=pltpu.CompilerParams(vmem_limit_bytes=8 << 20),
        name="clip",
    )(pos, total, *raw, mark)
    return (grad_q, grad_k, grad_filters)


def solution(mesh):
    return jax.shard_map(
        on_device,
        mesh=mesh,
        in_specs=(
            P(None, "ctx", "ch"),
            P(None, "ctx", "ch"),
            P(None, "ctx", "ch"),
            P("ch", None),
            P(None, "ctx", "ch"),
        ),
        out_specs=(P(None, "ctx", "ch"), P(None, "ctx", "ch"), P("ch", "ctx")),
        check_vma=False,
    )
```

```python
import functools
import math

import jax
import jax.numpy as jnp
from jax import lax
from jax.experimental import pallas as pl
from jax.experimental.pallas import tpu as pltpu
from jax.sharding import PartitionSpec as P

WIDTH = 8192
GROUP = 16
LANES = 128
NT = (((1,), (1,)), ((), ()))
BF16, F32 = jnp.bfloat16, jnp.float32


def gate_kernel(pos_ref, left_ref, right_ref, *refs, reverse, sizes):
    _, *outs, mark_ref, left, right, out, in_sem, out_sem = refs
    mark_ref[...] = jnp.zeros_like(mark_ref)
    local = left.shape[0] // LANES
    per_device = sum(sizes)
    copies = []
    for i in range(local):
        here = pl.ds(i * LANES, LANES)
        copies.append(
            (
                pltpu.make_async_copy(left_ref.at[0, here], left.at[here], in_sem.at[i, 0]),
                pltpu.make_async_copy(right_ref.at[0, here], right.at[here], in_sem.at[i, 1]),
            )
        )
    for pair in copies:
        for copy in pair:
            copy.start()
    sends = []
    for i in range(local):
        for copy in copies[i]:
            copy.wait()
        rows = slice(i * LANES, (i + 1) * LANES)
        value = (left[rows].astype(F32) * right[rows].astype(F32)).astype(BF16)
        if reverse:
            row_id = lax.broadcasted_iota(jnp.int32, (LANES, LANES), 0)
            col_id = lax.broadcasted_iota(jnp.int32, (LANES, LANES), 1)
            flip = (row_id + col_id == LANES - 1).astype(BF16)
            value = jnp.dot(flip, value, preferred_element_type=F32).astype(BF16)
        value = value.T
        out[i % 2, i // 2] = value.reshape(out.shape[2:])
        for n, target in enumerate(outs):
            k, chunk = divmod(n, len(sizes))
            first = jnp.bitwise_xor(pos_ref[0], k) * per_device + sum(sizes[:chunk])
            send = pltpu.make_async_copy(
                out.at[i % 2, i // 2, pl.ds(first, sizes[chunk])],
                target.at[:, i % 2, i // 2],
                out_sem.at[i, n],
            )
            send.start()
            sends.append(send)
    for send in sends:
        send.wait()


def ungate_kernel(pos_ref, q_ref, k_ref, *refs):
    *grads, gq_ref, gk_ref, mark_ref, grad, q_in, k_in, gq, gk, in_sem, out_sem = refs
    local = q_in.shape[0] // LANES
    per_device = grads[0].shape[0]
    owners = len(grads)
    mark_ref[...] = jnp.zeros_like(mark_ref)
    copies, sends = [], []
    for i in range(local):
        here = pl.ds(i * LANES, LANES)
        row = [
            pltpu.make_async_copy(q_ref.at[0, here], q_in.at[here], in_sem.at[i, owners]),
            pltpu.make_async_copy(k_ref.at[0, here], k_in.at[here], in_sem.at[i, owners + 1]),
        ]
        for k, source in enumerate(grads):
            first = jnp.bitwise_xor(pos_ref[0], k) * per_device
            row.append(
                pltpu.make_async_copy(
                    source.at[:, i % 2, i // 2], grad.at[i, pl.ds(first, per_device)], in_sem.at[i, k]
                )
            )
        copies.append(row)
    for row in copies:
        for copy in row:
            copy.start()
    for i in range(local):
        for copy in copies[i]:
            copy.wait()
        here = pl.ds(i * LANES, LANES)
        rows = slice(i * LANES, (i + 1) * LANES)
        value = grad[i].reshape(q_in.shape[1], LANES).T.astype(F32)
        gq[rows] = (value * k_in[rows].astype(F32)).astype(BF16)
        gk[rows] = (value * q_in[rows].astype(F32)).astype(BF16)
        for n, (source, target) in enumerate(((gq, gq_ref), (gk, gk_ref))):
            send = pltpu.make_async_copy(source.at[here], target.at[0, here], out_sem.at[i, n])
            send.start()
            sends.append(send)
    for send in sends:
        send.wait()


def clip_kernel(pos_ref, total_ref, *refs, threshold):
    *parts, _, out_ref, stage = refs
    per_device, each = stage.shape[1:3]
    for k, part in enumerate(parts):
        stage[jnp.bitwise_xor(pos_ref[0], k)] = part[...]
    total = jnp.sum(total_ref[...], axis=(0, 1, 2), keepdims=True)[0]
    factor = jnp.minimum(1.0, threshold / jnp.sqrt(total + 1e-06))
    for owner in range(stage.shape[0]):
        for n in range(each):
            rows = slice(owner * per_device, (owner + 1) * per_device)
            out_ref[rows, n * LANES : (n + 1) * LANES] = stage[owner, :, n] * factor


def spread_rows(pos_ref, sources, f, target):
    for k, source in enumerate(sources):
        count = source.shape[2] * GROUP
        at = pl.multiple_of(jnp.bitwise_xor(pos_ref[0], k) * count, count)
        for half in range(2):
            target[half, pl.ds(at, count)] = source[f, half].reshape(count, LANES)


def reverse_taps(owner, filt_ref, taps):
    per_device, blocks = taps.shape[0], taps.shape[1] - 1
    groups = filt_ref.shape[0]
    picks = max(per_device, 8)
    row_id = lax.broadcasted_iota(jnp.int32, (picks, groups), 0)
    col_id = lax.broadcasted_iota(jnp.int32, (picks, groups), 1)
    pick = (col_id == row_id + owner * per_device).astype(BF16)
    width = min((blocks + 1) * LANES, filt_ref.shape[1])
    mine = jnp.dot(pick, filt_ref[:, :width], preferred_element_type=F32).astype(BF16)
    empty = jnp.zeros((picks, LANES), BF16)
    mine = jnp.concatenate([empty, mine, empty], axis=1)
    row_id = lax.broadcasted_iota(jnp.int32, (2 * LANES, LANES), 0)
    col_id = lax.broadcasted_iota(jnp.int32, (2 * LANES, LANES), 1)
    flip = (row_id + col_id == LANES).astype(BF16)
    for block in range(blocks + 1):
        near = mine[:, block * LANES : (block + 2) * LANES]
        back = jnp.dot(near, flip, preferred_element_type=F32)
        for f in range(per_device):
            taps[f, block] = back[f : f + 1]


def build_blocks(taps, f, toep):
    row_id = lax.broadcasted_iota(jnp.int32, (LANES, LANES), 0)
    col_id = lax.broadcasted_iota(jnp.int32, (LANES, LANES), 1)
    upper = col_id >= row_id
    before = None
    for block in range(taps.shape[1]):
        tap = jnp.broadcast_to(taps[f, block], (LANES, LANES))
        rolled = pltpu.roll(tap, 0, 1, stride=1, stride_axis=0)
        if block:
            toep[block] = jnp.where(upper, before, rolled).astype(BF16)
        before = rolled


def weights(toep, pair):
    at = 2 * pair + 1
    top = jnp.concatenate([toep[at], toep[at - 1]], axis=1)
    low = jnp.concatenate([toep[at + 1], toep[at]], axis=1)
    return jnp.concatenate([top, low], axis=0)


def blocks_kernel(pos_ref, filt_ref, *refs):
    _, *toeps, taps = refs
    unroll = len(toeps)
    reverse_taps(pos_ref[0], filt_ref, taps)

    def some(i, carry):
        for u in range(unroll):
            toep = toeps[u].at[i]
            toep[0] = jnp.zeros((LANES, LANES), BF16)
            build_blocks(taps, i * unroll + u, toep)
        return carry

    lax.fori_loop(0, toeps[0].shape[0], some, 0)


def conv_kernel(pos_ref, *refs, owners, unroll):
    toeps, refs = refs[:unroll], refs[unroll:]
    ins, outs, refs = refs[:owners], refs[owners : 2 * owners], refs[2 * owners :]
    pads, accs = refs[:unroll], refs[unroll:]
    per_device, blocks = ins[0].shape[0], toeps[0].shape[1] - 1
    rows = pads[0].shape[1]

    def one(toep, pad, out):
        acc = jnp.zeros((rows, 2 * LANES), F32)
        for pair in range(blocks // 2):
            start = pair * GROUP
            left = jnp.concatenate([pad[0, start:], pad[1, start:]], axis=1)
            part = jnp.dot(left, weights(toep, pair), preferred_element_type=F32)
            if start:
                part = jnp.concatenate([part, jnp.zeros((start, 2 * LANES), F32)], axis=0)
            acc = acc + part
        for half in range(2):
            out[half] = acc[:, half * LANES : (half + 1) * LANES].astype(BF16)

    def some(i, carry):
        for u in range(unroll):
            spread_rows(pos_ref, ins, i * unroll + u, pads[u])
        for u in range(unroll):
            one(toeps[u].at[i], pads[u], accs[u])
        for u in range(unroll):
            for k, target in enumerate(outs):
                count = target.shape[2] * GROUP
                at = pl.multiple_of(jnp.bitwise_xor(pos_ref[0], k) * count, count)
                for half in range(2):
                    value = accs[u][half, pl.ds(at, count)]
                    target[i * unroll + u, half] = value.reshape(target.shape[2:])
        return carry

    lax.fori_loop(0, per_device // unroll, some, 0)


def lag_sums(pad, flipped, rows, blocks):
    row_id = lax.broadcasted_iota(jnp.int32, (LANES, LANES), 0)
    col_id = lax.broadcasted_iota(jnp.int32, (LANES, LANES), 1)
    wraps = col_id <= row_id
    prod = jnp.concatenate([flipped[half, :rows].T for half in range(2)], axis=1)
    after = jnp.zeros((LANES, LANES), F32)
    sums = {}
    for pair in reversed(range(blocks // 2)):
        start = pair * GROUP
        here, later = slice(start, start + rows), slice(start + GROUP, start + GROUP + rows)
        even = jnp.concatenate([pad[0, here], pad[1, here]], axis=0)
        odd = jnp.concatenate([pad[1, here], pad[0, later]], axis=0)
        both = jnp.dot(prod, jnp.concatenate([even, odd], axis=1), preferred_element_type=F32)
        for half in (1, 0):
            rolled = pltpu.roll(
                both[:, half * LANES : (half + 1) * LANES], 1, 1, stride=1, stride_axis=0
            )
            part = jnp.where(wraps, rolled, after)
            sums[2 * pair + half] = jnp.sum(part, axis=0, keepdims=True)
            after = rolled
    return sums


def lag_kernel(pos_ref, *refs, owners, unroll, scale, first, last):
    grads, prods, refs = refs[:owners], refs[owners : 2 * owners], refs[2 * owners :]
    olds, refs = (refs[: owners + 1], refs[owners + 1 :]) if first else ([], refs[1:])
    raws, sum_ref, refs = refs[:owners], refs[owners], refs[owners + 1 :]
    pads, flips, lags_v, sq_v = refs[:unroll], refs[unroll : 2 * unroll], refs[-2], refs[-1]
    per_owner = raws[0].shape[1]
    blocks = owners * per_owner
    rows = flips[0].shape[1]
    for pad in pads:
        pad[:, rows:] = jnp.zeros((2, rows, LANES), BF16)
    sq_v[...] = olds[-1][...] if olds else jnp.zeros_like(sq_v)

    def one(slot, pad, flipped):
        sums = lag_sums(pad, flipped, rows, blocks)
        for owner in range(owners):
            lags = jnp.concatenate(
                [sums[owner * per_owner + n] for n in range(per_owner)], axis=0
            ) * scale
            lags_v[slot, owner] = lags
            sq_v[...] += lags * lags

    def some(i, carry):
        for u in range(unroll):
            spread_rows(pos_ref, grads, first + i * unroll + u, pads[u])
            spread_rows(pos_ref, prods, i * unroll + u, flips[u])
        for u in range(unroll):
            one(u, pads[u], flips[u])
        for u in range(unroll):
            for k, target in enumerate(raws):
                target[first + i * unroll + u] = lags_v[u, jnp.bitwise_xor(pos_ref[0], k)]
        return carry

    lax.fori_loop(0, prods[0].shape[0] // unroll, some, 0)
    if not last:
        sum_ref[...] = sq_v[...]
        return
    squares = jnp.sum(sq_v[...], axis=0, keepdims=True)
    sum_ref[...] = jnp.zeros_like(sum_ref)
    sum_ref[:, :1] = jnp.broadcast_to(squares[None], (sum_ref.shape[0], 1, LANES))


def cost(flops, moved):
    return pl.CostEstimate(flops=int(flops), bytes_accessed=int(moved), transcendentals=0)


def on_device(q_branch, k_branch, out_gate, filters, grad_out):
    seqs, block_len, chans = q_branch.shape
    owners = lax.axis_size("ctx")
    groups = chans // GROUP
    per_device = groups // owners
    local = block_len // LANES
    length = owners * block_len
    blocks = length // LANES
    rows = length * GROUP // (2 * LANES)
    scale = 4.0 / math.sqrt(seqs * GROUP)
    size = block_len * chans * 2
    anywhere = pl.BlockSpec(memory_space=pl.ANY)
    vmem = pl.BlockSpec(memory_space=pltpu.VMEM)
    smem = pl.BlockSpec(memory_space=pltpu.SMEM)
    tail = (2, local // 2, GROUP, LANES)
    whole = (owners, per_device) + tail
    pos = lax.axis_index("ctx").astype(jnp.int32).reshape(1)
    piece = jax.ShapeDtypeStruct((per_device,) + tail, BF16)
    lag_piece = jax.ShapeDtypeStruct((per_device, blocks // owners, LANES), F32)

    def gate(left, right, after, reverse, sizes, limit, name):
        parts = [jax.ShapeDtypeStruct((n,) + tail, BF16) for n in sizes]
        out = pl.pallas_call(
            functools.partial(gate_kernel, reverse=reverse, sizes=sizes),
            in_specs=[smem] + [anywhere] * 2 + [vmem],
            out_specs=[anywhere] * (owners * len(sizes)) + [vmem],
            out_shape=parts * owners + [jax.ShapeDtypeStruct((8, LANES), F32)],
            scratch_shapes=[
                pltpu.VMEM((block_len, chans), BF16),
                pltpu.VMEM((block_len, chans), BF16),
                pltpu.VMEM((2, local // 2, groups, GROUP, LANES), BF16),
                pltpu.SemaphoreType.DMA((local, 2)),
                pltpu.SemaphoreType.DMA((local, owners * len(sizes))),
            ],
            cost_estimate=cost(block_len * chans, 3 * size),
            compiler_params=pltpu.CompilerParams(vmem_limit_bytes=limit << 20),
            name=name,
        )(pos, left, right, after)
        return [out[n : -1 : len(sizes)] for n in range(len(sizes))], out[-1]

    def swap(values):
        out = [values[0]]
        for k in range(1, owners):
            out.append(lax.ppermute(values[k], "ctx", [(i, i ^ k) for i in range(owners)]))
        return out

    sizes = (8, 4, 4) if per_device == 16 else (per_device,)
    mark = jnp.zeros((8, LANES), F32)
    (grad_send,), mark = gate(grad_out, out_gate, mark, False, (per_device,), 56, "gate_grad")
    grad_got = swap(grad_send)
    prod_send, mark = gate(q_branch, k_branch, mark, True, sizes, 12, "gate_prod")
    prod_got = []
    for part in prod_send:
        if prod_got:
            part, prod_got[-1][1] = lax.optimization_barrier((part, prod_got[-1][1]))
        prod_got.append(swap(part))
    unroll = math.gcd(4, per_device)
    toeps = pl.pallas_call(
        blocks_kernel,
        in_specs=[smem, vmem, vmem],
        out_specs=[vmem] * unroll,
        out_shape=[
            jax.ShapeDtypeStruct((per_device // unroll, blocks + 1, LANES, LANES), BF16)
        ] * unroll,
        scratch_shapes=[pltpu.VMEM((per_device, blocks + 1, 1, LANES), F32)],
        cost_estimate=cost(1, 1),
        compiler_params=pltpu.CompilerParams(vmem_limit_bytes=16 << 20),
        name="blocks",
    )(pos, filters, mark)
    conv = pl.pallas_call(
        functools.partial(conv_kernel, owners=owners, unroll=unroll),
        in_specs=[smem] + [vmem] * (unroll + owners),
        out_specs=[vmem] * owners,
        out_shape=[piece] * owners,
        scratch_shapes=[pltpu.VMEM((2, rows, LANES), BF16)] * (2 * unroll),
        cost_estimate=cost(per_device * rows * length * 4096, 2 * size + groups * length * 2),
        compiler_params=pltpu.CompilerParams(vmem_limit_bytes=16 << 20),
        name="conv",
    )(pos, *toeps, *grad_got)
    back = swap(conv)
    both = ("ctx", "ch")
    count = lax.axis_size(both)
    old = [conv[0]]
    for n, each in enumerate(sizes):
        last = n == len(sizes) - 1
        unroll = math.gcd(8, each)
        sums = jax.ShapeDtypeStruct((count, 8, LANES) if last else (blocks // owners, LANES), F32)
        old = pl.pallas_call(
            functools.partial(
                lag_kernel, owners=owners, unroll=unroll, scale=scale, first=sum(sizes[:n]), last=last
            ),
            in_specs=[smem] + [vmem] * (2 * owners) + ([vmem] * (owners + 1) if n else [anywhere]),
            out_specs=[vmem] * (owners + 1),
            out_shape=[lag_piece] * owners + [sums],
            input_output_aliases={2 * owners + 1 + k: k for k in range(owners)} if n else {},
            scratch_shapes=[pltpu.VMEM((2, 2 * rows, LANES), BF16)] * unroll
            + [pltpu.VMEM((2, rows, LANES), BF16)] * unroll
            + [
                pltpu.VMEM((unroll, owners, blocks // owners, LANES), F32),
                pltpu.VMEM((blocks // owners, LANES), F32),
            ],
            cost_estimate=cost(each * 2 * rows * length * 2048, 2 * size),
            compiler_params=pltpu.CompilerParams(vmem_limit_bytes=16 << 20),
            name="lags",
        )(pos, *grad_got, *prod_got[n], *old)
    *raw, spread = old
    total = lax.all_to_all(spread, both, 0, 0, tiled=True)
    raw = swap(raw)
    threshold = math.sqrt(WIDTH // GROUP * length)
    grad_q, grad_k, mark = pl.pallas_call(
        ungate_kernel,
        in_specs=[smem] + [anywhere] * (2 + owners),
        out_specs=[anywhere] * 2 + [vmem],
        out_shape=[jax.ShapeDtypeStruct(q_branch.shape, BF16)] * 2
        + [jax.ShapeDtypeStruct((8, LANES), F32)],
        scratch_shapes=[
            pltpu.VMEM((local, groups, GROUP, LANES), BF16),
            pltpu.VMEM((block_len, chans), BF16),
            pltpu.VMEM((block_len, chans), BF16),
            pltpu.VMEM((block_len, chans), BF16),
            pltpu.VMEM((block_len, chans), BF16),
            pltpu.SemaphoreType.DMA((local, owners + 2)),
            pltpu.SemaphoreType.DMA((local, 2)),
        ],
        cost_estimate=cost(2 * block_len * chans, 5 * size),
        compiler_params=pltpu.CompilerParams(vmem_limit_bytes=16 << 20),
        name="ungate",
    )(pos, q_branch, k_branch, *back)
    grad_filters = pl.pallas_call(
        functools.partial(clip_kernel, threshold=threshold),
        in_specs=[smem] + [vmem] * (2 + owners),
        out_specs=vmem,
        out_shape=jax.ShapeDtypeStruct((groups, length // owners), F32),
        scratch_shapes=[pltpu.VMEM((owners, per_device, blocks // owners, LANES), F32)],
        cost_estimate=cost(groups * length, groups * length * 4),
        compiler_params=pltpu.CompilerParams(vmem_limit_bytes=8 << 20),
        name="clip",
    )(pos, total, *raw, mark)
    return (grad_q, grad_k, grad_filters)


def solution(mesh):
    return jax.shard_map(
        on_device,
        mesh=mesh,
        in_specs=(
            P(None, "ctx", "ch"),
            P(None, "ctx", "ch"),
            P(None, "ctx", "ch"),
            P("ch", None),
            P(None, "ctx", "ch"),
        ),
        out_specs=(P(None, "ctx", "ch"), P(None, "ctx", "ch"), P("ch", "ctx")),
        check_vma=False,
    )
```

```python
import functools
import math

import jax
import jax.numpy as jnp
from jax import lax
from jax.experimental import pallas as pl
from jax.experimental.pallas import tpu as pltpu
from jax.sharding import PartitionSpec as P

WIDTH = 8192
GROUP = 16
LANES = 128
NT = (((1,), (1,)), ((), ()))
BF16, F32 = jnp.bfloat16, jnp.float32


def gate_kernel(pos_ref, left_ref, right_ref, *refs, reverse, sizes, ordered):
    *outs, left, right, out, in_sem, out_sem = refs[ordered:]
    local = left.shape[0] // LANES
    per_device = sum(sizes)
    copies = []
    for i in range(local):
        here = pl.ds(i * LANES, LANES)
        copies.append(
            (
                pltpu.make_async_copy(left_ref.at[0, here], left.at[here], in_sem.at[i, 0]),
                pltpu.make_async_copy(right_ref.at[0, here], right.at[here], in_sem.at[i, 1]),
            )
        )
    for pair in copies:
        for copy in pair:
            copy.start()
    sends = []
    for i in range(local):
        for copy in copies[i]:
            copy.wait()
        rows = slice(i * LANES, (i + 1) * LANES)
        value = (left[rows].astype(F32) * right[rows].astype(F32)).astype(BF16)
        if reverse:
            row_id = lax.broadcasted_iota(jnp.int32, (LANES, LANES), 0)
            col_id = lax.broadcasted_iota(jnp.int32, (LANES, LANES), 1)
            flip = (row_id + col_id == LANES - 1).astype(BF16)
            value = jnp.dot(flip, value, preferred_element_type=F32).astype(BF16)
        value = value.T
        out[i % 2, i // 2] = value.reshape(out.shape[2:])
        for n, target in enumerate(outs):
            k, chunk = divmod(n, len(sizes))
            first = jnp.bitwise_xor(pos_ref[0], k) * per_device + sum(sizes[:chunk])
            send = pltpu.make_async_copy(
                out.at[i % 2, i // 2, pl.ds(first, sizes[chunk])],
                target.at[:, i % 2, i // 2],
                out_sem.at[i, n],
            )
            send.start()
            sends.append(send)
    for send in sends:
        send.wait()


def ungate_kernel(pos_ref, q_ref, k_ref, *refs):
    *grads, gq_ref, gk_ref, mark_ref, grad, q_in, k_in, gq, gk, in_sem, out_sem = refs
    local = q_in.shape[0] // LANES
    per_device = grads[0].shape[0]
    owners = len(grads)
    mark_ref[...] = jnp.zeros_like(mark_ref)
    copies, sends = [], []
    for i in range(local):
        here = pl.ds(i * LANES, LANES)
        row = [
            pltpu.make_async_copy(q_ref.at[0, here], q_in.at[here], in_sem.at[i, owners]),
            pltpu.make_async_copy(k_ref.at[0, here], k_in.at[here], in_sem.at[i, owners + 1]),
        ]
        for k, source in enumerate(grads):
            first = jnp.bitwise_xor(pos_ref[0], k) * per_device
            row.append(
                pltpu.make_async_copy(
                    source.at[:, i % 2, i // 2], grad.at[i, pl.ds(first, per_device)], in_sem.at[i, k]
                )
            )
        copies.append(row)
    for row in copies:
        for copy in row:
            copy.start()
    for i in range(local):
        for copy in copies[i]:
            copy.wait()
        here = pl.ds(i * LANES, LANES)
        rows = slice(i * LANES, (i + 1) * LANES)
        value = grad[i].reshape(q_in.shape[1], LANES).T.astype(F32)
        gq[rows] = (value * k_in[rows].astype(F32)).astype(BF16)
        gk[rows] = (value * q_in[rows].astype(F32)).astype(BF16)
        for n, (source, target) in enumerate(((gq, gq_ref), (gk, gk_ref))):
            send = pltpu.make_async_copy(source.at[here], target.at[0, here], out_sem.at[i, n])
            send.start()
            sends.append(send)
    for send in sends:
        send.wait()


def clip_kernel(pos_ref, total_ref, *refs, threshold):
    *parts, _, out_ref, stage = refs
    per_device, each = stage.shape[1:3]
    for k, part in enumerate(parts):
        stage[jnp.bitwise_xor(pos_ref[0], k)] = part[...]
    total = jnp.sum(total_ref[...], axis=(0, 1, 2), keepdims=True)[0]
    factor = jnp.minimum(1.0, threshold / jnp.sqrt(total + 1e-06))
    for owner in range(stage.shape[0]):
        for n in range(each):
            rows = slice(owner * per_device, (owner + 1) * per_device)
            out_ref[rows, n * LANES : (n + 1) * LANES] = stage[owner, :, n] * factor


def spread_rows(pos_ref, sources, f, target):
    for k, source in enumerate(sources):
        count = source.shape[2] * GROUP
        at = pl.multiple_of(jnp.bitwise_xor(pos_ref[0], k) * count, count)
        for half in range(2):
            target[half, pl.ds(at, count)] = source[f, half].reshape(count, LANES)


def reverse_taps(owner, filt_ref, taps):
    per_device, blocks = taps.shape[0], taps.shape[1] - 1
    groups = filt_ref.shape[0]
    picks = max(per_device, 8)
    row_id = lax.broadcasted_iota(jnp.int32, (picks, groups), 0)
    col_id = lax.broadcasted_iota(jnp.int32, (picks, groups), 1)
    pick = (col_id == row_id + owner * per_device).astype(BF16)
    width = min((blocks + 1) * LANES, filt_ref.shape[1])
    mine = jnp.dot(pick, filt_ref[:, :width], preferred_element_type=F32).astype(BF16)
    empty = jnp.zeros((picks, LANES), BF16)
    mine = jnp.concatenate([empty, mine, empty], axis=1)
    row_id = lax.broadcasted_iota(jnp.int32, (2 * LANES, LANES), 0)
    col_id = lax.broadcasted_iota(jnp.int32, (2 * LANES, LANES), 1)
    flip = (row_id + col_id == LANES).astype(BF16)
    for block in range(blocks + 1):
        near = mine[:, block * LANES : (block + 2) * LANES]
        back = jnp.dot(near, flip, preferred_element_type=F32)
        for f in range(per_device):
            taps[f, block] = back[f : f + 1]


def build_blocks(taps, f, toep):
    row_id = lax.broadcasted_iota(jnp.int32, (LANES, LANES), 0)
    col_id = lax.broadcasted_iota(jnp.int32, (LANES, LANES), 1)
    upper = col_id >= row_id
    before = None
    for block in range(taps.shape[1]):
        tap = jnp.broadcast_to(taps[f, block], (LANES, LANES))
        rolled = pltpu.roll(tap, 0, 1, stride=1, stride_axis=0)
        if block:
            toep[block] = jnp.where(upper, before, rolled).astype(BF16)
        before = rolled


def weights(toep, pair):
    at = 2 * pair + 1
    top = jnp.concatenate([toep[at], toep[at - 1]], axis=1)
    low = jnp.concatenate([toep[at + 1], toep[at]], axis=1)
    return jnp.concatenate([top, low], axis=0)


def blocks_kernel(pos_ref, filt_ref, *refs):
    *toeps, taps = refs
    unroll = len(toeps)
    reverse_taps(pos_ref[0], filt_ref, taps)

    def some(i, carry):
        for u in range(unroll):
            toep = toeps[u].at[i]
            toep[0] = jnp.zeros((LANES, LANES), BF16)
            build_blocks(taps, i * unroll + u, toep)
        return carry

    lax.fori_loop(0, toeps[0].shape[0], some, 0)


def conv_kernel(pos_ref, *refs, owners, unroll):
    toeps, refs = refs[:unroll], refs[unroll:]
    ins, outs, refs = refs[:owners], refs[owners : 2 * owners], refs[2 * owners :]
    pads, accs = refs[:unroll], refs[unroll:]
    per_device, blocks = ins[0].shape[0], toeps[0].shape[1] - 1
    rows = pads[0].shape[1]

    def one(toep, pad, out):
        acc = jnp.zeros((rows, 2 * LANES), F32)
        for pair in range(blocks // 2):
            start = pair * GROUP
            left = jnp.concatenate([pad[0, start:], pad[1, start:]], axis=1)
            part = jnp.dot(left, weights(toep, pair), preferred_element_type=F32)
            if start:
                part = jnp.concatenate([part, jnp.zeros((start, 2 * LANES), F32)], axis=0)
            acc = acc + part
        for half in range(2):
            out[half] = acc[:, half * LANES : (half + 1) * LANES].astype(BF16)

    def some(i, carry):
        for u in range(unroll):
            spread_rows(pos_ref, ins, i * unroll + u, pads[u])
        for u in range(unroll):
            one(toeps[u].at[i], pads[u], accs[u])
        for u in range(unroll):
            for k, target in enumerate(outs):
                count = target.shape[2] * GROUP
                at = pl.multiple_of(jnp.bitwise_xor(pos_ref[0], k) * count, count)
                for half in range(2):
                    value = accs[u][half, pl.ds(at, count)]
                    target[i * unroll + u, half] = value.reshape(target.shape[2:])
        return carry

    lax.fori_loop(0, per_device // unroll, some, 0)


def lag_sums(pad, flipped, rows, blocks):
    row_id = lax.broadcasted_iota(jnp.int32, (LANES, LANES), 0)
    col_id = lax.broadcasted_iota(jnp.int32, (LANES, LANES), 1)
    wraps = col_id <= row_id
    prod = jnp.concatenate([flipped[half, :rows].T for half in range(2)], axis=1)
    after = jnp.zeros((LANES, LANES), F32)
    sums = {}
    for pair in reversed(range(blocks // 2)):
        start = pair * GROUP
        here, later = slice(start, start + rows), slice(start + GROUP, start + GROUP + rows)
        even = jnp.concatenate([pad[0, here], pad[1, here]], axis=0)
        odd = jnp.concatenate([pad[1, here], pad[0, later]], axis=0)
        both = jnp.dot(prod, jnp.concatenate([even, odd], axis=1), preferred_element_type=F32)
        for half in (1, 0):
            rolled = pltpu.roll(
                both[:, half * LANES : (half + 1) * LANES], 1, 1, stride=1, stride_axis=0
            )
            part = jnp.where(wraps, rolled, after)
            sums[2 * pair + half] = jnp.sum(part, axis=0, keepdims=True)
            after = rolled
    return sums


def lag_kernel(pos_ref, *refs, owners, unroll, scale, first, last):
    grads, prods, refs = refs[:owners], refs[owners : 2 * owners], refs[2 * owners :]
    olds, refs = (refs[: owners + 1], refs[owners + 1 :]) if first else ([], refs[1:])
    raws, sum_ref, refs = refs[:owners], refs[owners], refs[owners + 1 :]
    pads, flips, lags_v, sq_v = refs[:unroll], refs[unroll : 2 * unroll], refs[-2], refs[-1]
    per_owner = raws[0].shape[1]
    blocks = owners * per_owner
    rows = flips[0].shape[1]
    for pad in pads:
        pad[:, rows:] = jnp.zeros((2, rows, LANES), BF16)
    sq_v[...] = olds[-1][...] if olds else jnp.zeros_like(sq_v)

    def one(slot, pad, flipped):
        sums = lag_sums(pad, flipped, rows, blocks)
        for owner in range(owners):
            lags = jnp.concatenate(
                [sums[owner * per_owner + n] for n in range(per_owner)], axis=0
            ) * scale
            lags_v[slot, owner] = lags
            sq_v[...] += lags * lags

    def some(i, carry):
        for u in range(unroll):
            spread_rows(pos_ref, grads, first + i * unroll + u, pads[u])
            spread_rows(pos_ref, prods, i * unroll + u, flips[u])
        for u in range(unroll):
            one(u, pads[u], flips[u])
        for u in range(unroll):
            for k, target in enumerate(raws):
                target[first + i * unroll + u] = lags_v[u, jnp.bitwise_xor(pos_ref[0], k)]
        return carry

    lax.fori_loop(0, prods[0].shape[0] // unroll, some, 0)
    if not last:
        sum_ref[...] = sq_v[...]
        return
    squares = jnp.sum(sq_v[...], axis=0, keepdims=True)
    sum_ref[...] = jnp.zeros_like(sum_ref)
    sum_ref[:, :1] = jnp.broadcast_to(squares[None], (sum_ref.shape[0], 1, LANES))


def cost(flops, moved):
    return pl.CostEstimate(flops=int(flops), bytes_accessed=int(moved), transcendentals=0)


def on_device(q_branch, k_branch, out_gate, filters, grad_out):
    seqs, block_len, chans = q_branch.shape
    owners = lax.axis_size("ctx")
    groups = chans // GROUP
    per_device = groups // owners
    local = block_len // LANES
    length = owners * block_len
    blocks = length // LANES
    rows = length * GROUP // (2 * LANES)
    scale = 4.0 / math.sqrt(seqs * GROUP)
    size = block_len * chans * 2
    anywhere = pl.BlockSpec(memory_space=pl.ANY)
    vmem = pl.BlockSpec(memory_space=pltpu.VMEM)
    smem = pl.BlockSpec(memory_space=pltpu.SMEM)
    tail = (2, local // 2, GROUP, LANES)
    whole = (owners, per_device) + tail
    pos = lax.axis_index("ctx").astype(jnp.int32).reshape(1)
    piece = jax.ShapeDtypeStruct((per_device,) + tail, BF16)
    lag_piece = jax.ShapeDtypeStruct((per_device, blocks // owners, LANES), F32)

    def gate(left, right, after, reverse, sizes, limit, name):
        parts = [jax.ShapeDtypeStruct((n,) + tail, BF16) for n in sizes]
        out = pl.pallas_call(
            functools.partial(gate_kernel, reverse=reverse, sizes=sizes, ordered=len(after)),
            in_specs=[smem] + [pl.BlockSpec(memory_space=pltpu.HBM)] * 2 + [vmem] * len(after),
            out_specs=[anywhere] * (owners * len(sizes)),
            out_shape=parts * owners,
            scratch_shapes=[
                pltpu.VMEM((block_len, chans), BF16),
                pltpu.VMEM((block_len, chans), BF16),
                pltpu.VMEM((2, local // 2, groups, GROUP, LANES), BF16),
                pltpu.SemaphoreType.DMA((local, 2)),
                pltpu.SemaphoreType.DMA((local, owners * len(sizes))),
            ],
            cost_estimate=cost(block_len * chans, 3 * size),
            compiler_params=pltpu.CompilerParams(vmem_limit_bytes=limit << 20),
            name=name,
        )(pos, left, right, *after)
        return [out[n :: len(sizes)] for n in range(len(sizes))]

    def swap(values):
        out = [values[0]]
        for k in range(1, owners):
            out.append(lax.ppermute(values[k], "ctx", [(i, i ^ k) for i in range(owners)]))
        return out

    sizes = (8, 8) if per_device == 16 else (per_device,)
    (grad_send,) = gate(grad_out, out_gate, (), False, (per_device,), 56, "gate_grad")
    grad_got = swap(grad_send)
    prod_send = gate(q_branch, k_branch, grad_send[:1], True, sizes, 12, "gate_prod")
    prod_got = []
    for part in prod_send:
        if prod_got:
            part, prod_got[-1][1] = lax.optimization_barrier((part, prod_got[-1][1]))
        prod_got.append(swap(part))
    unroll = math.gcd(4, per_device)
    toeps = pl.pallas_call(
        blocks_kernel,
        in_specs=[smem, vmem],
        out_specs=[vmem] * unroll,
        out_shape=[
            jax.ShapeDtypeStruct((per_device // unroll, blocks + 1, LANES, LANES), BF16)
        ] * unroll,
        scratch_shapes=[pltpu.VMEM((per_device, blocks + 1, 1, LANES), F32)],
        cost_estimate=cost(1, 1),
        compiler_params=pltpu.CompilerParams(vmem_limit_bytes=16 << 20),
        name="blocks",
    )(pos, filters)
    conv = pl.pallas_call(
        functools.partial(conv_kernel, owners=owners, unroll=unroll),
        in_specs=[smem] + [vmem] * (unroll + owners),
        out_specs=[vmem] * owners,
        out_shape=[piece] * owners,
        scratch_shapes=[pltpu.VMEM((2, rows, LANES), BF16)] * (2 * unroll),
        cost_estimate=cost(per_device * rows * length * 4096, 2 * size + groups * length * 2),
        compiler_params=pltpu.CompilerParams(vmem_limit_bytes=16 << 20),
        name="conv",
    )(pos, *toeps, *grad_got)
    back = swap(conv)
    both = ("ctx", "ch")
    count = lax.axis_size(both)
    old = [conv[0]]
    for n, each in enumerate(sizes):
        last = n == len(sizes) - 1
        unroll = math.gcd(8, each)
        sums = jax.ShapeDtypeStruct((count, 8, LANES) if last else (blocks // owners, LANES), F32)
        old = pl.pallas_call(
            functools.partial(
                lag_kernel, owners=owners, unroll=unroll, scale=scale, first=sum(sizes[:n]), last=last
            ),
            in_specs=[smem] + [vmem] * (2 * owners) + ([vmem] * (owners + 1) if n else [anywhere]),
            out_specs=[vmem] * (owners + 1),
            out_shape=[lag_piece] * owners + [sums],
            input_output_aliases={2 * owners + 1 + k: k for k in range(owners)} if n else {},
            scratch_shapes=[pltpu.VMEM((2, 2 * rows, LANES), BF16)] * unroll
            + [pltpu.VMEM((2, rows, LANES), BF16)] * unroll
            + [
                pltpu.VMEM((unroll, owners, blocks // owners, LANES), F32),
                pltpu.VMEM((blocks // owners, LANES), F32),
            ],
            cost_estimate=cost(each * 2 * rows * length * 2048, 2 * size),
            compiler_params=pltpu.CompilerParams(vmem_limit_bytes=16 << 20),
            name="lags",
        )(pos, *grad_got, *prod_got[n], *old)
    *raw, spread = old
    total = lax.all_to_all(spread, both, 0, 0, tiled=True)
    raw = swap(raw)
    threshold = math.sqrt(WIDTH // GROUP * length)
    grad_q, grad_k, mark = pl.pallas_call(
        ungate_kernel,
        in_specs=[smem] + [anywhere] * (2 + owners),
        out_specs=[anywhere] * 2 + [vmem],
        out_shape=[jax.ShapeDtypeStruct(q_branch.shape, BF16)] * 2
        + [jax.ShapeDtypeStruct((8, LANES), F32)],
        scratch_shapes=[
            pltpu.VMEM((local, groups, GROUP, LANES), BF16),
            pltpu.VMEM((block_len, chans), BF16),
            pltpu.VMEM((block_len, chans), BF16),
            pltpu.VMEM((block_len, chans), BF16),
            pltpu.VMEM((block_len, chans), BF16),
            pltpu.SemaphoreType.DMA((local, owners + 2)),
            pltpu.SemaphoreType.DMA((local, 2)),
        ],
        cost_estimate=cost(2 * block_len * chans, 5 * size),
        compiler_params=pltpu.CompilerParams(vmem_limit_bytes=16 << 20),
        name="ungate",
    )(pos, q_branch, k_branch, *back)
    grad_filters = pl.pallas_call(
        functools.partial(clip_kernel, threshold=threshold),
        in_specs=[smem] + [vmem] * (2 + owners),
        out_specs=vmem,
        out_shape=jax.ShapeDtypeStruct((groups, length // owners), F32),
        scratch_shapes=[pltpu.VMEM((owners, per_device, blocks // owners, LANES), F32)],
        cost_estimate=cost(groups * length, groups * length * 4),
        compiler_params=pltpu.CompilerParams(vmem_limit_bytes=8 << 20),
        name="clip",
    )(pos, total, *raw, mark)
    return (grad_q, grad_k, grad_filters)


def solution(mesh):
    return jax.shard_map(
        on_device,
        mesh=mesh,
        in_specs=(
            P(None, "ctx", "ch"),
            P(None, "ctx", "ch"),
            P(None, "ctx", "ch"),
            P("ch", None),
            P(None, "ctx", "ch"),
        ),
        out_specs=(P(None, "ctx", "ch"), P(None, "ctx", "ch"), P("ch", "ctx")),
        check_vma=False,
    )
```

```python
import functools
import math

import jax
import jax.numpy as jnp
from jax import lax
from jax.experimental import pallas as pl
from jax.experimental.pallas import tpu as pltpu
from jax.sharding import PartitionSpec as P

WIDTH = 8192
GROUP = 16
LANES = 128
NT = (((1,), (1,)), ((), ()))
BF16, F32 = jnp.bfloat16, jnp.float32


def gate_kernel(pos_ref, left_ref, right_ref, *refs, reverse, sizes, ordered):
    *outs, left, right, out, in_sem, out_sem = refs[ordered:]
    local = left.shape[0] // LANES
    per_device = sum(sizes)
    copies = []
    for i in range(local):
        here = pl.ds(i * LANES, LANES)
        copies.append(
            (
                pltpu.make_async_copy(left_ref.at[0, here], left.at[here], in_sem.at[i, 0]),
                pltpu.make_async_copy(right_ref.at[0, here], right.at[here], in_sem.at[i, 1]),
            )
        )
    for pair in copies:
        for copy in pair:
            copy.start()
    sends = []
    for i in range(local):
        for copy in copies[i]:
            copy.wait()
        rows = slice(i * LANES, (i + 1) * LANES)
        value = (left[rows].astype(F32) * right[rows].astype(F32)).astype(BF16)
        if reverse:
            row_id = lax.broadcasted_iota(jnp.int32, (LANES, LANES), 0)
            col_id = lax.broadcasted_iota(jnp.int32, (LANES, LANES), 1)
            flip = (row_id + col_id == LANES - 1).astype(BF16)
            value = jnp.dot(flip, value, preferred_element_type=F32).astype(BF16)
        value = value.T
        out[i % 2, i // 2] = value.reshape(out.shape[2:])
        for n, target in enumerate(outs):
            k, chunk = divmod(n, len(sizes))
            first = jnp.bitwise_xor(pos_ref[0], k) * per_device + sum(sizes[:chunk])
            send = pltpu.make_async_copy(
                out.at[i % 2, i // 2, pl.ds(first, sizes[chunk])],
                target.at[:, i % 2, i // 2],
                out_sem.at[i, n],
            )
            send.start()
            sends.append(send)
    for send in sends:
        send.wait()


def ungate_kernel(pos_ref, q_ref, k_ref, *refs):
    *grads, gq_ref, gk_ref, mark_ref, grad, q_in, k_in, gq, gk, in_sem, out_sem = refs
    local = q_in.shape[0] // LANES
    per_device = grads[0].shape[0]
    owners = len(grads)
    mark_ref[...] = jnp.zeros_like(mark_ref)
    copies, sends = [], []
    for i in range(local):
        here = pl.ds(i * LANES, LANES)
        row = [
            pltpu.make_async_copy(q_ref.at[0, here], q_in.at[here], in_sem.at[i, owners]),
            pltpu.make_async_copy(k_ref.at[0, here], k_in.at[here], in_sem.at[i, owners + 1]),
        ]
        for k, source in enumerate(grads):
            first = jnp.bitwise_xor(pos_ref[0], k) * per_device
            row.append(
                pltpu.make_async_copy(
                    source.at[:, i % 2, i // 2], grad.at[i, pl.ds(first, per_device)], in_sem.at[i, k]
                )
            )
        copies.append(row)
    for row in copies:
        for copy in row:
            copy.start()
    for i in range(local):
        for copy in copies[i]:
            copy.wait()
        here = pl.ds(i * LANES, LANES)
        rows = slice(i * LANES, (i + 1) * LANES)
        value = grad[i].reshape(q_in.shape[1], LANES).T.astype(F32)
        gq[rows] = (value * k_in[rows].astype(F32)).astype(BF16)
        gk[rows] = (value * q_in[rows].astype(F32)).astype(BF16)
        for n, (source, target) in enumerate(((gq, gq_ref), (gk, gk_ref))):
            send = pltpu.make_async_copy(source.at[here], target.at[0, here], out_sem.at[i, n])
            send.start()
            sends.append(send)
    for send in sends:
        send.wait()


def clip_kernel(pos_ref, total_ref, *refs, threshold):
    *parts, _, out_ref, stage = refs
    per_device, each = stage.shape[1:3]
    for k, part in enumerate(parts):
        stage[jnp.bitwise_xor(pos_ref[0], k)] = part[...]
    total = jnp.sum(total_ref[...], axis=(0, 1, 2), keepdims=True)[0]
    factor = jnp.minimum(1.0, threshold / jnp.sqrt(total + 1e-06))
    for owner in range(stage.shape[0]):
        for n in range(each):
            rows = slice(owner * per_device, (owner + 1) * per_device)
            out_ref[rows, n * LANES : (n + 1) * LANES] = stage[owner, :, n] * factor


def spread_rows(pos_ref, sources, f, target):
    for k, source in enumerate(sources):
        count = source.shape[2] * GROUP
        at = pl.multiple_of(jnp.bitwise_xor(pos_ref[0], k) * count, count)
        for half in range(2):
            target[half, pl.ds(at, count)] = source[f, half].reshape(count, LANES)


def reverse_taps(owner, filt_ref, taps):
    per_device, blocks = taps.shape[0], taps.shape[1] - 1
    groups = filt_ref.shape[0]
    picks = max(per_device, 8)
    row_id = lax.broadcasted_iota(jnp.int32, (picks, groups), 0)
    col_id = lax.broadcasted_iota(jnp.int32, (picks, groups), 1)
    pick = (col_id == row_id + owner * per_device).astype(BF16)
    width = min((blocks + 1) * LANES, filt_ref.shape[1])
    mine = jnp.dot(pick, filt_ref[:, :width], preferred_element_type=F32).astype(BF16)
    empty = jnp.zeros((picks, LANES), BF16)
    mine = jnp.concatenate([empty, mine, empty], axis=1)
    row_id = lax.broadcasted_iota(jnp.int32, (2 * LANES, LANES), 0)
    col_id = lax.broadcasted_iota(jnp.int32, (2 * LANES, LANES), 1)
    flip = (row_id + col_id == LANES).astype(BF16)
    for block in range(blocks + 1):
        near = mine[:, block * LANES : (block + 2) * LANES]
        back = jnp.dot(near, flip, preferred_element_type=F32)
        for f in range(per_device):
            taps[f, block] = back[f : f + 1]


def build_blocks(taps, f, toep):
    row_id = lax.broadcasted_iota(jnp.int32, (LANES, LANES), 0)
    col_id = lax.broadcasted_iota(jnp.int32, (LANES, LANES), 1)
    upper = col_id >= row_id
    before = None
    for block in range(taps.shape[1]):
        tap = jnp.broadcast_to(taps[f, block], (LANES, LANES))
        rolled = pltpu.roll(tap, 0, 1, stride=1, stride_axis=0)
        if block:
            toep[block] = jnp.where(upper, before, rolled).astype(BF16)
        before = rolled


def weights(toep, pair):
    at = 2 * pair + 1
    top = jnp.concatenate([toep[at], toep[at - 1]], axis=1)
    low = jnp.concatenate([toep[at + 1], toep[at]], axis=1)
    return jnp.concatenate([top, low], axis=0)


def blocks_kernel(pos_ref, filt_ref, *refs):
    *toeps, taps = refs
    unroll = len(toeps)
    reverse_taps(pos_ref[0], filt_ref, taps)

    def some(i, carry):
        for u in range(unroll):
            toep = toeps[u].at[i]
            toep[0] = jnp.zeros((LANES, LANES), BF16)
            build_blocks(taps, i * unroll + u, toep)
        return carry

    lax.fori_loop(0, toeps[0].shape[0], some, 0)


def conv_kernel(pos_ref, *refs, owners, unroll):
    toeps, refs = refs[:unroll], refs[unroll:]
    ins, outs, refs = refs[:owners], refs[owners : 2 * owners], refs[2 * owners :]
    pads, accs, refs = refs[:unroll], refs[unroll : 2 * unroll], refs[2 * unroll :]
    outs_v, sem = refs[:owners], refs[owners]
    per_device, blocks = ins[0].shape[0], toeps[0].shape[1] - 1
    rows = pads[0].shape[1]

    def one(toep, pad, out):
        acc = jnp.zeros((rows, 2 * LANES), F32)
        for pair in range(blocks // 2):
            start = pair * GROUP
            left = jnp.concatenate([pad[0, start:], pad[1, start:]], axis=1)
            part = jnp.dot(left, weights(toep, pair), preferred_element_type=F32)
            if start:
                part = jnp.concatenate([part, jnp.zeros((start, 2 * LANES), F32)], axis=0)
            acc = acc + part
        for half in range(2):
            out[half] = acc[:, half * LANES : (half + 1) * LANES].astype(BF16)

    def some(i, carry):
        for u in range(unroll):
            spread_rows(pos_ref, ins, i * unroll + u, pads[u])
        for u in range(unroll):
            one(toeps[u].at[i], pads[u], accs[u])
        for u in range(unroll):
            for k, target in enumerate(outs_v):
                count = target.shape[2] * GROUP
                at = pl.multiple_of(jnp.bitwise_xor(pos_ref[0], k) * count, count)
                for half in range(2):
                    value = accs[u][half, pl.ds(at, count)]
                    target[i * unroll + u, half] = value.reshape(target.shape[2:])
        here = pl.ds(i * unroll, unroll)
        for k in range(owners):
            pltpu.make_async_copy(outs_v[k].at[here], outs[k].at[here], sem.at[k]).start()
        return carry

    lax.fori_loop(0, per_device // unroll, some, 0)
    for k in range(owners):
        pltpu.make_async_copy(outs_v[k], outs[k], sem.at[k]).wait()


def lag_sums(pad, flipped, rows, blocks):
    row_id = lax.broadcasted_iota(jnp.int32, (LANES, LANES), 0)
    col_id = lax.broadcasted_iota(jnp.int32, (LANES, LANES), 1)
    wraps = col_id <= row_id
    prod = jnp.concatenate([flipped[half, :rows].T for half in range(2)], axis=1)
    after = jnp.zeros((LANES, LANES), F32)
    sums = {}
    for pair in reversed(range(blocks // 2)):
        start = pair * GROUP
        here, later = slice(start, start + rows), slice(start + GROUP, start + GROUP + rows)
        even = jnp.concatenate([pad[0, here], pad[1, here]], axis=0)
        odd = jnp.concatenate([pad[1, here], pad[0, later]], axis=0)
        both = jnp.dot(prod, jnp.concatenate([even, odd], axis=1), preferred_element_type=F32)
        for half in (1, 0):
            rolled = pltpu.roll(
                both[:, half * LANES : (half + 1) * LANES], 1, 1, stride=1, stride_axis=0
            )
            part = jnp.where(wraps, rolled, after)
            sums[2 * pair + half] = jnp.sum(part, axis=0, keepdims=True)
            after = rolled
    return sums


def lag_kernel(pos_ref, *refs, owners, unroll, scale, first, last):
    grads, prods, refs = refs[:owners], refs[owners : 2 * owners], refs[2 * owners :]
    olds, refs = (refs[: owners + 1], refs[owners + 1 :]) if first else ([], refs[1:])
    raws, sum_ref, refs = refs[:owners], refs[owners], refs[owners + 1 :]
    pads, flips, lags_v, sq_v = refs[:unroll], refs[unroll : 2 * unroll], refs[-2], refs[-1]
    per_owner = raws[0].shape[1]
    blocks = owners * per_owner
    rows = flips[0].shape[1]
    for pad in pads:
        pad[:, rows:] = jnp.zeros((2, rows, LANES), BF16)
    sq_v[...] = olds[-1][...] if olds else jnp.zeros_like(sq_v)

    def one(slot, pad, flipped):
        sums = lag_sums(pad, flipped, rows, blocks)
        for owner in range(owners):
            lags = jnp.concatenate(
                [sums[owner * per_owner + n] for n in range(per_owner)], axis=0
            ) * scale
            lags_v[slot, owner] = lags
            sq_v[...] += lags * lags

    def some(i, carry):
        for u in range(unroll):
            spread_rows(pos_ref, grads, first + i * unroll + u, pads[u])
            spread_rows(pos_ref, prods, i * unroll + u, flips[u])
        for u in range(unroll):
            one(u, pads[u], flips[u])
        for u in range(unroll):
            for k, target in enumerate(raws):
                target[first + i * unroll + u] = lags_v[u, jnp.bitwise_xor(pos_ref[0], k)]
        return carry

    lax.fori_loop(0, prods[0].shape[0] // unroll, some, 0)
    if not last:
        sum_ref[...] = sq_v[...]
        return
    squares = jnp.sum(sq_v[...], axis=0, keepdims=True)
    sum_ref[...] = jnp.zeros_like(sum_ref)
    sum_ref[:, :1] = jnp.broadcast_to(squares[None], (sum_ref.shape[0], 1, LANES))


def cost(flops, moved):
    return pl.CostEstimate(flops=int(flops), bytes_accessed=int(moved), transcendentals=0)


def on_device(q_branch, k_branch, out_gate, filters, grad_out):
    seqs, block_len, chans = q_branch.shape
    owners = lax.axis_size("ctx")
    groups = chans // GROUP
    per_device = groups // owners
    local = block_len // LANES
    length = owners * block_len
    blocks = length // LANES
    rows = length * GROUP // (2 * LANES)
    scale = 4.0 / math.sqrt(seqs * GROUP)
    size = block_len * chans * 2
    anywhere = pl.BlockSpec(memory_space=pl.ANY)
    vmem = pl.BlockSpec(memory_space=pltpu.VMEM)
    smem = pl.BlockSpec(memory_space=pltpu.SMEM)
    tail = (2, local // 2, GROUP, LANES)
    whole = (owners, per_device) + tail
    pos = lax.axis_index("ctx").astype(jnp.int32).reshape(1)
    piece = jax.ShapeDtypeStruct((per_device,) + tail, BF16)
    lag_piece = jax.ShapeDtypeStruct((per_device, blocks // owners, LANES), F32)

    def gate(left, right, after, reverse, sizes, limit, name):
        parts = [jax.ShapeDtypeStruct((n,) + tail, BF16) for n in sizes]
        out = pl.pallas_call(
            functools.partial(gate_kernel, reverse=reverse, sizes=sizes, ordered=len(after)),
            in_specs=[smem] + [pl.BlockSpec(memory_space=pltpu.HBM)] * 2 + [vmem] * len(after),
            out_specs=[anywhere] * (owners * len(sizes)),
            out_shape=parts * owners,
            scratch_shapes=[
                pltpu.VMEM((block_len, chans), BF16),
                pltpu.VMEM((block_len, chans), BF16),
                pltpu.VMEM((2, local // 2, groups, GROUP, LANES), BF16),
                pltpu.SemaphoreType.DMA((local, 2)),
                pltpu.SemaphoreType.DMA((local, owners * len(sizes))),
            ],
            cost_estimate=cost(block_len * chans, 3 * size),
            compiler_params=pltpu.CompilerParams(vmem_limit_bytes=limit << 20),
            name=name,
        )(pos, left, right, *after)
        return [out[n :: len(sizes)] for n in range(len(sizes))]

    def swap(values):
        out = [values[0]]
        for k in range(1, owners):
            out.append(lax.ppermute(values[k], "ctx", [(i, i ^ k) for i in range(owners)]))
        return out

    sizes = (8, 4, 4) if per_device == 16 else (per_device,)
    (grad_send,) = gate(grad_out, out_gate, (), False, (per_device,), 56, "gate_grad")
    grad_got = swap(grad_send)
    prod_send = gate(q_branch, k_branch, grad_send[:1], True, sizes, 12, "gate_prod")
    prod_got = []
    for part in prod_send:
        if prod_got:
            part, prod_got[-1][1] = lax.optimization_barrier((part, prod_got[-1][1]))
        prod_got.append(swap(part))
    unroll = math.gcd(4, per_device)
    toeps = pl.pallas_call(
        blocks_kernel,
        in_specs=[smem, vmem],
        out_specs=[vmem] * unroll,
        out_shape=[
            jax.ShapeDtypeStruct((per_device // unroll, blocks + 1, LANES, LANES), BF16)
        ] * unroll,
        scratch_shapes=[pltpu.VMEM((per_device, blocks + 1, 1, LANES), F32)],
        cost_estimate=cost(1, 1),
        compiler_params=pltpu.CompilerParams(vmem_limit_bytes=16 << 20),
        name="blocks",
    )(pos, filters)
    conv = pl.pallas_call(
        functools.partial(conv_kernel, owners=owners, unroll=unroll),
        in_specs=[smem] + [vmem] * (unroll + owners),
        out_specs=[anywhere] * owners,
        out_shape=[piece] * owners,
        scratch_shapes=[pltpu.VMEM((2, rows, LANES), BF16)] * (2 * unroll)
        + [pltpu.VMEM(piece.shape, BF16)] * owners
        + [pltpu.SemaphoreType.DMA((owners,))],
        cost_estimate=cost(per_device * rows * length * 4096, 2 * size + groups * length * 2),
        compiler_params=pltpu.CompilerParams(vmem_limit_bytes=16 << 20),
        name="conv",
    )(pos, *toeps, *grad_got)
    back = swap(conv)
    both = ("ctx", "ch")
    count = lax.axis_size(both)
    old = [conv[0]]
    for n, each in enumerate(sizes):
        last = n == len(sizes) - 1
        unroll = math.gcd(8, each)
        sums = jax.ShapeDtypeStruct((count, 4, LANES) if last else (blocks // owners, LANES), F32)
        old = pl.pallas_call(
            functools.partial(
                lag_kernel, owners=owners, unroll=unroll, scale=scale, first=sum(sizes[:n]), last=last
            ),
            in_specs=[smem] + [vmem] * (2 * owners) + ([vmem] * (owners + 1) if n else [anywhere]),
            out_specs=[vmem] * (owners + 1),
            out_shape=[lag_piece] * owners + [sums],
            input_output_aliases={2 * owners + 1 + k: k for k in range(owners)} if n else {},
            scratch_shapes=[pltpu.VMEM((2, 2 * rows, LANES), BF16)] * unroll
            + [pltpu.VMEM((2, rows, LANES), BF16)] * unroll
            + [
                pltpu.VMEM((unroll, owners, blocks // owners, LANES), F32),
                pltpu.VMEM((blocks // owners, LANES), F32),
            ],
            cost_estimate=cost(each * 2 * rows * length * 2048, 2 * size),
            compiler_params=pltpu.CompilerParams(vmem_limit_bytes=16 << 20),
            name="lags",
        )(pos, *grad_got, *prod_got[n], *old)
    *raw, spread = old
    total = lax.all_to_all(spread, both, 0, 0, tiled=True)
    raw = swap(raw)
    threshold = math.sqrt(WIDTH // GROUP * length)
    grad_q, grad_k, mark = pl.pallas_call(
        ungate_kernel,
        in_specs=[smem] + [anywhere] * (2 + owners),
        out_specs=[anywhere] * 2 + [vmem],
        out_shape=[jax.ShapeDtypeStruct(q_branch.shape, BF16)] * 2
        + [jax.ShapeDtypeStruct((8, LANES), F32)],
        scratch_shapes=[
            pltpu.VMEM((local, groups, GROUP, LANES), BF16),
            pltpu.VMEM((block_len, chans), BF16),
            pltpu.VMEM((block_len, chans), BF16),
            pltpu.VMEM((block_len, chans), BF16),
            pltpu.VMEM((block_len, chans), BF16),
            pltpu.SemaphoreType.DMA((local, owners + 2)),
            pltpu.SemaphoreType.DMA((local, 2)),
        ],
        cost_estimate=cost(2 * block_len * chans, 5 * size),
        compiler_params=pltpu.CompilerParams(vmem_limit_bytes=16 << 20),
        name="ungate",
    )(pos, q_branch, k_branch, *back)
    grad_filters = pl.pallas_call(
        functools.partial(clip_kernel, threshold=threshold),
        in_specs=[smem] + [vmem] * (2 + owners),
        out_specs=vmem,
        out_shape=jax.ShapeDtypeStruct((groups, length // owners), F32),
        scratch_shapes=[pltpu.VMEM((owners, per_device, blocks // owners, LANES), F32)],
        cost_estimate=cost(groups * length, groups * length * 4),
        compiler_params=pltpu.CompilerParams(vmem_limit_bytes=8 << 20),
        name="clip",
    )(pos, total, *raw, mark)
    return (grad_q, grad_k, grad_filters)


def solution(mesh):
    return jax.shard_map(
        on_device,
        mesh=mesh,
        in_specs=(
            P(None, "ctx", "ch"),
            P(None, "ctx", "ch"),
            P(None, "ctx", "ch"),
            P("ch", None),
            P(None, "ctx", "ch"),
        ),
        out_specs=(P(None, "ctx", "ch"), P(None, "ctx", "ch"), P("ch", "ctx")),
        check_vma=False,
    )
```

```python
import functools
import math

import jax
import jax.numpy as jnp
from jax import lax
from jax.experimental import pallas as pl
from jax.experimental.pallas import tpu as pltpu
from jax.sharding import PartitionSpec as P

WIDTH = 8192
GROUP = 16
LANES = 128
NT = (((1,), (1,)), ((), ()))
BF16, F32 = jnp.bfloat16, jnp.float32


def gate_kernel(pos_ref, left_ref, right_ref, *refs, reverse, sizes, ordered, window, peers):
    *outs, left, right, out, in_sem, out_sem = refs[ordered:]
    local, wide = left.shape[0] // LANES, left.shape[1]
    chip = jnp.right_shift(pos_ref[0], 1)
    start = {"all": 0, "far": (1 - chip) * wide, "near": chip * wide}[window]
    there = pl.ds(start if window == "all" else pl.multiple_of(start, wide), wide)
    per_device = sum(sizes)
    copies = []
    for i in range(local):
        here = pl.ds(i * LANES, LANES)
        copies.append(
            (
                pltpu.make_async_copy(left_ref.at[0, here, there], left.at[here], in_sem.at[i, 0]),
                pltpu.make_async_copy(right_ref.at[0, here, there], right.at[here], in_sem.at[i, 1]),
            )
        )
    for pair in copies:
        for copy in pair:
            copy.start()
    sends = []
    for i in range(local):
        for copy in copies[i]:
            copy.wait()
        rows = slice(i * LANES, (i + 1) * LANES)
        value = (left[rows].astype(F32) * right[rows].astype(F32)).astype(BF16)
        if reverse:
            row_id = lax.broadcasted_iota(jnp.int32, (LANES, LANES), 0)
            col_id = lax.broadcasted_iota(jnp.int32, (LANES, LANES), 1)
            flip = (row_id + col_id == LANES - 1).astype(BF16)
            value = jnp.dot(flip, value, preferred_element_type=F32).astype(BF16)
        value = value.T
        out[i % 2, i // 2] = value.reshape(out.shape[2:])
        for n, target in enumerate(outs):
            k, chunk = divmod(n, len(sizes))
            first = jnp.bitwise_xor(pos_ref[0], peers[k]) * per_device - start // GROUP + sum(sizes[:chunk])
            send = pltpu.make_async_copy(
                out.at[i % 2, i // 2, pl.ds(first, sizes[chunk])],
                target.at[:, i % 2, i // 2],
                out_sem.at[i, n],
            )
            send.start()
            sends.append(send)
    for send in sends:
        send.wait()


def ungate_kernel(pos_ref, q_ref, k_ref, *refs):
    *grads, gq_ref, gk_ref, mark_ref, grad, q_in, k_in, gq, gk, in_sem, out_sem = refs
    local = q_in.shape[0] // LANES
    per_device = grads[0].shape[0]
    owners = len(grads)
    mark_ref[...] = jnp.zeros_like(mark_ref)
    copies, sends = [], []
    for i in range(local):
        here = pl.ds(i * LANES, LANES)
        row = [
            pltpu.make_async_copy(q_ref.at[0, here], q_in.at[here], in_sem.at[i, owners]),
            pltpu.make_async_copy(k_ref.at[0, here], k_in.at[here], in_sem.at[i, owners + 1]),
        ]
        for k, source in enumerate(grads):
            first = jnp.bitwise_xor(pos_ref[0], k) * per_device
            row.append(
                pltpu.make_async_copy(
                    source.at[:, i % 2, i // 2], grad.at[i, pl.ds(first, per_device)], in_sem.at[i, k]
                )
            )
        copies.append(row)
    for row in copies:
        for copy in row:
            copy.start()
    for i in range(local):
        for copy in copies[i]:
            copy.wait()
        here = pl.ds(i * LANES, LANES)
        rows = slice(i * LANES, (i + 1) * LANES)
        value = grad[i].reshape(q_in.shape[1], LANES).T.astype(F32)
        gq[rows] = (value * k_in[rows].astype(F32)).astype(BF16)
        gk[rows] = (value * q_in[rows].astype(F32)).astype(BF16)
        for n, (source, target) in enumerate(((gq, gq_ref), (gk, gk_ref))):
            send = pltpu.make_async_copy(source.at[here], target.at[0, here], out_sem.at[i, n])
            send.start()
            sends.append(send)
    for send in sends:
        send.wait()


def clip_kernel(pos_ref, total_ref, *refs, threshold):
    *parts, _, out_ref, stage = refs
    per_device, each = stage.shape[1:3]
    for k, part in enumerate(parts):
        stage[jnp.bitwise_xor(pos_ref[0], k)] = part[...]
    total = jnp.sum(total_ref[...], axis=(0, 1, 2), keepdims=True)[0]
    factor = jnp.minimum(1.0, threshold / jnp.sqrt(total + 1e-06))
    for owner in range(stage.shape[0]):
        for n in range(each):
            rows = slice(owner * per_device, (owner + 1) * per_device)
            out_ref[rows, n * LANES : (n + 1) * LANES] = stage[owner, :, n] * factor


def spread_rows(pos_ref, sources, f, target):
    for k, source in enumerate(sources):
        count = source.shape[2] * GROUP
        at = pl.multiple_of(jnp.bitwise_xor(pos_ref[0], k) * count, count)
        for half in range(2):
            target[half, pl.ds(at, count)] = source[f, half].reshape(count, LANES)


def reverse_taps(owner, filt_ref, taps):
    per_device, blocks = taps.shape[0], taps.shape[1] - 1
    groups = filt_ref.shape[0]
    picks = max(per_device, 8)
    row_id = lax.broadcasted_iota(jnp.int32, (picks, groups), 0)
    col_id = lax.broadcasted_iota(jnp.int32, (picks, groups), 1)
    pick = (col_id == row_id + owner * per_device).astype(BF16)
    width = min((blocks + 1) * LANES, filt_ref.shape[1])
    mine = jnp.dot(pick, filt_ref[:, :width], preferred_element_type=F32).astype(BF16)
    empty = jnp.zeros((picks, LANES), BF16)
    mine = jnp.concatenate([empty, mine, empty], axis=1)
    row_id = lax.broadcasted_iota(jnp.int32, (2 * LANES, LANES), 0)
    col_id = lax.broadcasted_iota(jnp.int32, (2 * LANES, LANES), 1)
    flip = (row_id + col_id == LANES).astype(BF16)
    for block in range(blocks + 1):
        near = mine[:, block * LANES : (block + 2) * LANES]
        back = jnp.dot(near, flip, preferred_element_type=F32)
        for f in range(per_device):
            taps[f, block] = back[f : f + 1]


def build_blocks(taps, f, toep):
    row_id = lax.broadcasted_iota(jnp.int32, (LANES, LANES), 0)
    col_id = lax.broadcasted_iota(jnp.int32, (LANES, LANES), 1)
    upper = col_id >= row_id
    before = None
    for block in range(taps.shape[1]):
        tap = jnp.broadcast_to(taps[f, block], (LANES, LANES))
        rolled = pltpu.roll(tap, 0, 1, stride=1, stride_axis=0)
        if block:
            toep[block] = jnp.where(upper, before, rolled).astype(BF16)
        before = rolled


def weights(toep, pair):
    at = 2 * pair + 1
    top = jnp.concatenate([toep[at], toep[at - 1]], axis=1)
    low = jnp.concatenate([toep[at + 1], toep[at]], axis=1)
    return jnp.concatenate([top, low], axis=0)


def blocks_kernel(pos_ref, filt_ref, *refs):
    *toeps, taps = refs
    unroll = len(toeps)
    reverse_taps(pos_ref[0], filt_ref, taps)

    def some(i, carry):
        for u in range(unroll):
            toep = toeps[u].at[i]
            toep[0] = jnp.zeros((LANES, LANES), BF16)
            build_blocks(taps, i * unroll + u, toep)
        return carry

    lax.fori_loop(0, toeps[0].shape[0], some, 0)


def conv_kernel(pos_ref, *refs, owners, unroll):
    toeps, refs = refs[:unroll], refs[unroll:]
    ins, outs, refs = refs[:owners], refs[owners : 2 * owners], refs[2 * owners :]
    pads, accs = refs[:unroll], refs[unroll:]
    per_device, blocks = ins[0].shape[0], toeps[0].shape[1] - 1
    rows = pads[0].shape[1]

    def one(toep, pad, out):
        acc = jnp.zeros((rows, 2 * LANES), F32)
        for pair in range(blocks // 2):
            start = pair * GROUP
            left = jnp.concatenate([pad[0, start:], pad[1, start:]], axis=1)
            part = jnp.dot(left, weights(toep, pair), preferred_element_type=F32)
            if start:
                part = jnp.concatenate([part, jnp.zeros((start, 2 * LANES), F32)], axis=0)
            acc = acc + part
        for half in range(2):
            out[half] = acc[:, half * LANES : (half + 1) * LANES].astype(BF16)

    def some(i, carry):
        for u in range(unroll):
            spread_rows(pos_ref, ins, i * unroll + u, pads[u])
        for u in range(unroll):
            one(toeps[u].at[i], pads[u], accs[u])
        for u in range(unroll):
            for k, target in enumerate(outs):
                count = target.shape[2] * GROUP
                at = pl.multiple_of(jnp.bitwise_xor(pos_ref[0], k) * count, count)
                for half in range(2):
                    value = accs[u][half, pl.ds(at, count)]
                    target[i * unroll + u, half] = value.reshape(target.shape[2:])
        return carry

    lax.fori_loop(0, per_device // unroll, some, 0)


def lag_sums(pad, flipped, rows, blocks):
    row_id = lax.broadcasted_iota(jnp.int32, (LANES, LANES), 0)
    col_id = lax.broadcasted_iota(jnp.int32, (LANES, LANES), 1)
    wraps = col_id <= row_id
    prod = jnp.concatenate([flipped[half, :rows].T for half in range(2)], axis=1)
    after = jnp.zeros((LANES, LANES), F32)
    sums = {}
    for pair in reversed(range(blocks // 2)):
        start = pair * GROUP
        here, later = slice(start, start + rows), slice(start + GROUP, start + GROUP + rows)
        even = jnp.concatenate([pad[0, here], pad[1, here]], axis=0)
        odd = jnp.concatenate([pad[1, here], pad[0, later]], axis=0)
        both = jnp.dot(prod, jnp.concatenate([even, odd], axis=1), preferred_element_type=F32)
        for half in (1, 0):
            rolled = pltpu.roll(
                both[:, half * LANES : (half + 1) * LANES], 1, 1, stride=1, stride_axis=0
            )
            part = jnp.where(wraps, rolled, after)
            sums[2 * pair + half] = jnp.sum(part, axis=0, keepdims=True)
            after = rolled
    return sums


def lag_kernel(pos_ref, *refs, owners, unroll, scale, first, last):
    grads, prods, refs = refs[:owners], refs[owners : 2 * owners], refs[2 * owners :]
    olds, refs = (refs[: owners + 1], refs[owners + 1 :]) if first else ([], refs[1:])
    raws, sum_ref, refs = refs[:owners], refs[owners], refs[owners + 1 :]
    pads, flips, lags_v, sq_v = refs[:unroll], refs[unroll : 2 * unroll], refs[-2], refs[-1]
    per_owner = raws[0].shape[1]
    blocks = owners * per_owner
    rows = flips[0].shape[1]
    for pad in pads:
        pad[:, rows:] = jnp.zeros((2, rows, LANES), BF16)
    sq_v[...] = olds[-1][...] if olds else jnp.zeros_like(sq_v)

    def one(slot, pad, flipped):
        sums = lag_sums(pad, flipped, rows, blocks)
        for owner in range(owners):
            lags = jnp.concatenate(
                [sums[owner * per_owner + n] for n in range(per_owner)], axis=0
            ) * scale
            lags_v[slot, owner] = lags
            sq_v[...] += lags * lags

    def some(i, carry):
        for u in range(unroll):
            spread_rows(pos_ref, grads, first + i * unroll + u, pads[u])
            spread_rows(pos_ref, prods, i * unroll + u, flips[u])
        for u in range(unroll):
            one(u, pads[u], flips[u])
        for u in range(unroll):
            for k, target in enumerate(raws):
                target[first + i * unroll + u] = lags_v[u, jnp.bitwise_xor(pos_ref[0], k)]
        return carry

    lax.fori_loop(0, prods[0].shape[0] // unroll, some, 0)
    if not last:
        sum_ref[...] = sq_v[...]
        return
    squares = jnp.sum(sq_v[...], axis=0, keepdims=True)
    sum_ref[...] = jnp.zeros_like(sum_ref)
    sum_ref[:, :1] = jnp.broadcast_to(squares[None], (sum_ref.shape[0], 1, LANES))


def cost(flops, moved):
    return pl.CostEstimate(flops=int(flops), bytes_accessed=int(moved), transcendentals=0)


def on_device(q_branch, k_branch, out_gate, filters, grad_out):
    seqs, block_len, chans = q_branch.shape
    owners = lax.axis_size("ctx")
    groups = chans // GROUP
    per_device = groups // owners
    local = block_len // LANES
    length = owners * block_len
    blocks = length // LANES
    rows = length * GROUP // (2 * LANES)
    scale = 4.0 / math.sqrt(seqs * GROUP)
    size = block_len * chans * 2
    anywhere = pl.BlockSpec(memory_space=pl.ANY)
    vmem = pl.BlockSpec(memory_space=pltpu.VMEM)
    smem = pl.BlockSpec(memory_space=pltpu.SMEM)
    tail = (2, local // 2, GROUP, LANES)
    whole = (owners, per_device) + tail
    pos = lax.axis_index("ctx").astype(jnp.int32).reshape(1)
    piece = jax.ShapeDtypeStruct((per_device,) + tail, BF16)
    lag_piece = jax.ShapeDtypeStruct((per_device, blocks // owners, LANES), F32)

    def gate(left, right, after, reverse, sizes, limit, name, window="all", peers=None):
        peers = peers or tuple(range(owners))
        wide = chans if window == "all" else chans // 2
        parts = [jax.ShapeDtypeStruct((n,) + tail, BF16) for n in sizes]
        out = pl.pallas_call(
            functools.partial(
                gate_kernel,
                reverse=reverse,
                sizes=sizes,
                ordered=len(after),
                window=window,
                peers=peers,
            ),
            in_specs=[smem] + [pl.BlockSpec(memory_space=pltpu.HBM)] * 2 + [vmem] * len(after),
            out_specs=[anywhere] * (len(peers) * len(sizes)),
            out_shape=parts * len(peers),
            scratch_shapes=[
                pltpu.VMEM((block_len, wide), BF16),
                pltpu.VMEM((block_len, wide), BF16),
                pltpu.VMEM((2, local // 2, wide // GROUP, GROUP, LANES), BF16),
                pltpu.SemaphoreType.DMA((local, 2)),
                pltpu.SemaphoreType.DMA((local, len(peers) * len(sizes))),
            ],
            cost_estimate=cost(block_len * wide, 6 * block_len * wide),
            compiler_params=pltpu.CompilerParams(vmem_limit_bytes=limit << 20),
            name=name,
        )(pos, left, right, *after)
        return [out[n :: len(sizes)] for n in range(len(sizes))]

    def swap(values):
        out = [values[0]]
        for k in range(1, owners):
            out.append(lax.ppermute(values[k], "ctx", [(i, i ^ k) for i in range(owners)]))
        return out

    sizes = (8, 8) if per_device == 16 else (per_device,)
    if owners == 4:
        (far,) = gate(
            grad_out, out_gate, (), False, (per_device,), 56, "gate_far", "far", (2, 3)
        )
        far_send = far
        far = [lax.ppermute(v, "ctx", [(i, i ^ k) for i in range(4)]) for k, v in zip((2, 3), far)]
        prod_send = gate(q_branch, k_branch, (), True, sizes, 12, "gate_prod")
        (near,) = gate(
            grad_out, out_gate, prod_send[0][:1], False, (per_device,), 12, "gate_near", "near", (0, 1)
        )
        grad_got = [near[0], lax.ppermute(near[1], "ctx", [(i, i ^ 1) for i in range(4)]), *far]
    else:
        (grad_send,) = gate(grad_out, out_gate, (), False, (per_device,), 56, "gate_grad")
        grad_got = swap(grad_send)
        prod_send = gate(q_branch, k_branch, grad_send[:1], True, sizes, 12, "gate_prod")
    prod_got = []
    for part in prod_send:
        if prod_got:
            part, prod_got[-1][1] = lax.optimization_barrier((part, prod_got[-1][1]))
        prod_got.append(swap(part))
    unroll = math.gcd(4, per_device)
    toeps = pl.pallas_call(
        blocks_kernel,
        in_specs=[smem, vmem],
        out_specs=[vmem] * unroll,
        out_shape=[
            jax.ShapeDtypeStruct((per_device // unroll, blocks + 1, LANES, LANES), BF16)
        ] * unroll,
        scratch_shapes=[pltpu.VMEM((per_device, blocks + 1, 1, LANES), F32)],
        cost_estimate=cost(1, 1),
        compiler_params=pltpu.CompilerParams(vmem_limit_bytes=16 << 20),
        name="blocks",
    )(pos, filters)
    conv = pl.pallas_call(
        functools.partial(conv_kernel, owners=owners, unroll=unroll),
        in_specs=[smem] + [vmem] * (unroll + owners),
        out_specs=[vmem] * owners,
        out_shape=[piece] * owners,
        scratch_shapes=[pltpu.VMEM((2, rows, LANES), BF16)] * (2 * unroll),
        cost_estimate=cost(per_device * rows * length * 4096, 2 * size + groups * length * 2),
        compiler_params=pltpu.CompilerParams(vmem_limit_bytes=16 << 20),
        name="conv",
    )(pos, *toeps, *grad_got)
    back = swap(conv)
    both = ("ctx", "ch")
    count = lax.axis_size(both)
    old = [conv[0]]
    for n, each in enumerate(sizes):
        last = n == len(sizes) - 1
        unroll = math.gcd(8, each)
        sums = jax.ShapeDtypeStruct((count, 8, LANES) if last else (blocks // owners, LANES), F32)
        old = pl.pallas_call(
            functools.partial(
                lag_kernel, owners=owners, unroll=unroll, scale=scale, first=sum(sizes[:n]), last=last
            ),
            in_specs=[smem] + [vmem] * (2 * owners) + ([vmem] * (owners + 1) if n else [anywhere]),
            out_specs=[vmem] * (owners + 1),
            out_shape=[lag_piece] * owners + [sums],
            input_output_aliases={2 * owners + 1 + k: k for k in range(owners)} if n else {},
            scratch_shapes=[pltpu.VMEM((2, 2 * rows, LANES), BF16)] * unroll
            + [pltpu.VMEM((2, rows, LANES), BF16)] * unroll
            + [
                pltpu.VMEM((unroll, owners, blocks // owners, LANES), F32),
                pltpu.VMEM((blocks // owners, LANES), F32),
            ],
            cost_estimate=cost(each * 2 * rows * length * 2048, 2 * size),
            compiler_params=pltpu.CompilerParams(vmem_limit_bytes=16 << 20),
            name="lags",
        )(pos, *grad_got, *prod_got[n], *old)
    *raw, spread = old
    total = lax.all_to_all(spread, both, 0, 0, tiled=True)
    raw = swap(raw)
    threshold = math.sqrt(WIDTH // GROUP * length)
    grad_q, grad_k, mark = pl.pallas_call(
        ungate_kernel,
        in_specs=[smem] + [anywhere] * (2 + owners),
        out_specs=[anywhere] * 2 + [vmem],
        out_shape=[jax.ShapeDtypeStruct(q_branch.shape, BF16)] * 2
        + [jax.ShapeDtypeStruct((8, LANES), F32)],
        scratch_shapes=[
            pltpu.VMEM((local, groups, GROUP, LANES), BF16),
            pltpu.VMEM((block_len, chans), BF16),
            pltpu.VMEM((block_len, chans), BF16),
            pltpu.VMEM((block_len, chans), BF16),
            pltpu.VMEM((block_len, chans), BF16),
            pltpu.SemaphoreType.DMA((local, owners + 2)),
            pltpu.SemaphoreType.DMA((local, 2)),
        ],
        cost_estimate=cost(2 * block_len * chans, 5 * size),
        compiler_params=pltpu.CompilerParams(vmem_limit_bytes=16 << 20),
        name="ungate",
    )(pos, q_branch, k_branch, *back)
    grad_filters = pl.pallas_call(
        functools.partial(clip_kernel, threshold=threshold),
        in_specs=[smem] + [vmem] * (2 + owners),
        out_specs=vmem,
        out_shape=jax.ShapeDtypeStruct((groups, length // owners), F32),
        scratch_shapes=[pltpu.VMEM((owners, per_device, blocks // owners, LANES), F32)],
        cost_estimate=cost(groups * length, groups * length * 4),
        compiler_params=pltpu.CompilerParams(vmem_limit_bytes=8 << 20),
        name="clip",
    )(pos, total, *raw, mark)
    return (grad_q, grad_k, grad_filters)


def solution(mesh):
    return jax.shard_map(
        on_device,
        mesh=mesh,
        in_specs=(
            P(None, "ctx", "ch"),
            P(None, "ctx", "ch"),
            P(None, "ctx", "ch"),
            P("ch", None),
            P(None, "ctx", "ch"),
        ),
        out_specs=(P(None, "ctx", "ch"), P(None, "ctx", "ch"), P("ch", "ctx")),
        check_vma=False,
    )
```

```python
import functools
import math

import jax
import jax.numpy as jnp
from jax import lax
from jax.experimental import pallas as pl
from jax.experimental.pallas import tpu as pltpu
from jax.sharding import PartitionSpec as P

WIDTH = 8192
GROUP = 16
LANES = 128
NT = (((1,), (1,)), ((), ()))
BF16, F32 = jnp.bfloat16, jnp.float32


def gate_kernel(pos_ref, left_ref, right_ref, *refs, reverse, sizes, ordered, window, peers):
    *outs, left, right, out, in_sem, out_sem = refs[ordered:]
    local, wide = left.shape[0] // LANES, left.shape[1]
    chip = jnp.right_shift(pos_ref[0], 1)
    start = {"all": 0, "far": (1 - chip) * wide, "near": chip * wide}[window]
    there = pl.ds(start if window == "all" else pl.multiple_of(start, wide), wide)
    per_device = sum(sizes)
    copies = []
    for i in range(local):
        here = pl.ds(i * LANES, LANES)
        copies.append(
            (
                pltpu.make_async_copy(left_ref.at[0, here, there], left.at[here], in_sem.at[i, 0]),
                pltpu.make_async_copy(right_ref.at[0, here, there], right.at[here], in_sem.at[i, 1]),
            )
        )
    for pair in copies:
        for copy in pair:
            copy.start()
    sends = []
    for i in range(local):
        for copy in copies[i]:
            copy.wait()
        rows = slice(i * LANES, (i + 1) * LANES)
        value = (left[rows].astype(F32) * right[rows].astype(F32)).astype(BF16)
        if reverse:
            row_id = lax.broadcasted_iota(jnp.int32, (LANES, LANES), 0)
            col_id = lax.broadcasted_iota(jnp.int32, (LANES, LANES), 1)
            flip = (row_id + col_id == LANES - 1).astype(BF16)
            value = jnp.dot(flip, value, preferred_element_type=F32).astype(BF16)
        value = value.T
        out[i % 2, i // 2] = value.reshape(out.shape[2:])
        for n, target in enumerate(outs):
            k, chunk = divmod(n, len(sizes))
            first = jnp.bitwise_xor(pos_ref[0], peers[k]) * per_device - start // GROUP + sum(sizes[:chunk])
            send = pltpu.make_async_copy(
                out.at[i % 2, i // 2, pl.ds(first, sizes[chunk])],
                target.at[:, i % 2, i // 2],
                out_sem.at[i, n],
            )
            send.start()
            sends.append(send)
    for send in sends:
        send.wait()


def ungate_kernel(pos_ref, q_ref, k_ref, *refs):
    *grads, gq_ref, gk_ref, mark_ref, grad, q_in, k_in, gq, gk, in_sem, out_sem = refs
    local = q_in.shape[0] // LANES
    per_device = grads[0].shape[0]
    owners = len(grads)
    mark_ref[...] = jnp.zeros_like(mark_ref)
    copies, sends = [], []
    for i in range(local):
        here = pl.ds(i * LANES, LANES)
        row = [
            pltpu.make_async_copy(q_ref.at[0, here], q_in.at[here], in_sem.at[i, owners]),
            pltpu.make_async_copy(k_ref.at[0, here], k_in.at[here], in_sem.at[i, owners + 1]),
        ]
        for k, source in enumerate(grads):
            first = jnp.bitwise_xor(pos_ref[0], k) * per_device
            row.append(
                pltpu.make_async_copy(
                    source.at[:, i % 2, i // 2], grad.at[i, pl.ds(first, per_device)], in_sem.at[i, k]
                )
            )
        copies.append(row)
    for row in copies:
        for copy in row:
            copy.start()
    for i in range(local):
        for copy in copies[i]:
            copy.wait()
        here = pl.ds(i * LANES, LANES)
        rows = slice(i * LANES, (i + 1) * LANES)
        value = grad[i].reshape(q_in.shape[1], LANES).T.astype(F32)
        gq[rows] = (value * k_in[rows].astype(F32)).astype(BF16)
        gk[rows] = (value * q_in[rows].astype(F32)).astype(BF16)
        for n, (source, target) in enumerate(((gq, gq_ref), (gk, gk_ref))):
            send = pltpu.make_async_copy(source.at[here], target.at[0, here], out_sem.at[i, n])
            send.start()
            sends.append(send)
    for send in sends:
        send.wait()


def clip_kernel(pos_ref, total_ref, *refs, threshold):
    *parts, _, out_ref, stage = refs
    per_device, each = stage.shape[1:3]
    for k, part in enumerate(parts):
        stage[jnp.bitwise_xor(pos_ref[0], k)] = part[...]
    total = jnp.sum(total_ref[...], axis=(0, 1, 2), keepdims=True)[0]
    factor = jnp.minimum(1.0, threshold / jnp.sqrt(total + 1e-06))
    for owner in range(stage.shape[0]):
        for n in range(each):
            rows = slice(owner * per_device, (owner + 1) * per_device)
            out_ref[rows, n * LANES : (n + 1) * LANES] = stage[owner, :, n] * factor


def spread_rows(pos_ref, sources, f, target):
    for k, source in enumerate(sources):
        count = source.shape[2] * GROUP
        at = pl.multiple_of(jnp.bitwise_xor(pos_ref[0], k) * count, count)
        for half in range(2):
            target[half, pl.ds(at, count)] = source[f, half].reshape(count, LANES)


def reverse_taps(owner, filt_ref, taps):
    per_device, blocks = taps.shape[0], taps.shape[1] - 1
    groups = filt_ref.shape[0]
    picks = max(per_device, 8)
    row_id = lax.broadcasted_iota(jnp.int32, (picks, groups), 0)
    col_id = lax.broadcasted_iota(jnp.int32, (picks, groups), 1)
    pick = (col_id == row_id + owner * per_device).astype(BF16)
    width = min((blocks + 1) * LANES, filt_ref.shape[1])
    mine = jnp.dot(pick, filt_ref[:, :width], preferred_element_type=F32).astype(BF16)
    empty = jnp.zeros((picks, LANES), BF16)
    mine = jnp.concatenate([empty, mine, empty], axis=1)
    row_id = lax.broadcasted_iota(jnp.int32, (2 * LANES, LANES), 0)
    col_id = lax.broadcasted_iota(jnp.int32, (2 * LANES, LANES), 1)
    flip = (row_id + col_id == LANES).astype(BF16)
    for block in range(blocks + 1):
        near = mine[:, block * LANES : (block + 2) * LANES]
        back = jnp.dot(near, flip, preferred_element_type=F32)
        for f in range(per_device):
            taps[f, block] = back[f : f + 1]


def build_blocks(taps, f, toep):
    row_id = lax.broadcasted_iota(jnp.int32, (LANES, LANES), 0)
    col_id = lax.broadcasted_iota(jnp.int32, (LANES, LANES), 1)
    upper = col_id >= row_id
    before = None
    for block in range(taps.shape[1]):
        tap = jnp.broadcast_to(taps[f, block], (LANES, LANES))
        rolled = pltpu.roll(tap, 0, 1, stride=1, stride_axis=0)
        if block:
            toep[block] = jnp.where(upper, before, rolled).astype(BF16)
        before = rolled


def weights(toep, pair):
    at = 2 * pair + 1
    top = jnp.concatenate([toep[at], toep[at - 1]], axis=1)
    low = jnp.concatenate([toep[at + 1], toep[at]], axis=1)
    return jnp.concatenate([top, low], axis=0)


def blocks_kernel(pos_ref, filt_ref, *refs):
    *toeps, taps = refs
    unroll = len(toeps)
    reverse_taps(pos_ref[0], filt_ref, taps)

    def some(i, carry):
        for u in range(unroll):
            toep = toeps[u].at[i]
            toep[0] = jnp.zeros((LANES, LANES), BF16)
            build_blocks(taps, i * unroll + u, toep)
        return carry

    lax.fori_loop(0, toeps[0].shape[0], some, 0)


def conv_kernel(pos_ref, *refs, owners, unroll):
    toeps, refs = refs[:unroll], refs[unroll:]
    ins, outs, refs = refs[:owners], refs[owners : 2 * owners], refs[2 * owners :]
    pads, accs = refs[:unroll], refs[unroll:]
    per_device, blocks = ins[0].shape[0], toeps[0].shape[1] - 1
    rows = pads[0].shape[1]

    def one(toep, pad, out):
        acc = jnp.zeros((rows, 2 * LANES), F32)
        for pair in range(blocks // 2):
            start = pair * GROUP
            left = jnp.concatenate([pad[0, start:], pad[1, start:]], axis=1)
            part = jnp.dot(left, weights(toep, pair), preferred_element_type=F32)
            if start:
                part = jnp.concatenate([part, jnp.zeros((start, 2 * LANES), F32)], axis=0)
            acc = acc + part
        for half in range(2):
            out[half] = acc[:, half * LANES : (half + 1) * LANES].astype(BF16)

    def some(i, carry):
        for u in range(unroll):
            spread_rows(pos_ref, ins, i * unroll + u, pads[u])
        for u in range(unroll):
            one(toeps[u].at[i], pads[u], accs[u])
        for u in range(unroll):
            for k, target in enumerate(outs):
                count = target.shape[2] * GROUP
                at = pl.multiple_of(jnp.bitwise_xor(pos_ref[0], k) * count, count)
                for half in range(2):
                    value = accs[u][half, pl.ds(at, count)]
                    target[i * unroll + u, half] = value.reshape(target.shape[2:])
        return carry

    lax.fori_loop(0, per_device // unroll, some, 0)


def lag_sums(pad, flipped, rows, blocks):
    row_id = lax.broadcasted_iota(jnp.int32, (LANES, LANES), 0)
    col_id = lax.broadcasted_iota(jnp.int32, (LANES, LANES), 1)
    wraps = col_id <= row_id
    prod = jnp.concatenate([flipped[half, :rows].T for half in range(2)], axis=1)
    after = jnp.zeros((LANES, LANES), F32)
    sums = {}
    for pair in reversed(range(blocks // 2)):
        start = pair * GROUP
        here, later = slice(start, start + rows), slice(start + GROUP, start + GROUP + rows)
        even = jnp.concatenate([pad[0, here], pad[1, here]], axis=0)
        odd = jnp.concatenate([pad[1, here], pad[0, later]], axis=0)
        both = jnp.dot(prod, jnp.concatenate([even, odd], axis=1), preferred_element_type=F32)
        for half in (1, 0):
            rolled = pltpu.roll(
                both[:, half * LANES : (half + 1) * LANES], 1, 1, stride=1, stride_axis=0
            )
            part = jnp.where(wraps, rolled, after)
            sums[2 * pair + half] = jnp.sum(part, axis=0, keepdims=True)
            after = rolled
    return sums


def lag_kernel(pos_ref, *refs, owners, unroll, scale, first, last):
    grads, prods, refs = refs[:owners], refs[owners : 2 * owners], refs[2 * owners :]
    olds, refs = (refs[: owners + 1], refs[owners + 1 :]) if first else ([], refs[1:])
    raws, sum_ref, refs = refs[:owners], refs[owners], refs[owners + 1 :]
    pads, flips, lags_v, sq_v = refs[:unroll], refs[unroll : 2 * unroll], refs[-2], refs[-1]
    per_owner = raws[0].shape[1]
    blocks = owners * per_owner
    rows = flips[0].shape[1]
    for pad in pads:
        pad[:, rows:] = jnp.zeros((2, rows, LANES), BF16)
    sq_v[...] = olds[-1][...] if olds else jnp.zeros_like(sq_v)

    def one(slot, pad, flipped):
        sums = lag_sums(pad, flipped, rows, blocks)
        for owner in range(owners):
            lags = jnp.concatenate(
                [sums[owner * per_owner + n] for n in range(per_owner)], axis=0
            ) * scale
            lags_v[slot, owner] = lags
            sq_v[...] += lags * lags

    def some(i, carry):
        for u in range(unroll):
            spread_rows(pos_ref, grads, first + i * unroll + u, pads[u])
            spread_rows(pos_ref, prods, i * unroll + u, flips[u])
        for u in range(unroll):
            one(u, pads[u], flips[u])
        for u in range(unroll):
            for k, target in enumerate(raws):
                target[first + i * unroll + u] = lags_v[u, jnp.bitwise_xor(pos_ref[0], k)]
        return carry

    lax.fori_loop(0, prods[0].shape[0] // unroll, some, 0)
    if not last:
        sum_ref[...] = sq_v[...]
        return
    squares = jnp.sum(sq_v[...], axis=0, keepdims=True)
    sum_ref[...] = jnp.zeros_like(sum_ref)
    sum_ref[:, :1] = jnp.broadcast_to(squares[None], (sum_ref.shape[0], 1, LANES))


def cost(flops, moved):
    return pl.CostEstimate(flops=int(flops), bytes_accessed=int(moved), transcendentals=0)


def on_device(q_branch, k_branch, out_gate, filters, grad_out):
    seqs, block_len, chans = q_branch.shape
    owners = lax.axis_size("ctx")
    groups = chans // GROUP
    per_device = groups // owners
    local = block_len // LANES
    length = owners * block_len
    blocks = length // LANES
    rows = length * GROUP // (2 * LANES)
    scale = 4.0 / math.sqrt(seqs * GROUP)
    size = block_len * chans * 2
    anywhere = pl.BlockSpec(memory_space=pl.ANY)
    vmem = pl.BlockSpec(memory_space=pltpu.VMEM)
    smem = pl.BlockSpec(memory_space=pltpu.SMEM)
    tail = (2, local // 2, GROUP, LANES)
    whole = (owners, per_device) + tail
    pos = lax.axis_index("ctx").astype(jnp.int32).reshape(1)
    piece = jax.ShapeDtypeStruct((per_device,) + tail, BF16)
    lag_piece = jax.ShapeDtypeStruct((per_device, blocks // owners, LANES), F32)

    def gate(left, right, after, reverse, sizes, limit, name, window="all", peers=None):
        peers = peers or tuple(range(owners))
        wide = chans if window == "all" else chans // 2
        parts = [jax.ShapeDtypeStruct((n,) + tail, BF16) for n in sizes]
        out = pl.pallas_call(
            functools.partial(
                gate_kernel,
                reverse=reverse,
                sizes=sizes,
                ordered=len(after),
                window=window,
                peers=peers,
            ),
            in_specs=[smem] + [pl.BlockSpec(memory_space=pltpu.HBM)] * 2 + [vmem] * len(after),
            out_specs=[anywhere] * (len(peers) * len(sizes)),
            out_shape=parts * len(peers),
            scratch_shapes=[
                pltpu.VMEM((block_len, wide), BF16),
                pltpu.VMEM((block_len, wide), BF16),
                pltpu.VMEM((2, local // 2, wide // GROUP, GROUP, LANES), BF16),
                pltpu.SemaphoreType.DMA((local, 2)),
                pltpu.SemaphoreType.DMA((local, len(peers) * len(sizes))),
            ],
            cost_estimate=cost(block_len * wide, 6 * block_len * wide),
            compiler_params=pltpu.CompilerParams(vmem_limit_bytes=limit << 20),
            name=name,
        )(pos, left, right, *after)
        return [out[n :: len(sizes)] for n in range(len(sizes))]

    def swap(values):
        out = [values[0]]
        for k in range(1, owners):
            out.append(lax.ppermute(values[k], "ctx", [(i, i ^ k) for i in range(owners)]))
        return out

    sizes = (8, 8) if per_device == 16 else (per_device,)
    if owners == 4:
        (far,) = gate(
            *(pltpu.with_memory_space_constraint(v, pltpu.HBM) for v in (grad_out, out_gate)),
            (), False, (per_device,), 12, "gate_far", "far", (2, 3)
        )
        far_send = far
        far = [lax.ppermute(v, "ctx", [(i, i ^ k) for i in range(4)]) for k, v in zip((2, 3), far)]
        prod_send = gate(q_branch, k_branch, (), True, sizes, 12, "gate_prod")
        (near,) = gate(
            grad_out, out_gate, prod_send[0][:1], False, (per_device,), 12, "gate_near", "near", (0, 1)
        )
        grad_got = [near[0], lax.ppermute(near[1], "ctx", [(i, i ^ 1) for i in range(4)]), *far]
    else:
        (grad_send,) = gate(grad_out, out_gate, (), False, (per_device,), 56, "gate_grad")
        grad_got = swap(grad_send)
        prod_send = gate(q_branch, k_branch, grad_send[:1], True, sizes, 12, "gate_prod")
    prod_got = []
    for part in prod_send:
        if prod_got:
            part, prod_got[-1][1] = lax.optimization_barrier((part, prod_got[-1][1]))
        prod_got.append(swap(part))
    unroll = math.gcd(4, per_device)
    toeps = pl.pallas_call(
        blocks_kernel,
        in_specs=[smem, vmem],
        out_specs=[vmem] * unroll,
        out_shape=[
            jax.ShapeDtypeStruct((per_device // unroll, blocks + 1, LANES, LANES), BF16)
        ] * unroll,
        scratch_shapes=[pltpu.VMEM((per_device, blocks + 1, 1, LANES), F32)],
        cost_estimate=cost(1, 1),
        compiler_params=pltpu.CompilerParams(vmem_limit_bytes=16 << 20),
        name="blocks",
    )(pos, filters)
    conv = pl.pallas_call(
        functools.partial(conv_kernel, owners=owners, unroll=unroll),
        in_specs=[smem] + [vmem] * (unroll + owners),
        out_specs=[vmem] * owners,
        out_shape=[piece] * owners,
        scratch_shapes=[pltpu.VMEM((2, rows, LANES), BF16)] * (2 * unroll),
        cost_estimate=cost(per_device * rows * length * 4096, 2 * size + groups * length * 2),
        compiler_params=pltpu.CompilerParams(vmem_limit_bytes=16 << 20),
        name="conv",
    )(pos, *toeps, *grad_got)
    back = swap(conv)
    both = ("ctx", "ch")
    count = lax.axis_size(both)
    old = [conv[0]]
    for n, each in enumerate(sizes):
        last = n == len(sizes) - 1
        unroll = math.gcd(8, each)
        sums = jax.ShapeDtypeStruct((count, 4, LANES) if last else (blocks // owners, LANES), F32)
        old = pl.pallas_call(
            functools.partial(
                lag_kernel, owners=owners, unroll=unroll, scale=scale, first=sum(sizes[:n]), last=last
            ),
            in_specs=[smem] + [vmem] * (2 * owners) + ([vmem] * (owners + 1) if n else [anywhere]),
            out_specs=[vmem] * (owners + 1),
            out_shape=[lag_piece] * owners + [sums],
            input_output_aliases={2 * owners + 1 + k: k for k in range(owners)} if n else {},
            scratch_shapes=[pltpu.VMEM((2, 2 * rows, LANES), BF16)] * unroll
            + [pltpu.VMEM((2, rows, LANES), BF16)] * unroll
            + [
                pltpu.VMEM((unroll, owners, blocks // owners, LANES), F32),
                pltpu.VMEM((blocks // owners, LANES), F32),
            ],
            cost_estimate=cost(each * 2 * rows * length * 2048, 2 * size),
            compiler_params=pltpu.CompilerParams(vmem_limit_bytes=16 << 20),
            name="lags",
        )(pos, *grad_got, *prod_got[n], *old)
    *raw, spread = old
    total = lax.all_to_all(spread, both, 0, 0, tiled=True)
    raw = swap(raw)
    threshold = math.sqrt(WIDTH // GROUP * length)
    grad_q, grad_k, mark = pl.pallas_call(
        ungate_kernel,
        in_specs=[smem] + [anywhere] * (2 + owners),
        out_specs=[anywhere] * 2 + [vmem],
        out_shape=[jax.ShapeDtypeStruct(q_branch.shape, BF16)] * 2
        + [jax.ShapeDtypeStruct((8, LANES), F32)],
        scratch_shapes=[
            pltpu.VMEM((local, groups, GROUP, LANES), BF16),
            pltpu.VMEM((block_len, chans), BF16),
            pltpu.VMEM((block_len, chans), BF16),
            pltpu.VMEM((block_len, chans), BF16),
            pltpu.VMEM((block_len, chans), BF16),
            pltpu.SemaphoreType.DMA((local, owners + 2)),
            pltpu.SemaphoreType.DMA((local, 2)),
        ],
        cost_estimate=cost(2 * block_len * chans, 5 * size),
        compiler_params=pltpu.CompilerParams(vmem_limit_bytes=16 << 20),
        name="ungate",
    )(pos, q_branch, k_branch, *back)
    grad_filters = pl.pallas_call(
        functools.partial(clip_kernel, threshold=threshold),
        in_specs=[smem] + [vmem] * (2 + owners),
        out_specs=vmem,
        out_shape=jax.ShapeDtypeStruct((groups, length // owners), F32),
        scratch_shapes=[pltpu.VMEM((owners, per_device, blocks // owners, LANES), F32)],
        cost_estimate=cost(groups * length, groups * length * 4),
        compiler_params=pltpu.CompilerParams(vmem_limit_bytes=8 << 20),
        name="clip",
    )(pos, total, *raw, mark)
    return (grad_q, grad_k, grad_filters)


def solution(mesh):
    return jax.shard_map(
        on_device,
        mesh=mesh,
        in_specs=(
            P(None, "ctx", "ch"),
            P(None, "ctx", "ch"),
            P(None, "ctx", "ch"),
            P("ch", None),
            P(None, "ctx", "ch"),
        ),
        out_specs=(P(None, "ctx", "ch"), P(None, "ctx", "ch"), P("ch", "ctx")),
        check_vma=False,
    )
```

```python
import functools
import math

import jax
import jax.numpy as jnp
from jax import lax
from jax.experimental import pallas as pl
from jax.experimental.pallas import tpu as pltpu
from jax.sharding import PartitionSpec as P

WIDTH = 8192
GROUP = 16
LANES = 128
NT = (((1,), (1,)), ((), ()))
BF16, F32 = jnp.bfloat16, jnp.float32


def gate_kernel(pos_ref, left_ref, right_ref, *refs, reverse, sizes, ordered, window, peers):
    *outs, left, right, out, in_sem, out_sem = refs[ordered:]
    local, wide = left.shape[0] // LANES, left.shape[1]
    chip = jnp.right_shift(pos_ref[0], 1)
    start = {"all": 0, "far": (1 - chip) * wide, "near": chip * wide}[window]
    there = pl.ds(start if window == "all" else pl.multiple_of(start, wide), wide)
    per_device = sum(sizes)
    copies = []
    for i in range(local):
        here = pl.ds(i * LANES, LANES)
        copies.append(
            (
                pltpu.make_async_copy(left_ref.at[0, here, there], left.at[here], in_sem.at[i, 0]),
                pltpu.make_async_copy(right_ref.at[0, here, there], right.at[here], in_sem.at[i, 1]),
            )
        )
    for pair in copies:
        for copy in pair:
            copy.start()
    sends = []
    for i in range(local):
        for copy in copies[i]:
            copy.wait()
        rows = slice(i * LANES, (i + 1) * LANES)
        value = (left[rows].astype(F32) * right[rows].astype(F32)).astype(BF16)
        if reverse:
            row_id = lax.broadcasted_iota(jnp.int32, (LANES, LANES), 0)
            col_id = lax.broadcasted_iota(jnp.int32, (LANES, LANES), 1)
            flip = (row_id + col_id == LANES - 1).astype(BF16)
            value = jnp.dot(flip, value, preferred_element_type=F32).astype(BF16)
        value = value.T
        out[i % 2, i // 2] = value.reshape(out.shape[2:])
        for n, target in enumerate(outs):
            k, chunk = divmod(n, len(sizes))
            first = jnp.bitwise_xor(pos_ref[0], peers[k]) * per_device - start // GROUP + sum(sizes[:chunk])
            send = pltpu.make_async_copy(
                out.at[i % 2, i // 2, pl.ds(first, sizes[chunk])],
                target.at[:, i % 2, i // 2],
                out_sem.at[i, n],
            )
            send.start()
            sends.append(send)
    for send in sends:
        send.wait()


def ungate_kernel(pos_ref, q_ref, k_ref, *refs):
    *grads, gq_ref, gk_ref, mark_ref, grad, q_in, k_in, gq, gk, in_sem, out_sem = refs
    local = q_in.shape[0] // LANES
    per_device = grads[0].shape[0]
    owners = len(grads)
    mark_ref[...] = jnp.zeros_like(mark_ref)
    copies, sends = [], []
    for i in range(local):
        here = pl.ds(i * LANES, LANES)
        row = [
            pltpu.make_async_copy(q_ref.at[0, here], q_in.at[here], in_sem.at[i, owners]),
            pltpu.make_async_copy(k_ref.at[0, here], k_in.at[here], in_sem.at[i, owners + 1]),
        ]
        for k, source in enumerate(grads):
            first = jnp.bitwise_xor(pos_ref[0], k) * per_device
            row.append(
                pltpu.make_async_copy(
                    source.at[:, i % 2, i // 2], grad.at[i, pl.ds(first, per_device)], in_sem.at[i, k]
                )
            )
        copies.append(row)
    for row in copies:
        for copy in row:
            copy.start()
    for i in range(local):
        for copy in copies[i]:
            copy.wait()
        here = pl.ds(i * LANES, LANES)
        rows = slice(i * LANES, (i + 1) * LANES)
        value = grad[i].reshape(q_in.shape[1], LANES).T.astype(F32)
        gq[rows] = (value * k_in[rows].astype(F32)).astype(BF16)
        gk[rows] = (value * q_in[rows].astype(F32)).astype(BF16)
        for n, (source, target) in enumerate(((gq, gq_ref), (gk, gk_ref))):
            send = pltpu.make_async_copy(source.at[here], target.at[0, here], out_sem.at[i, n])
            send.start()
            sends.append(send)
    for send in sends:
        send.wait()


def clip_kernel(pos_ref, total_ref, *refs, threshold):
    *parts, _, out_ref, stage = refs
    per_device, each = stage.shape[1:3]
    for k, part in enumerate(parts):
        stage[jnp.bitwise_xor(pos_ref[0], k)] = part[...]
    total = jnp.sum(total_ref[...], axis=(0, 1, 2), keepdims=True)[0]
    factor = jnp.minimum(1.0, threshold / jnp.sqrt(total + 1e-06))
    for owner in range(stage.shape[0]):
        for n in range(each):
            rows = slice(owner * per_device, (owner + 1) * per_device)
            out_ref[rows, n * LANES : (n + 1) * LANES] = stage[owner, :, n] * factor


def spread_rows(pos_ref, sources, f, target):
    for k, source in enumerate(sources):
        count = source.shape[2] * GROUP
        at = pl.multiple_of(jnp.bitwise_xor(pos_ref[0], k) * count, count)
        for half in range(2):
            target[half, pl.ds(at, count)] = source[f, half].reshape(count, LANES)


def reverse_taps(owner, filt_ref, taps):
    per_device, blocks = taps.shape[0], taps.shape[1] - 1
    groups = filt_ref.shape[0]
    picks = max(per_device, 8)
    row_id = lax.broadcasted_iota(jnp.int32, (picks, groups), 0)
    col_id = lax.broadcasted_iota(jnp.int32, (picks, groups), 1)
    pick = (col_id == row_id + owner * per_device).astype(BF16)
    width = min((blocks + 1) * LANES, filt_ref.shape[1])
    mine = jnp.dot(pick, filt_ref[:, :width], preferred_element_type=F32).astype(BF16)
    empty = jnp.zeros((picks, LANES), BF16)
    mine = jnp.concatenate([empty, mine, empty], axis=1)
    row_id = lax.broadcasted_iota(jnp.int32, (2 * LANES, LANES), 0)
    col_id = lax.broadcasted_iota(jnp.int32, (2 * LANES, LANES), 1)
    flip = (row_id + col_id == LANES).astype(BF16)
    for block in range(blocks + 1):
        near = mine[:, block * LANES : (block + 2) * LANES]
        back = jnp.dot(near, flip, preferred_element_type=F32)
        for f in range(per_device):
            taps[f, block] = back[f : f + 1]


def build_blocks(taps, f, toep):
    row_id = lax.broadcasted_iota(jnp.int32, (LANES, LANES), 0)
    col_id = lax.broadcasted_iota(jnp.int32, (LANES, LANES), 1)
    upper = col_id >= row_id
    before = None
    for block in range(taps.shape[1]):
        tap = jnp.broadcast_to(taps[f, block], (LANES, LANES))
        rolled = pltpu.roll(tap, 0, 1, stride=1, stride_axis=0)
        if block:
            toep[block] = jnp.where(upper, before, rolled).astype(BF16)
        before = rolled


def weights(toep, pair):
    at = 2 * pair + 1
    top = jnp.concatenate([toep[at], toep[at - 1]], axis=1)
    low = jnp.concatenate([toep[at + 1], toep[at]], axis=1)
    return jnp.concatenate([top, low], axis=0)


def blocks_kernel(pos_ref, filt_ref, *refs):
    *toeps, taps = refs
    unroll = len(toeps)
    reverse_taps(pos_ref[0], filt_ref, taps)

    def some(i, carry):
        for u in range(unroll):
            toep = toeps[u].at[i]
            toep[0] = jnp.zeros((LANES, LANES), BF16)
            build_blocks(taps, i * unroll + u, toep)
        return carry

    lax.fori_loop(0, toeps[0].shape[0], some, 0)


def conv_kernel(pos_ref, *refs, owners, unroll):
    toeps, refs = refs[:unroll], refs[unroll:]
    ins, outs, refs = refs[:owners], refs[owners : 2 * owners], refs[2 * owners :]
    pads, accs = refs[:unroll], refs[unroll:]
    per_device, blocks = ins[0].shape[0], toeps[0].shape[1] - 1
    rows = pads[0].shape[1]

    def one(toep, pad, out):
        acc = jnp.zeros((rows, 2 * LANES), F32)
        for pair in range(blocks // 2):
            start = pair * GROUP
            left = jnp.concatenate([pad[0, start:], pad[1, start:]], axis=1)
            part = jnp.dot(left, weights(toep, pair), preferred_element_type=F32)
            if start:
                part = jnp.concatenate([part, jnp.zeros((start, 2 * LANES), F32)], axis=0)
            acc = acc + part
        for half in range(2):
            out[half] = acc[:, half * LANES : (half + 1) * LANES].astype(BF16)

    def some(i, carry):
        for u in range(unroll):
            spread_rows(pos_ref, ins, i * unroll + u, pads[u])
        for u in range(unroll):
            one(toeps[u].at[i], pads[u], accs[u])
        for u in range(unroll):
            for k, target in enumerate(outs):
                count = target.shape[2] * GROUP
                at = pl.multiple_of(jnp.bitwise_xor(pos_ref[0], k) * count, count)
                for half in range(2):
                    value = accs[u][half, pl.ds(at, count)]
                    target[i * unroll + u, half] = value.reshape(target.shape[2:])
        return carry

    lax.fori_loop(0, per_device // unroll, some, 0)


def lag_sums(pad, flipped, rows, blocks):
    row_id = lax.broadcasted_iota(jnp.int32, (LANES, LANES), 0)
    col_id = lax.broadcasted_iota(jnp.int32, (LANES, LANES), 1)
    wraps = col_id <= row_id
    prod = jnp.concatenate([flipped[half, :rows].T for half in range(2)], axis=1)
    after = jnp.zeros((LANES, LANES), F32)
    sums = {}
    for pair in reversed(range(blocks // 2)):
        start = pair * GROUP
        here, later = slice(start, start + rows), slice(start + GROUP, start + GROUP + rows)
        even = jnp.concatenate([pad[0, here], pad[1, here]], axis=0)
        odd = jnp.concatenate([pad[1, here], pad[0, later]], axis=0)
        both = jnp.dot(prod, jnp.concatenate([even, odd], axis=1), preferred_element_type=F32)
        for half in (1, 0):
            rolled = pltpu.roll(
                both[:, half * LANES : (half + 1) * LANES], 1, 1, stride=1, stride_axis=0
            )
            part = jnp.where(wraps, rolled, after)
            sums[2 * pair + half] = jnp.sum(part, axis=0, keepdims=True)
            after = rolled
    return sums


def lag_kernel(pos_ref, *refs, owners, unroll, scale, first, last):
    grads, prods, refs = refs[:owners], refs[owners : 2 * owners], refs[2 * owners :]
    olds, refs = (refs[: owners + 1], refs[owners + 1 :]) if first else ([], refs[1:])
    raws, sum_ref, refs = refs[:owners], refs[owners], refs[owners + 1 :]
    pads, flips, lags_v, sq_v = refs[:unroll], refs[unroll : 2 * unroll], refs[-2], refs[-1]
    per_owner = raws[0].shape[1]
    blocks = owners * per_owner
    rows = flips[0].shape[1]
    for pad in pads:
        pad[:, rows:] = jnp.zeros((2, rows, LANES), BF16)
    sq_v[...] = olds[-1][...] if olds else jnp.zeros_like(sq_v)

    def one(slot, pad, flipped):
        sums = lag_sums(pad, flipped, rows, blocks)
        for owner in range(owners):
            lags = jnp.concatenate(
                [sums[owner * per_owner + n] for n in range(per_owner)], axis=0
            ) * scale
            lags_v[slot, owner] = lags
            sq_v[...] += lags * lags

    def some(i, carry):
        for u in range(unroll):
            spread_rows(pos_ref, grads, first + i * unroll + u, pads[u])
            spread_rows(pos_ref, prods, i * unroll + u, flips[u])
        for u in range(unroll):
            one(u, pads[u], flips[u])
        for u in range(unroll):
            for k, target in enumerate(raws):
                target[first + i * unroll + u] = lags_v[u, jnp.bitwise_xor(pos_ref[0], k)]
        return carry

    lax.fori_loop(0, prods[0].shape[0] // unroll, some, 0)
    if not last:
        sum_ref[...] = sq_v[...]
        return
    squares = jnp.sum(sq_v[...], axis=0, keepdims=True)
    sum_ref[...] = jnp.zeros_like(sum_ref)
    sum_ref[:, :1] = jnp.broadcast_to(squares[None], (sum_ref.shape[0], 1, LANES))


def in_hbm(value):
    return pltpu.with_memory_space_constraint(value, pltpu.HBM)


def cost(flops, moved):
    return pl.CostEstimate(flops=int(flops), bytes_accessed=int(moved), transcendentals=0)


def on_device(q_branch, k_branch, out_gate, filters, grad_out):
    seqs, block_len, chans = q_branch.shape
    owners = lax.axis_size("ctx")
    groups = chans // GROUP
    per_device = groups // owners
    local = block_len // LANES
    length = owners * block_len
    blocks = length // LANES
    rows = length * GROUP // (2 * LANES)
    scale = 4.0 / math.sqrt(seqs * GROUP)
    size = block_len * chans * 2
    anywhere = pl.BlockSpec(memory_space=pl.ANY)
    vmem = pl.BlockSpec(memory_space=pltpu.VMEM)
    smem = pl.BlockSpec(memory_space=pltpu.SMEM)
    tail = (2, local // 2, GROUP, LANES)
    whole = (owners, per_device) + tail
    pos = lax.axis_index("ctx").astype(jnp.int32).reshape(1)
    piece = jax.ShapeDtypeStruct((per_device,) + tail, BF16)
    lag_piece = jax.ShapeDtypeStruct((per_device, blocks // owners, LANES), F32)

    def gate(left, right, after, reverse, sizes, limit, name, window="all", peers=None):
        peers = peers or tuple(range(owners))
        wide = chans if window == "all" else chans // 2
        parts = [jax.ShapeDtypeStruct((n,) + tail, BF16) for n in sizes]
        out = pl.pallas_call(
            functools.partial(
                gate_kernel,
                reverse=reverse,
                sizes=sizes,
                ordered=len(after),
                window=window,
                peers=peers,
            ),
            in_specs=[smem] + [pl.BlockSpec(memory_space=pltpu.HBM)] * 2 + [vmem] * len(after),
            out_specs=[anywhere] * (len(peers) * len(sizes)),
            out_shape=parts * len(peers),
            scratch_shapes=[
                pltpu.VMEM((block_len, wide), BF16),
                pltpu.VMEM((block_len, wide), BF16),
                pltpu.VMEM((2, local // 2, wide // GROUP, GROUP, LANES), BF16),
                pltpu.SemaphoreType.DMA((local, 2)),
                pltpu.SemaphoreType.DMA((local, len(peers) * len(sizes))),
            ],
            cost_estimate=cost(block_len * wide, 6 * block_len * wide),
            compiler_params=pltpu.CompilerParams(vmem_limit_bytes=limit << 20),
            name=name,
        )(pos, left, right, *after)
        return [out[n :: len(sizes)] for n in range(len(sizes))]

    def swap(values):
        out = [values[0]]
        for k in range(1, owners):
            out.append(lax.ppermute(values[k], "ctx", [(i, i ^ k) for i in range(owners)]))
        return out

    sizes = (8, 8) if per_device == 16 else (per_device,)
    if owners == 4:
        (far,) = gate(
            in_hbm(grad_out), in_hbm(out_gate), (), False, (per_device,), 12, "gate_far", "far", (2, 3)
        )
        far_send = far
        far = [lax.ppermute(v, "ctx", [(i, i ^ k) for i in range(4)]) for k, v in zip((2, 3), far)]
        prod_send = gate(in_hbm(q_branch), in_hbm(k_branch), (), True, sizes, 12, "gate_prod")
        (near,) = gate(
            grad_out, out_gate, prod_send[0][:1], False, (per_device,), 12, "gate_near", "near", (0, 1)
        )
        grad_got = [near[0], lax.ppermute(near[1], "ctx", [(i, i ^ 1) for i in range(4)]), *far]
    else:
        (grad_send,) = gate(grad_out, out_gate, (), False, (per_device,), 56, "gate_grad")
        grad_got = swap(grad_send)
        prod_send = gate(q_branch, k_branch, grad_send[:1], True, sizes, 12, "gate_prod")
    prod_got = []
    for part in prod_send:
        if prod_got:
            part, prod_got[-1][1] = lax.optimization_barrier((part, prod_got[-1][1]))
        prod_got.append(swap(part))
    unroll = math.gcd(4, per_device)
    toeps = pl.pallas_call(
        blocks_kernel,
        in_specs=[smem, vmem],
        out_specs=[vmem] * unroll,
        out_shape=[
            jax.ShapeDtypeStruct((per_device // unroll, blocks + 1, LANES, LANES), BF16)
        ] * unroll,
        scratch_shapes=[pltpu.VMEM((per_device, blocks + 1, 1, LANES), F32)],
        cost_estimate=cost(1, 1),
        compiler_params=pltpu.CompilerParams(vmem_limit_bytes=16 << 20),
        name="blocks",
    )(pos, filters)
    conv = pl.pallas_call(
        functools.partial(conv_kernel, owners=owners, unroll=unroll),
        in_specs=[smem] + [vmem] * (unroll + owners),
        out_specs=[vmem] * owners,
        out_shape=[piece] * owners,
        scratch_shapes=[pltpu.VMEM((2, rows, LANES), BF16)] * (2 * unroll),
        cost_estimate=cost(per_device * rows * length * 4096, 2 * size + groups * length * 2),
        compiler_params=pltpu.CompilerParams(vmem_limit_bytes=16 << 20),
        name="conv",
    )(pos, *toeps, *grad_got)
    back = swap(conv)
    both = ("ctx", "ch")
    count = lax.axis_size(both)
    old = [conv[0]]
    for n, each in enumerate(sizes):
        last = n == len(sizes) - 1
        unroll = math.gcd(8, each)
        sums = jax.ShapeDtypeStruct((count, 4, LANES) if last else (blocks // owners, LANES), F32)
        old = pl.pallas_call(
            functools.partial(
                lag_kernel, owners=owners, unroll=unroll, scale=scale, first=sum(sizes[:n]), last=last
            ),
            in_specs=[smem] + [vmem] * (2 * owners) + ([vmem] * (owners + 1) if n else [anywhere]),
            out_specs=[vmem] * (owners + 1),
            out_shape=[lag_piece] * owners + [sums],
            input_output_aliases={2 * owners + 1 + k: k for k in range(owners)} if n else {},
            scratch_shapes=[pltpu.VMEM((2, 2 * rows, LANES), BF16)] * unroll
            + [pltpu.VMEM((2, rows, LANES), BF16)] * unroll
            + [
                pltpu.VMEM((unroll, owners, blocks // owners, LANES), F32),
                pltpu.VMEM((blocks // owners, LANES), F32),
            ],
            cost_estimate=cost(each * 2 * rows * length * 2048, 2 * size),
            compiler_params=pltpu.CompilerParams(vmem_limit_bytes=16 << 20),
            name="lags",
        )(pos, *grad_got, *prod_got[n], *old)
    *raw, spread = old
    total = lax.all_to_all(spread, both, 0, 0, tiled=True)
    raw = swap(raw)
    threshold = math.sqrt(WIDTH // GROUP * length)
    grad_q, grad_k, mark = pl.pallas_call(
        ungate_kernel,
        in_specs=[smem] + [anywhere] * (2 + owners),
        out_specs=[anywhere] * 2 + [vmem],
        out_shape=[jax.ShapeDtypeStruct(q_branch.shape, BF16)] * 2
        + [jax.ShapeDtypeStruct((8, LANES), F32)],
        scratch_shapes=[
            pltpu.VMEM((local, groups, GROUP, LANES), BF16),
            pltpu.VMEM((block_len, chans), BF16),
            pltpu.VMEM((block_len, chans), BF16),
            pltpu.VMEM((block_len, chans), BF16),
            pltpu.VMEM((block_len, chans), BF16),
            pltpu.SemaphoreType.DMA((local, owners + 2)),
            pltpu.SemaphoreType.DMA((local, 2)),
        ],
        cost_estimate=cost(2 * block_len * chans, 5 * size),
        compiler_params=pltpu.CompilerParams(vmem_limit_bytes=16 << 20),
        name="ungate",
    )(pos, q_branch, k_branch, *back)
    grad_filters = pl.pallas_call(
        functools.partial(clip_kernel, threshold=threshold),
        in_specs=[smem] + [vmem] * (2 + owners),
        out_specs=vmem,
        out_shape=jax.ShapeDtypeStruct((groups, length // owners), F32),
        scratch_shapes=[pltpu.VMEM((owners, per_device, blocks // owners, LANES), F32)],
        cost_estimate=cost(groups * length, groups * length * 4),
        compiler_params=pltpu.CompilerParams(vmem_limit_bytes=8 << 20),
        name="clip",
    )(pos, total, *raw, mark)
    return (grad_q, grad_k, grad_filters)


def solution(mesh):
    return jax.shard_map(
        on_device,
        mesh=mesh,
        in_specs=(
            P(None, "ctx", "ch"),
            P(None, "ctx", "ch"),
            P(None, "ctx", "ch"),
            P("ch", None),
            P(None, "ctx", "ch"),
        ),
        out_specs=(P(None, "ctx", "ch"), P(None, "ctx", "ch"), P("ch", "ctx")),
        check_vma=False,
    )
```

```python
import functools
import math

import jax
import jax.numpy as jnp
from jax import lax
from jax.experimental import pallas as pl
from jax.experimental.pallas import tpu as pltpu
from jax.sharding import PartitionSpec as P

WIDTH = 8192
GROUP = 16
LANES = 128
NT = (((1,), (1,)), ((), ()))
BF16, F32 = jnp.bfloat16, jnp.float32


def gate_kernel(pos_ref, left_ref, right_ref, *refs, reverse, sizes, ordered, window, peers):
    *outs, left, right, out, in_sem, out_sem = refs[ordered:]
    local, wide = left.shape[0] // LANES, left.shape[1]
    chip = jnp.right_shift(pos_ref[0], 1)
    start = {"all": 0, "far": (1 - chip) * wide, "near": chip * wide}[window]
    there = pl.ds(start if window == "all" else pl.multiple_of(start, wide), wide)
    per_device = sum(sizes)
    copies = []
    for i in range(local):
        here = pl.ds(i * LANES, LANES)
        copies.append(
            (
                pltpu.make_async_copy(left_ref.at[0, here, there], left.at[here], in_sem.at[i, 0]),
                pltpu.make_async_copy(right_ref.at[0, here, there], right.at[here], in_sem.at[i, 1]),
            )
        )
    for pair in copies:
        for copy in pair:
            copy.start()
    sends = []
    for i in range(local):
        for copy in copies[i]:
            copy.wait()
        rows = slice(i * LANES, (i + 1) * LANES)
        value = (left[rows].astype(F32) * right[rows].astype(F32)).astype(BF16)
        if reverse:
            row_id = lax.broadcasted_iota(jnp.int32, (LANES, LANES), 0)
            col_id = lax.broadcasted_iota(jnp.int32, (LANES, LANES), 1)
            flip = (row_id + col_id == LANES - 1).astype(BF16)
            value = jnp.dot(flip, value, preferred_element_type=F32).astype(BF16)
        value = value.T
        out[i % 2, i // 2] = value.reshape(out.shape[2:])
        for n, target in enumerate(outs):
            k, chunk = divmod(n, len(sizes))
            first = jnp.bitwise_xor(pos_ref[0], peers[k]) * per_device - start // GROUP + sum(sizes[:chunk])
            send = pltpu.make_async_copy(
                out.at[i % 2, i // 2, pl.ds(first, sizes[chunk])],
                target.at[:, i % 2, i // 2],
                out_sem.at[i, n],
            )
            send.start()
            sends.append(send)
    for send in sends:
        send.wait()


def ungate_kernel(pos_ref, q_ref, k_ref, *refs):
    *grads, gq_ref, gk_ref, mark_ref, grad, q_in, k_in, gq, gk, in_sem, out_sem = refs
    local = q_in.shape[0] // LANES
    per_device = grads[0].shape[0]
    owners = len(grads)
    mark_ref[...] = jnp.zeros_like(mark_ref)
    copies, sends = [], []
    for i in range(local):
        here = pl.ds(i * LANES, LANES)
        row = [
            pltpu.make_async_copy(q_ref.at[0, here], q_in.at[here], in_sem.at[i, owners]),
            pltpu.make_async_copy(k_ref.at[0, here], k_in.at[here], in_sem.at[i, owners + 1]),
        ]
        for k, source in enumerate(grads):
            first = jnp.bitwise_xor(pos_ref[0], k) * per_device
            row.append(
                pltpu.make_async_copy(
                    source.at[:, i % 2, i // 2], grad.at[i, pl.ds(first, per_device)], in_sem.at[i, k]
                )
            )
        copies.append(row)
    for row in copies:
        for copy in row:
            copy.start()
    for i in range(local):
        for copy in copies[i]:
            copy.wait()
        here = pl.ds(i * LANES, LANES)
        rows = slice(i * LANES, (i + 1) * LANES)
        value = grad[i].reshape(q_in.shape[1], LANES).T.astype(F32)
        gq[rows] = (value * k_in[rows].astype(F32)).astype(BF16)
        gk[rows] = (value * q_in[rows].astype(F32)).astype(BF16)
        for n, (source, target) in enumerate(((gq, gq_ref), (gk, gk_ref))):
            send = pltpu.make_async_copy(source.at[here], target.at[0, here], out_sem.at[i, n])
            send.start()
            sends.append(send)
    for send in sends:
        send.wait()


def clip_kernel(pos_ref, total_ref, *refs, threshold):
    *parts, _, out_ref, stage = refs
    per_device, each = stage.shape[1:3]
    for k, part in enumerate(parts):
        stage[jnp.bitwise_xor(pos_ref[0], k)] = part[...]
    total = jnp.sum(total_ref[...], axis=(0, 1, 2), keepdims=True)[0]
    factor = jnp.minimum(1.0, threshold / jnp.sqrt(total + 1e-06))
    for owner in range(stage.shape[0]):
        for n in range(each):
            rows = slice(owner * per_device, (owner + 1) * per_device)
            out_ref[rows, n * LANES : (n + 1) * LANES] = stage[owner, :, n] * factor


def spread_rows(pos_ref, sources, f, target):
    for k, source in enumerate(sources):
        count = source.shape[2] * GROUP
        at = pl.multiple_of(jnp.bitwise_xor(pos_ref[0], k) * count, count)
        for half in range(2):
            target[half, pl.ds(at, count)] = source[f, half].reshape(count, LANES)


def reverse_taps(owner, filt_ref, taps):
    per_device, blocks = taps.shape[0], taps.shape[1] - 1
    groups = filt_ref.shape[0]
    picks = max(per_device, 8)
    row_id = lax.broadcasted_iota(jnp.int32, (picks, groups), 0)
    col_id = lax.broadcasted_iota(jnp.int32, (picks, groups), 1)
    pick = (col_id == row_id + owner * per_device).astype(BF16)
    width = min((blocks + 1) * LANES, filt_ref.shape[1])
    mine = jnp.dot(pick, filt_ref[:, :width], preferred_element_type=F32).astype(BF16)
    empty = jnp.zeros((picks, LANES), BF16)
    mine = jnp.concatenate([empty, mine, empty], axis=1)
    row_id = lax.broadcasted_iota(jnp.int32, (2 * LANES, LANES), 0)
    col_id = lax.broadcasted_iota(jnp.int32, (2 * LANES, LANES), 1)
    flip = (row_id + col_id == LANES).astype(BF16)
    for block in range(blocks + 1):
        near = mine[:, block * LANES : (block + 2) * LANES]
        back = jnp.dot(near, flip, preferred_element_type=F32)
        for f in range(per_device):
            taps[f, block] = back[f : f + 1]


def build_blocks(taps, f, toep):
    row_id = lax.broadcasted_iota(jnp.int32, (LANES, LANES), 0)
    col_id = lax.broadcasted_iota(jnp.int32, (LANES, LANES), 1)
    upper = col_id >= row_id
    before = None
    for block in range(taps.shape[1]):
        tap = jnp.broadcast_to(taps[f, block], (LANES, LANES))
        rolled = pltpu.roll(tap, 0, 1, stride=1, stride_axis=0)
        if block:
            toep[block] = jnp.where(upper, before, rolled).astype(BF16)
        before = rolled


def weights(toep, pair):
    at = 2 * pair + 1
    top = jnp.concatenate([toep[at], toep[at - 1]], axis=1)
    low = jnp.concatenate([toep[at + 1], toep[at]], axis=1)
    return jnp.concatenate([top, low], axis=0)


def blocks_kernel(pos_ref, filt_ref, *refs):
    *toeps, taps = refs
    unroll = len(toeps)
    reverse_taps(pos_ref[0], filt_ref, taps)

    def some(i, carry):
        for u in range(unroll):
            toep = toeps[u].at[i]
            toep[0] = jnp.zeros((LANES, LANES), BF16)
            build_blocks(taps, i * unroll + u, toep)
        return carry

    lax.fori_loop(0, toeps[0].shape[0], some, 0)


def conv_kernel(pos_ref, *refs, owners, unroll):
    toeps, refs = refs[:unroll], refs[unroll:]
    ins, outs, refs = refs[:owners], refs[owners : 2 * owners], refs[2 * owners :]
    pads, accs = refs[:unroll], refs[unroll:]
    per_device, blocks = ins[0].shape[0], toeps[0].shape[1] - 1
    rows = pads[0].shape[1]

    def one(toep, pad, out):
        acc = jnp.zeros((rows, 2 * LANES), F32)
        for pair in range(blocks // 2):
            start = pair * GROUP
            left = jnp.concatenate([pad[0, start:], pad[1, start:]], axis=1)
            part = jnp.dot(left, weights(toep, pair), preferred_element_type=F32)
            if start:
                part = jnp.concatenate([part, jnp.zeros((start, 2 * LANES), F32)], axis=0)
            acc = acc + part
        for half in range(2):
            out[half] = acc[:, half * LANES : (half + 1) * LANES].astype(BF16)

    def some(i, carry):
        for u in range(unroll):
            spread_rows(pos_ref, ins, i * unroll + u, pads[u])
        for u in range(unroll):
            one(toeps[u].at[i], pads[u], accs[u])
        for u in range(unroll):
            for k, target in enumerate(outs):
                count = target.shape[2] * GROUP
                at = pl.multiple_of(jnp.bitwise_xor(pos_ref[0], k) * count, count)
                for half in range(2):
                    value = accs[u][half, pl.ds(at, count)]
                    target[i * unroll + u, half] = value.reshape(target.shape[2:])
        return carry

    lax.fori_loop(0, per_device // unroll, some, 0)


def lag_sums(pad, flipped, rows, blocks):
    row_id = lax.broadcasted_iota(jnp.int32, (LANES, LANES), 0)
    col_id = lax.broadcasted_iota(jnp.int32, (LANES, LANES), 1)
    wraps = col_id <= row_id
    prod = jnp.concatenate([flipped[half, :rows].T for half in range(2)], axis=1)
    after = jnp.zeros((LANES, LANES), F32)
    sums = {}
    for pair in reversed(range(blocks // 2)):
        start = pair * GROUP
        here, later = slice(start, start + rows), slice(start + GROUP, start + GROUP + rows)
        even = jnp.concatenate([pad[0, here], pad[1, here]], axis=0)
        odd = jnp.concatenate([pad[1, here], pad[0, later]], axis=0)
        both = jnp.dot(prod, jnp.concatenate([even, odd], axis=1), preferred_element_type=F32)
        for half in (1, 0):
            rolled = pltpu.roll(
                both[:, half * LANES : (half + 1) * LANES], 1, 1, stride=1, stride_axis=0
            )
            part = jnp.where(wraps, rolled, after)
            sums[2 * pair + half] = jnp.sum(part, axis=0, keepdims=True)
            after = rolled
    return sums


def lag_kernel(pos_ref, *refs, owners, unroll, scale, first, last):
    grads, prods, refs = refs[:owners], refs[owners : 2 * owners], refs[2 * owners :]
    olds, refs = (refs[: owners + 1], refs[owners + 1 :]) if first else ([], refs[1:])
    raws, sum_ref, refs = refs[:owners], refs[owners], refs[owners + 1 :]
    pads, flips, lags_v, sq_v = refs[:unroll], refs[unroll : 2 * unroll], refs[-2], refs[-1]
    per_owner = raws[0].shape[1]
    blocks = owners * per_owner
    rows = flips[0].shape[1]
    for pad in pads:
        pad[:, rows:] = jnp.zeros((2, rows, LANES), BF16)
    sq_v[...] = olds[-1][...] if olds else jnp.zeros_like(sq_v)

    def one(slot, pad, flipped):
        sums = lag_sums(pad, flipped, rows, blocks)
        for owner in range(owners):
            lags = jnp.concatenate(
                [sums[owner * per_owner + n] for n in range(per_owner)], axis=0
            ) * scale
            lags_v[slot, owner] = lags
            sq_v[...] += lags * lags

    def some(i, carry):
        for u in range(unroll):
            spread_rows(pos_ref, grads, first + i * unroll + u, pads[u])
            spread_rows(pos_ref, prods, i * unroll + u, flips[u])
        for u in range(unroll):
            one(u, pads[u], flips[u])
        for u in range(unroll):
            for k, target in enumerate(raws):
                target[first + i * unroll + u] = lags_v[u, jnp.bitwise_xor(pos_ref[0], k)]
        return carry

    lax.fori_loop(0, prods[0].shape[0] // unroll, some, 0)
    if not last:
        sum_ref[...] = sq_v[...]
        return
    squares = jnp.sum(sq_v[...], axis=0, keepdims=True)
    sum_ref[...] = jnp.zeros_like(sum_ref)
    sum_ref[:, :1] = jnp.broadcast_to(squares[None], (sum_ref.shape[0], 1, LANES))


def in_hbm(value):
    return pltpu.with_memory_space_constraint(value, pltpu.HBM)


def cost(flops, moved):
    return pl.CostEstimate(flops=int(flops), bytes_accessed=int(moved), transcendentals=0)


def on_device(q_branch, k_branch, out_gate, filters, grad_out):
    seqs, block_len, chans = q_branch.shape
    owners = lax.axis_size("ctx")
    groups = chans // GROUP
    per_device = groups // owners
    local = block_len // LANES
    length = owners * block_len
    blocks = length // LANES
    rows = length * GROUP // (2 * LANES)
    scale = 4.0 / math.sqrt(seqs * GROUP)
    size = block_len * chans * 2
    anywhere = pl.BlockSpec(memory_space=pl.ANY)
    vmem = pl.BlockSpec(memory_space=pltpu.VMEM)
    smem = pl.BlockSpec(memory_space=pltpu.SMEM)
    tail = (2, local // 2, GROUP, LANES)
    whole = (owners, per_device) + tail
    pos = lax.axis_index("ctx").astype(jnp.int32).reshape(1)
    piece = jax.ShapeDtypeStruct((per_device,) + tail, BF16)
    lag_piece = jax.ShapeDtypeStruct((per_device, blocks // owners, LANES), F32)

    def gate(left, right, after, reverse, sizes, limit, name, window="all", peers=None):
        peers = peers or tuple(range(owners))
        wide = chans if window == "all" else chans // 2
        parts = [jax.ShapeDtypeStruct((n,) + tail, BF16) for n in sizes]
        out = pl.pallas_call(
            functools.partial(
                gate_kernel,
                reverse=reverse,
                sizes=sizes,
                ordered=len(after),
                window=window,
                peers=peers,
            ),
            in_specs=[smem] + [pl.BlockSpec(memory_space=pltpu.HBM)] * 2 + [vmem] * len(after),
            out_specs=[anywhere] * (len(peers) * len(sizes)),
            out_shape=parts * len(peers),
            scratch_shapes=[
                pltpu.VMEM((block_len, wide), BF16),
                pltpu.VMEM((block_len, wide), BF16),
                pltpu.VMEM((2, local // 2, wide // GROUP, GROUP, LANES), BF16),
                pltpu.SemaphoreType.DMA((local, 2)),
                pltpu.SemaphoreType.DMA((local, len(peers) * len(sizes))),
            ],
            cost_estimate=cost(block_len * wide, 6 * block_len * wide),
            compiler_params=pltpu.CompilerParams(vmem_limit_bytes=limit << 20),
            name=name,
        )(pos, left, right, *after)
        return [out[n :: len(sizes)] for n in range(len(sizes))]

    def swap(values):
        out = [values[0]]
        for k in range(1, owners):
            out.append(lax.ppermute(values[k], "ctx", [(i, i ^ k) for i in range(owners)]))
        return out

    sizes = (8, 8) if per_device == 16 else (per_device,)
    if owners == 4:
        (far,) = gate(
            in_hbm(grad_out), in_hbm(out_gate), (), False, (per_device,), 12, "gate_far", "far", (2, 3)
        )
        far_send = far
        far = [lax.ppermute(v, "ctx", [(i, i ^ k) for i in range(4)]) for k, v in zip((2, 3), far)]
        prod_send = gate(in_hbm(q_branch), in_hbm(k_branch), (), True, sizes, 12, "gate_prod")
        (near,) = gate(
            grad_out, out_gate, prod_send[0][:1], False, (per_device,), 12, "gate_near", "near", (0, 1)
        )
        grad_got = [near[0], lax.ppermute(near[1], "ctx", [(i, i ^ 1) for i in range(4)]), *far]
    else:
        (grad_send,) = gate(grad_out, out_gate, (), False, (per_device,), 56, "gate_grad")
        grad_got = swap(grad_send)
        prod_send = gate(q_branch, k_branch, grad_send[:1], True, sizes, 12, "gate_prod")
    prod_got = []
    for part in prod_send:
        if prod_got:
            part, grad_got[2] = lax.optimization_barrier((part, grad_got[2]))
        prod_got.append(swap(part))
    unroll = math.gcd(4, per_device)
    toeps = pl.pallas_call(
        blocks_kernel,
        in_specs=[smem, vmem],
        out_specs=[vmem] * unroll,
        out_shape=[
            jax.ShapeDtypeStruct((per_device // unroll, blocks + 1, LANES, LANES), BF16)
        ] * unroll,
        scratch_shapes=[pltpu.VMEM((per_device, blocks + 1, 1, LANES), F32)],
        cost_estimate=cost(1, 1),
        compiler_params=pltpu.CompilerParams(vmem_limit_bytes=16 << 20),
        name="blocks",
    )(pos, filters)
    conv = pl.pallas_call(
        functools.partial(conv_kernel, owners=owners, unroll=unroll),
        in_specs=[smem] + [vmem] * (unroll + owners),
        out_specs=[vmem] * owners,
        out_shape=[piece] * owners,
        scratch_shapes=[pltpu.VMEM((2, rows, LANES), BF16)] * (2 * unroll),
        cost_estimate=cost(per_device * rows * length * 4096, 2 * size + groups * length * 2),
        compiler_params=pltpu.CompilerParams(vmem_limit_bytes=16 << 20),
        name="conv",
    )(pos, *toeps, *grad_got)
    back = swap(conv)
    both = ("ctx", "ch")
    count = lax.axis_size(both)
    old = [conv[0]]
    for n, each in enumerate(sizes):
        last = n == len(sizes) - 1
        unroll = math.gcd(8, each)
        sums = jax.ShapeDtypeStruct((count, 4, LANES) if last else (blocks // owners, LANES), F32)
        old = pl.pallas_call(
            functools.partial(
                lag_kernel, owners=owners, unroll=unroll, scale=scale, first=sum(sizes[:n]), last=last
            ),
            in_specs=[smem] + [vmem] * (2 * owners) + ([vmem] * (owners + 1) if n else [anywhere]),
            out_specs=[vmem] * (owners + 1),
            out_shape=[lag_piece] * owners + [sums],
            input_output_aliases={2 * owners + 1 + k: k for k in range(owners)} if n else {},
            scratch_shapes=[pltpu.VMEM((2, 2 * rows, LANES), BF16)] * unroll
            + [pltpu.VMEM((2, rows, LANES), BF16)] * unroll
            + [
                pltpu.VMEM((unroll, owners, blocks // owners, LANES), F32),
                pltpu.VMEM((blocks // owners, LANES), F32),
            ],
            cost_estimate=cost(each * 2 * rows * length * 2048, 2 * size),
            compiler_params=pltpu.CompilerParams(vmem_limit_bytes=16 << 20),
            name="lags",
        )(pos, *grad_got, *prod_got[n], *old)
    *raw, spread = old
    total = lax.all_to_all(spread, both, 0, 0, tiled=True)
    raw = swap(raw)
    threshold = math.sqrt(WIDTH // GROUP * length)
    grad_q, grad_k, mark = pl.pallas_call(
        ungate_kernel,
        in_specs=[smem] + [anywhere] * (2 + owners),
        out_specs=[anywhere] * 2 + [vmem],
        out_shape=[jax.ShapeDtypeStruct(q_branch.shape, BF16)] * 2
        + [jax.ShapeDtypeStruct((8, LANES), F32)],
        scratch_shapes=[
            pltpu.VMEM((local, groups, GROUP, LANES), BF16),
            pltpu.VMEM((block_len, chans), BF16),
            pltpu.VMEM((block_len, chans), BF16),
            pltpu.VMEM((block_len, chans), BF16),
            pltpu.VMEM((block_len, chans), BF16),
            pltpu.SemaphoreType.DMA((local, owners + 2)),
            pltpu.SemaphoreType.DMA((local, 2)),
        ],
        cost_estimate=cost(2 * block_len * chans, 5 * size),
        compiler_params=pltpu.CompilerParams(vmem_limit_bytes=16 << 20),
        name="ungate",
    )(pos, q_branch, k_branch, *back)
    grad_filters = pl.pallas_call(
        functools.partial(clip_kernel, threshold=threshold),
        in_specs=[smem] + [vmem] * (2 + owners),
        out_specs=vmem,
        out_shape=jax.ShapeDtypeStruct((groups, length // owners), F32),
        scratch_shapes=[pltpu.VMEM((owners, per_device, blocks // owners, LANES), F32)],
        cost_estimate=cost(groups * length, groups * length * 4),
        compiler_params=pltpu.CompilerParams(vmem_limit_bytes=8 << 20),
        name="clip",
    )(pos, total, *raw, mark)
    return (grad_q, grad_k, grad_filters)


def solution(mesh):
    return jax.shard_map(
        on_device,
        mesh=mesh,
        in_specs=(
            P(None, "ctx", "ch"),
            P(None, "ctx", "ch"),
            P(None, "ctx", "ch"),
            P("ch", None),
            P(None, "ctx", "ch"),
        ),
        out_specs=(P(None, "ctx", "ch"), P(None, "ctx", "ch"), P("ch", "ctx")),
        check_vma=False,
    )
```

```python
import functools
import math

import jax
import jax.numpy as jnp
from jax import lax
from jax.experimental import pallas as pl
from jax.experimental.pallas import tpu as pltpu
from jax.sharding import PartitionSpec as P

WIDTH = 8192
GROUP = 16
LANES = 128
NT = (((1,), (1,)), ((), ()))
BF16, F32 = jnp.bfloat16, jnp.float32


def gate_kernel(pos_ref, left_ref, right_ref, *refs, reverse, sizes, ordered, window, peers):
    *outs, left, right, out, in_sem, out_sem = refs[ordered:]
    local, wide = left.shape[0] // LANES, left.shape[1]
    chip = jnp.right_shift(pos_ref[0], 1)
    start = {"all": 0, "far": (1 - chip) * wide, "near": chip * wide}[window]
    there = pl.ds(start if window == "all" else pl.multiple_of(start, wide), wide)
    per_device = sum(sizes)
    copies = []
    for i in range(local):
        here = pl.ds(i * LANES, LANES)
        copies.append(
            (
                pltpu.make_async_copy(left_ref.at[0, here, there], left.at[here], in_sem.at[i, 0]),
                pltpu.make_async_copy(right_ref.at[0, here, there], right.at[here], in_sem.at[i, 1]),
            )
        )
    for pair in copies:
        for copy in pair:
            copy.start()
    sends = []
    for i in range(local):
        for copy in copies[i]:
            copy.wait()
        rows = slice(i * LANES, (i + 1) * LANES)
        value = (left[rows].astype(F32) * right[rows].astype(F32)).astype(BF16)
        if reverse:
            row_id = lax.broadcasted_iota(jnp.int32, (LANES, LANES), 0)
            col_id = lax.broadcasted_iota(jnp.int32, (LANES, LANES), 1)
            flip = (row_id + col_id == LANES - 1).astype(BF16)
            value = jnp.dot(flip, value, preferred_element_type=F32).astype(BF16)
        value = value.T
        out[i % 2, i // 2] = value.reshape(out.shape[2:])
        for n, target in enumerate(outs):
            k, chunk = divmod(n, len(sizes))
            first = jnp.bitwise_xor(pos_ref[0], peers[k]) * per_device - start // GROUP + sum(sizes[:chunk])
            send = pltpu.make_async_copy(
                out.at[i % 2, i // 2, pl.ds(first, sizes[chunk])],
                target.at[:, i % 2, i // 2],
                out_sem.at[i, n],
            )
            send.start()
            sends.append(send)
    for send in sends:
        send.wait()


def ungate_kernel(pos_ref, q_ref, k_ref, *refs):
    *grads, gq_ref, gk_ref, mark_ref, grad, q_in, k_in, gq, gk, in_sem, out_sem = refs
    local = q_in.shape[0] // LANES
    per_device = grads[0].shape[0]
    owners = len(grads)
    mark_ref[...] = jnp.zeros_like(mark_ref)
    copies, sends = [], []
    for i in range(local):
        here = pl.ds(i * LANES, LANES)
        row = [
            pltpu.make_async_copy(q_ref.at[0, here], q_in.at[here], in_sem.at[i, owners]),
            pltpu.make_async_copy(k_ref.at[0, here], k_in.at[here], in_sem.at[i, owners + 1]),
        ]
        for k, source in enumerate(grads):
            first = jnp.bitwise_xor(pos_ref[0], k) * per_device
            row.append(
                pltpu.make_async_copy(
                    source.at[:, i % 2, i // 2], grad.at[i, pl.ds(first, per_device)], in_sem.at[i, k]
                )
            )
        copies.append(row)
    for row in copies:
        for copy in row:
            copy.start()
    for i in range(local):
        for copy in copies[i]:
            copy.wait()
        here = pl.ds(i * LANES, LANES)
        rows = slice(i * LANES, (i + 1) * LANES)
        value = grad[i].reshape(q_in.shape[1], LANES).T.astype(F32)
        gq[rows] = (value * k_in[rows].astype(F32)).astype(BF16)
        gk[rows] = (value * q_in[rows].astype(F32)).astype(BF16)
        for n, (source, target) in enumerate(((gq, gq_ref), (gk, gk_ref))):
            send = pltpu.make_async_copy(source.at[here], target.at[0, here], out_sem.at[i, n])
            send.start()
            sends.append(send)
    for send in sends:
        send.wait()


def clip_kernel(pos_ref, total_ref, *refs, threshold):
    *parts, _, out_ref, stage = refs
    per_device, each = stage.shape[1:3]
    for k, part in enumerate(parts):
        stage[jnp.bitwise_xor(pos_ref[0], k)] = part[...]
    total = jnp.sum(total_ref[...], axis=(0, 1, 2), keepdims=True)[0]
    factor = jnp.minimum(1.0, threshold / jnp.sqrt(total + 1e-06))
    for owner in range(stage.shape[0]):
        for n in range(each):
            rows = slice(owner * per_device, (owner + 1) * per_device)
            out_ref[rows, n * LANES : (n + 1) * LANES] = stage[owner, :, n] * factor


def spread_rows(pos_ref, sources, f, target):
    for k, source in enumerate(sources):
        count = source.shape[2] * GROUP
        at = pl.multiple_of(jnp.bitwise_xor(pos_ref[0], k) * count, count)
        for half in range(2):
            target[half, pl.ds(at, count)] = source[f, half].reshape(count, LANES)


def reverse_taps(owner, filt_ref, taps):
    per_device, blocks = taps.shape[0], taps.shape[1] - 1
    groups = filt_ref.shape[0]
    picks = max(per_device, 8)
    row_id = lax.broadcasted_iota(jnp.int32, (picks, groups), 0)
    col_id = lax.broadcasted_iota(jnp.int32, (picks, groups), 1)
    pick = (col_id == row_id + owner * per_device).astype(BF16)
    width = min((blocks + 1) * LANES, filt_ref.shape[1])
    mine = jnp.dot(pick, filt_ref[:, :width], preferred_element_type=F32).astype(BF16)
    empty = jnp.zeros((picks, LANES), BF16)
    mine = jnp.concatenate([empty, mine, empty], axis=1)
    row_id = lax.broadcasted_iota(jnp.int32, (2 * LANES, LANES), 0)
    col_id = lax.broadcasted_iota(jnp.int32, (2 * LANES, LANES), 1)
    flip = (row_id + col_id == LANES).astype(BF16)
    for block in range(blocks + 1):
        near = mine[:, block * LANES : (block + 2) * LANES]
        back = jnp.dot(near, flip, preferred_element_type=F32)
        for f in range(per_device):
            taps[f, block] = back[f : f + 1]


def build_blocks(taps, f, toep):
    row_id = lax.broadcasted_iota(jnp.int32, (LANES, LANES), 0)
    col_id = lax.broadcasted_iota(jnp.int32, (LANES, LANES), 1)
    upper = col_id >= row_id
    before = None
    for block in range(taps.shape[1]):
        tap = jnp.broadcast_to(taps[f, block], (LANES, LANES))
        rolled = pltpu.roll(tap, 0, 1, stride=1, stride_axis=0)
        if block:
            toep[block] = jnp.where(upper, before, rolled).astype(BF16)
        before = rolled


def weights(toep, pair):
    at = 2 * pair + 1
    top = jnp.concatenate([toep[at], toep[at - 1]], axis=1)
    low = jnp.concatenate([toep[at + 1], toep[at]], axis=1)
    return jnp.concatenate([top, low], axis=0)


def blocks_kernel(pos_ref, filt_ref, *refs):
    *toeps, taps = refs
    unroll = len(toeps)
    reverse_taps(pos_ref[0], filt_ref, taps)

    def some(i, carry):
        for u in range(unroll):
            toep = toeps[u].at[i]
            toep[0] = jnp.zeros((LANES, LANES), BF16)
            build_blocks(taps, i * unroll + u, toep)
        return carry

    lax.fori_loop(0, toeps[0].shape[0], some, 0)


def conv_kernel(pos_ref, *refs, owners, unroll):
    toeps, refs = refs[:unroll], refs[unroll:]
    ins, outs, refs = refs[:owners], refs[owners : 2 * owners], refs[2 * owners :]
    pads, accs = refs[:unroll], refs[unroll:]
    per_device, blocks = ins[0].shape[0], toeps[0].shape[1] - 1
    rows = pads[0].shape[1]

    def one(toep, pad, out):
        acc = jnp.zeros((rows, 2 * LANES), F32)
        for pair in range(blocks // 2):
            start = pair * GROUP
            left = jnp.concatenate([pad[0, start:], pad[1, start:]], axis=1)
            part = jnp.dot(left, weights(toep, pair), preferred_element_type=F32)
            if start:
                part = jnp.concatenate([part, jnp.zeros((start, 2 * LANES), F32)], axis=0)
            acc = acc + part
        for half in range(2):
            out[half] = acc[:, half * LANES : (half + 1) * LANES].astype(BF16)

    def some(i, carry):
        for u in range(unroll):
            spread_rows(pos_ref, ins, i * unroll + u, pads[u])
        for u in range(unroll):
            one(toeps[u].at[i], pads[u], accs[u])
        for u in range(unroll):
            for k, target in enumerate(outs):
                count = target.shape[2] * GROUP
                at = pl.multiple_of(jnp.bitwise_xor(pos_ref[0], k) * count, count)
                for half in range(2):
                    value = accs[u][half, pl.ds(at, count)]
                    target[i * unroll + u, half] = value.reshape(target.shape[2:])
        return carry

    lax.fori_loop(0, per_device // unroll, some, 0)


def lag_sums(pad, flipped, rows, blocks):
    row_id = lax.broadcasted_iota(jnp.int32, (LANES, LANES), 0)
    col_id = lax.broadcasted_iota(jnp.int32, (LANES, LANES), 1)
    wraps = col_id <= row_id
    prod = jnp.concatenate([flipped[half, :rows].T for half in range(2)], axis=1)
    after = jnp.zeros((LANES, LANES), F32)
    sums = {}
    for pair in reversed(range(blocks // 2)):
        start = pair * GROUP
        here, later = slice(start, start + rows), slice(start + GROUP, start + GROUP + rows)
        even = jnp.concatenate([pad[0, here], pad[1, here]], axis=0)
        odd = jnp.concatenate([pad[1, here], pad[0, later]], axis=0)
        both = jnp.dot(prod, jnp.concatenate([even, odd], axis=1), preferred_element_type=F32)
        for half in (1, 0):
            rolled = pltpu.roll(
                both[:, half * LANES : (half + 1) * LANES], 1, 1, stride=1, stride_axis=0
            )
            part = jnp.where(wraps, rolled, after)
            sums[2 * pair + half] = jnp.sum(part, axis=0, keepdims=True)
            after = rolled
    return sums


def lag_kernel(pos_ref, *refs, owners, unroll, scale, first, last):
    grads, prods, refs = refs[:owners], refs[owners : 2 * owners], refs[2 * owners :]
    olds, refs = (refs[: owners + 1], refs[owners + 1 :]) if first else ([], refs[1:])
    raws, sum_ref, refs = refs[:owners], refs[owners], refs[owners + 1 :]
    pads, flips, lags_v, sq_v = refs[:unroll], refs[unroll : 2 * unroll], refs[-2], refs[-1]
    per_owner = raws[0].shape[1]
    blocks = owners * per_owner
    rows = flips[0].shape[1]
    for pad in pads:
        pad[:, rows:] = jnp.zeros((2, rows, LANES), BF16)
    sq_v[...] = olds[-1][...] if olds else jnp.zeros_like(sq_v)

    def one(slot, pad, flipped):
        sums = lag_sums(pad, flipped, rows, blocks)
        for owner in range(owners):
            lags = jnp.concatenate(
                [sums[owner * per_owner + n] for n in range(per_owner)], axis=0
            ) * scale
            lags_v[slot, owner] = lags
            sq_v[...] += lags * lags

    def some(i, carry):
        for u in range(unroll):
            spread_rows(pos_ref, grads, first + i * unroll + u, pads[u])
            spread_rows(pos_ref, prods, i * unroll + u, flips[u])
        for u in range(unroll):
            one(u, pads[u], flips[u])
        for u in range(unroll):
            for k, target in enumerate(raws):
                target[first + i * unroll + u] = lags_v[u, jnp.bitwise_xor(pos_ref[0], k)]
        return carry

    lax.fori_loop(0, prods[0].shape[0] // unroll, some, 0)
    if not last:
        sum_ref[...] = sq_v[...]
        return
    squares = jnp.sum(sq_v[...], axis=0, keepdims=True)
    sum_ref[...] = jnp.zeros_like(sum_ref)
    sum_ref[:, :1] = jnp.broadcast_to(squares[None], (sum_ref.shape[0], 1, LANES))


def in_hbm(value):
    return pltpu.with_memory_space_constraint(value, pltpu.HBM)


def cost(flops, moved):
    return pl.CostEstimate(flops=int(flops), bytes_accessed=int(moved), transcendentals=0)


def on_device(q_branch, k_branch, out_gate, filters, grad_out):
    seqs, block_len, chans = q_branch.shape
    owners = lax.axis_size("ctx")
    groups = chans // GROUP
    per_device = groups // owners
    local = block_len // LANES
    length = owners * block_len
    blocks = length // LANES
    rows = length * GROUP // (2 * LANES)
    scale = 4.0 / math.sqrt(seqs * GROUP)
    size = block_len * chans * 2
    anywhere = pl.BlockSpec(memory_space=pl.ANY)
    vmem = pl.BlockSpec(memory_space=pltpu.VMEM)
    smem = pl.BlockSpec(memory_space=pltpu.SMEM)
    tail = (2, local // 2, GROUP, LANES)
    whole = (owners, per_device) + tail
    pos = lax.axis_index("ctx").astype(jnp.int32).reshape(1)
    piece = jax.ShapeDtypeStruct((per_device,) + tail, BF16)
    lag_piece = jax.ShapeDtypeStruct((per_device, blocks // owners, LANES), F32)

    def gate(left, right, after, reverse, sizes, limit, name, window="all", peers=None):
        peers = peers or tuple(range(owners))
        wide = chans if window == "all" else chans // 2
        parts = [jax.ShapeDtypeStruct((n,) + tail, BF16) for n in sizes]
        out = pl.pallas_call(
            functools.partial(
                gate_kernel,
                reverse=reverse,
                sizes=sizes,
                ordered=len(after),
                window=window,
                peers=peers,
            ),
            in_specs=[smem] + [pl.BlockSpec(memory_space=pltpu.HBM)] * 2 + [vmem] * len(after),
            out_specs=[anywhere] * (len(peers) * len(sizes)),
            out_shape=parts * len(peers),
            scratch_shapes=[
                pltpu.VMEM((block_len, wide), BF16),
                pltpu.VMEM((block_len, wide), BF16),
                pltpu.VMEM((2, local // 2, wide // GROUP, GROUP, LANES), BF16),
                pltpu.SemaphoreType.DMA((local, 2)),
                pltpu.SemaphoreType.DMA((local, len(peers) * len(sizes))),
            ],
            cost_estimate=cost(block_len * wide, 6 * block_len * wide),
            compiler_params=pltpu.CompilerParams(vmem_limit_bytes=limit << 20),
            name=name,
        )(pos, left, right, *after)
        return [out[n :: len(sizes)] for n in range(len(sizes))]

    def swap(values):
        out = [values[0]]
        for k in range(1, owners):
            out.append(lax.ppermute(values[k], "ctx", [(i, i ^ k) for i in range(owners)]))
        return out

    sizes = (8, 8) if per_device == 16 else (per_device,)
    if owners == 4:
        (far,) = gate(
            in_hbm(grad_out), in_hbm(out_gate), (), False, (per_device,), 12, "gate_far", "far", (2, 3)
        )
        far_send = far
        far = [lax.ppermute(v, "ctx", [(i, i ^ k) for i in range(4)]) for k, v in zip((2, 3), far)]
        prod_send = gate(in_hbm(q_branch), in_hbm(k_branch), (), True, sizes, 12, "gate_prod")
        (near,) = gate(
            grad_out, out_gate, prod_send[0][:1], False, (per_device,), 12, "gate_near", "near", (0, 1)
        )
        grad_got = [near[0], lax.ppermute(near[1], "ctx", [(i, i ^ 1) for i in range(4)]), *far]
    else:
        (grad_send,) = gate(grad_out, out_gate, (), False, (per_device,), 56, "gate_grad")
        grad_got = swap(grad_send)
        prod_send = gate(q_branch, k_branch, grad_send[:1], True, sizes, 12, "gate_prod")
    first_got = swap(prod_send[0])
    unroll = math.gcd(4, per_device)
    toeps = pl.pallas_call(
        blocks_kernel,
        in_specs=[smem, vmem],
        out_specs=[vmem] * unroll,
        out_shape=[
            jax.ShapeDtypeStruct((per_device // unroll, blocks + 1, LANES, LANES), BF16)
        ] * unroll,
        scratch_shapes=[pltpu.VMEM((per_device, blocks + 1, 1, LANES), F32)],
        cost_estimate=cost(1, 1),
        compiler_params=pltpu.CompilerParams(vmem_limit_bytes=16 << 20),
        name="blocks",
    )(pos, filters)
    conv = pl.pallas_call(
        functools.partial(conv_kernel, owners=owners, unroll=unroll),
        in_specs=[smem] + [vmem] * (unroll + owners),
        out_specs=[vmem] * owners,
        out_shape=[piece] * owners,
        scratch_shapes=[pltpu.VMEM((2, rows, LANES), BF16)] * (2 * unroll),
        cost_estimate=cost(per_device * rows * length * 4096, 2 * size + groups * length * 2),
        compiler_params=pltpu.CompilerParams(vmem_limit_bytes=16 << 20),
        name="conv",
    )(pos, *toeps, *grad_got)
    conv, prod_got = list(conv), [first_got]
    for part in prod_send[1:]:
        part, conv[0] = lax.optimization_barrier((part, conv[0]))
        prod_got.append(swap(part))
    back = swap(conv)
    both = ("ctx", "ch")
    count = lax.axis_size(both)
    old = [conv[0]]
    for n, each in enumerate(sizes):
        last = n == len(sizes) - 1
        unroll = math.gcd(8, each)
        sums = jax.ShapeDtypeStruct((count, 4, LANES) if last else (blocks // owners, LANES), F32)
        old = pl.pallas_call(
            functools.partial(
                lag_kernel, owners=owners, unroll=unroll, scale=scale, first=sum(sizes[:n]), last=last
            ),
            in_specs=[smem] + [vmem] * (2 * owners) + ([vmem] * (owners + 1) if n else [anywhere]),
            out_specs=[vmem] * (owners + 1),
            out_shape=[lag_piece] * owners + [sums],
            input_output_aliases={2 * owners + 1 + k: k for k in range(owners)} if n else {},
            scratch_shapes=[pltpu.VMEM((2, 2 * rows, LANES), BF16)] * unroll
            + [pltpu.VMEM((2, rows, LANES), BF16)] * unroll
            + [
                pltpu.VMEM((unroll, owners, blocks // owners, LANES), F32),
                pltpu.VMEM((blocks // owners, LANES), F32),
            ],
            cost_estimate=cost(each * 2 * rows * length * 2048, 2 * size),
            compiler_params=pltpu.CompilerParams(vmem_limit_bytes=16 << 20),
            name="lags",
        )(pos, *grad_got, *prod_got[n], *old)
    *raw, spread = old
    total = lax.all_to_all(spread, both, 0, 0, tiled=True)
    raw = swap(raw)
    threshold = math.sqrt(WIDTH // GROUP * length)
    grad_q, grad_k, mark = pl.pallas_call(
        ungate_kernel,
        in_specs=[smem] + [anywhere] * (2 + owners),
        out_specs=[anywhere] * 2 + [vmem],
        out_shape=[jax.ShapeDtypeStruct(q_branch.shape, BF16)] * 2
        + [jax.ShapeDtypeStruct((8, LANES), F32)],
        scratch_shapes=[
            pltpu.VMEM((local, groups, GROUP, LANES), BF16),
            pltpu.VMEM((block_len, chans), BF16),
            pltpu.VMEM((block_len, chans), BF16),
            pltpu.VMEM((block_len, chans), BF16),
            pltpu.VMEM((block_len, chans), BF16),
            pltpu.SemaphoreType.DMA((local, owners + 2)),
            pltpu.SemaphoreType.DMA((local, 2)),
        ],
        cost_estimate=cost(2 * block_len * chans, 5 * size),
        compiler_params=pltpu.CompilerParams(vmem_limit_bytes=16 << 20),
        name="ungate",
    )(pos, q_branch, k_branch, *back)
    grad_filters = pl.pallas_call(
        functools.partial(clip_kernel, threshold=threshold),
        in_specs=[smem] + [vmem] * (2 + owners),
        out_specs=vmem,
        out_shape=jax.ShapeDtypeStruct((groups, length // owners), F32),
        scratch_shapes=[pltpu.VMEM((owners, per_device, blocks // owners, LANES), F32)],
        cost_estimate=cost(groups * length, groups * length * 4),
        compiler_params=pltpu.CompilerParams(vmem_limit_bytes=8 << 20),
        name="clip",
    )(pos, total, *raw, mark)
    return (grad_q, grad_k, grad_filters)


def solution(mesh):
    return jax.shard_map(
        on_device,
        mesh=mesh,
        in_specs=(
            P(None, "ctx", "ch"),
            P(None, "ctx", "ch"),
            P(None, "ctx", "ch"),
            P("ch", None),
            P(None, "ctx", "ch"),
        ),
        out_specs=(P(None, "ctx", "ch"), P(None, "ctx", "ch"), P("ch", "ctx")),
        check_vma=False,
    )
```

```python
import functools
import math

import jax
import jax.numpy as jnp
from jax import lax
from jax.experimental import pallas as pl
from jax.experimental.pallas import tpu as pltpu
from jax.sharding import PartitionSpec as P

WIDTH = 8192
GROUP = 16
LANES = 128
NT = (((1,), (1,)), ((), ()))
BF16, F32 = jnp.bfloat16, jnp.float32


def gate_kernel(pos_ref, left_ref, right_ref, *refs, reverse, sizes, ordered, window, peers):
    *outs, left, right, out, in_sem, out_sem = refs[ordered:]
    local, wide = left.shape[0] // LANES, left.shape[1]
    chip = jnp.right_shift(pos_ref[0], 1)
    start = {"all": 0, "far": (1 - chip) * wide, "near": chip * wide}[window]
    there = pl.ds(start if window == "all" else pl.multiple_of(start, wide), wide)
    per_device = sum(sizes)
    copies = []
    for i in range(local):
        here = pl.ds(i * LANES, LANES)
        copies.append(
            (
                pltpu.make_async_copy(left_ref.at[0, here, there], left.at[here], in_sem.at[i, 0]),
                pltpu.make_async_copy(right_ref.at[0, here, there], right.at[here], in_sem.at[i, 1]),
            )
        )
    for pair in copies:
        for copy in pair:
            copy.start()
    sends = []
    for i in range(local):
        for copy in copies[i]:
            copy.wait()
        rows = slice(i * LANES, (i + 1) * LANES)
        value = (left[rows].astype(F32) * right[rows].astype(F32)).astype(BF16)
        if reverse:
            row_id = lax.broadcasted_iota(jnp.int32, (LANES, LANES), 0)
            col_id = lax.broadcasted_iota(jnp.int32, (LANES, LANES), 1)
            flip = (row_id + col_id == LANES - 1).astype(BF16)
            value = jnp.dot(flip, value, preferred_element_type=F32).astype(BF16)
        value = value.T
        out[i % 2, i // 2] = value.reshape(out.shape[2:])
        for n, target in enumerate(outs):
            k, chunk = divmod(n, len(sizes))
            first = jnp.bitwise_xor(pos_ref[0], peers[k]) * per_device - start // GROUP + sum(sizes[:chunk])
            send = pltpu.make_async_copy(
                out.at[i % 2, i // 2, pl.ds(first, sizes[chunk])],
                target.at[:, i % 2, i // 2],
                out_sem.at[i, n],
            )
            send.start()
            sends.append(send)
    for send in sends:
        send.wait()


def ungate_kernel(pos_ref, q_ref, k_ref, *refs):
    *grads, gq_ref, gk_ref, mark_ref, grad, q_in, k_in, gq, gk, in_sem, out_sem = refs
    local = q_in.shape[0] // LANES
    per_device = grads[0].shape[0]
    owners = len(grads)
    mark_ref[...] = jnp.zeros_like(mark_ref)
    copies, sends = [], []
    for i in range(local):
        here = pl.ds(i * LANES, LANES)
        row = [
            pltpu.make_async_copy(q_ref.at[0, here], q_in.at[here], in_sem.at[i, owners]),
            pltpu.make_async_copy(k_ref.at[0, here], k_in.at[here], in_sem.at[i, owners + 1]),
        ]
        for k, source in enumerate(grads):
            first = jnp.bitwise_xor(pos_ref[0], k) * per_device
            row.append(
                pltpu.make_async_copy(
                    source.at[:, i % 2, i // 2], grad.at[i, pl.ds(first, per_device)], in_sem.at[i, k]
                )
            )
        copies.append(row)
    for row in copies:
        for copy in row:
            copy.start()
    for i in range(local):
        for copy in copies[i]:
            copy.wait()
        here = pl.ds(i * LANES, LANES)
        rows = slice(i * LANES, (i + 1) * LANES)
        value = grad[i].reshape(q_in.shape[1], LANES).T.astype(F32)
        gq[rows] = (value * k_in[rows].astype(F32)).astype(BF16)
        gk[rows] = (value * q_in[rows].astype(F32)).astype(BF16)
        for n, (source, target) in enumerate(((gq, gq_ref), (gk, gk_ref))):
            send = pltpu.make_async_copy(source.at[here], target.at[0, here], out_sem.at[i, n])
            send.start()
            sends.append(send)
    for send in sends:
        send.wait()


def clip_kernel(pos_ref, total_ref, *refs, threshold):
    *parts, _, out_ref, stage = refs
    per_device, each = stage.shape[1:3]
    for k, part in enumerate(parts):
        stage[jnp.bitwise_xor(pos_ref[0], k)] = part[...]
    total = jnp.sum(total_ref[...], axis=(0, 1, 2), keepdims=True)[0]
    factor = jnp.minimum(1.0, threshold / jnp.sqrt(total + 1e-06))
    for owner in range(stage.shape[0]):
        for n in range(each):
            rows = slice(owner * per_device, (owner + 1) * per_device)
            out_ref[rows, n * LANES : (n + 1) * LANES] = stage[owner, :, n] * factor


def spread_rows(pos_ref, sources, f, target):
    for k, source in enumerate(sources):
        count = source.shape[2] * GROUP
        at = pl.multiple_of(jnp.bitwise_xor(pos_ref[0], k) * count, count)
        for half in range(2):
            target[half, pl.ds(at, count)] = source[f, half].reshape(count, LANES)


def reverse_taps(owner, filt_ref, taps):
    per_device, blocks = taps.shape[0], taps.shape[1] - 1
    groups = filt_ref.shape[0]
    picks = max(per_device, 8)
    row_id = lax.broadcasted_iota(jnp.int32, (picks, groups), 0)
    col_id = lax.broadcasted_iota(jnp.int32, (picks, groups), 1)
    pick = (col_id == row_id + owner * per_device).astype(BF16)
    width = min((blocks + 1) * LANES, filt_ref.shape[1])
    mine = jnp.dot(pick, filt_ref[:, :width], preferred_element_type=F32).astype(BF16)
    empty = jnp.zeros((picks, LANES), BF16)
    mine = jnp.concatenate([empty, mine, empty], axis=1)
    row_id = lax.broadcasted_iota(jnp.int32, (2 * LANES, LANES), 0)
    col_id = lax.broadcasted_iota(jnp.int32, (2 * LANES, LANES), 1)
    flip = (row_id + col_id == LANES).astype(BF16)
    for block in range(blocks + 1):
        near = mine[:, block * LANES : (block + 2) * LANES]
        back = jnp.dot(near, flip, preferred_element_type=F32)
        for f in range(per_device):
            taps[f, block] = back[f : f + 1]


def build_blocks(taps, f, toep):
    row_id = lax.broadcasted_iota(jnp.int32, (LANES, LANES), 0)
    col_id = lax.broadcasted_iota(jnp.int32, (LANES, LANES), 1)
    upper = col_id >= row_id
    before = None
    for block in range(taps.shape[1]):
        tap = jnp.broadcast_to(taps[f, block], (LANES, LANES))
        rolled = pltpu.roll(tap, 0, 1, stride=1, stride_axis=0)
        if block:
            toep[block] = jnp.where(upper, before, rolled).astype(BF16)
        before = rolled


def weights(toep, pair):
    at = 2 * pair + 1
    top = jnp.concatenate([toep[at], toep[at - 1]], axis=1)
    low = jnp.concatenate([toep[at + 1], toep[at]], axis=1)
    return jnp.concatenate([top, low], axis=0)


def blocks_kernel(pos_ref, filt_ref, *refs):
    *toeps, taps = refs
    unroll = len(toeps)
    reverse_taps(pos_ref[0], filt_ref, taps)

    def some(i, carry):
        for u in range(unroll):
            toep = toeps[u].at[i]
            toep[0] = jnp.zeros((LANES, LANES), BF16)
            build_blocks(taps, i * unroll + u, toep)
        return carry

    lax.fori_loop(0, toeps[0].shape[0], some, 0)


def conv_kernel(pos_ref, *refs, owners, unroll):
    toeps, refs = refs[:unroll], refs[unroll:]
    ins, outs, refs = refs[:owners], refs[owners : 2 * owners], refs[2 * owners :]
    pads, accs = refs[:unroll], refs[unroll:]
    per_device, blocks = ins[0].shape[0], toeps[0].shape[1] - 1
    rows = pads[0].shape[1]

    def one(toep, pad, out):
        acc = jnp.zeros((rows, 2 * LANES), F32)
        for pair in range(blocks // 2):
            start = pair * GROUP
            left = jnp.concatenate([pad[0, start:], pad[1, start:]], axis=1)
            part = jnp.dot(left, weights(toep, pair), preferred_element_type=F32)
            if start:
                part = jnp.concatenate([part, jnp.zeros((start, 2 * LANES), F32)], axis=0)
            acc = acc + part
        for half in range(2):
            out[half] = acc[:, half * LANES : (half + 1) * LANES].astype(BF16)

    def some(i, carry):
        for u in range(unroll):
            spread_rows(pos_ref, ins, i * unroll + u, pads[u])
        for u in range(unroll):
            one(toeps[u].at[i], pads[u], accs[u])
        for u in range(unroll):
            for k, target in enumerate(outs):
                count = target.shape[2] * GROUP
                at = pl.multiple_of(jnp.bitwise_xor(pos_ref[0], k) * count, count)
                for half in range(2):
                    value = accs[u][half, pl.ds(at, count)]
                    target[i * unroll + u, half] = value.reshape(target.shape[2:])
        return carry

    lax.fori_loop(0, per_device // unroll, some, 0)


def lag_sums(pad, flipped, rows, blocks):
    row_id = lax.broadcasted_iota(jnp.int32, (LANES, LANES), 0)
    col_id = lax.broadcasted_iota(jnp.int32, (LANES, LANES), 1)
    wraps = col_id <= row_id
    prod = jnp.concatenate([flipped[half, :rows].T for half in range(2)], axis=1)
    after = jnp.zeros((LANES, LANES), F32)
    sums = {}
    for pair in reversed(range(blocks // 2)):
        start = pair * GROUP
        here, later = slice(start, start + rows), slice(start + GROUP, start + GROUP + rows)
        even = jnp.concatenate([pad[0, here], pad[1, here]], axis=0)
        odd = jnp.concatenate([pad[1, here], pad[0, later]], axis=0)
        both = jnp.dot(prod, jnp.concatenate([even, odd], axis=1), preferred_element_type=F32)
        for half in (1, 0):
            rolled = pltpu.roll(
                both[:, half * LANES : (half + 1) * LANES], 1, 1, stride=1, stride_axis=0
            )
            part = jnp.where(wraps, rolled, after)
            sums[2 * pair + half] = jnp.sum(part, axis=0, keepdims=True)
            after = rolled
    return sums


def lag_kernel(pos_ref, *refs, owners, unroll, scale, first, last):
    grads, prods, refs = refs[:owners], refs[owners : 2 * owners], refs[2 * owners :]
    olds, refs = (refs[: owners + 1], refs[owners + 1 :]) if first else ([], refs[1:])
    raws, sum_ref, refs = refs[:owners], refs[owners], refs[owners + 1 :]
    pads, flips, lags_v, sq_v = refs[:unroll], refs[unroll : 2 * unroll], refs[-2], refs[-1]
    per_owner = raws[0].shape[1]
    blocks = owners * per_owner
    rows = flips[0].shape[1]
    for pad in pads:
        pad[:, rows:] = jnp.zeros((2, rows, LANES), BF16)
    sq_v[...] = olds[-1][...] if olds else jnp.zeros_like(sq_v)

    def one(slot, pad, flipped):
        sums = lag_sums(pad, flipped, rows, blocks)
        for owner in range(owners):
            lags = jnp.concatenate(
                [sums[owner * per_owner + n] for n in range(per_owner)], axis=0
            ) * scale
            lags_v[slot, owner] = lags
            sq_v[...] += lags * lags

    def some(i, carry):
        for u in range(unroll):
            spread_rows(pos_ref, grads, first + i * unroll + u, pads[u])
            spread_rows(pos_ref, prods, i * unroll + u, flips[u])
        for u in range(unroll):
            one(u, pads[u], flips[u])
        for u in range(unroll):
            for k, target in enumerate(raws):
                target[first + i * unroll + u] = lags_v[u, jnp.bitwise_xor(pos_ref[0], k)]
        return carry

    lax.fori_loop(0, prods[0].shape[0] // unroll, some, 0)
    if not last:
        sum_ref[...] = sq_v[...]
        return
    squares = jnp.sum(sq_v[...], axis=0, keepdims=True)
    sum_ref[...] = jnp.zeros_like(sum_ref)
    sum_ref[:, :1] = jnp.broadcast_to(squares[None], (sum_ref.shape[0], 1, LANES))


def in_hbm(value):
    return pltpu.with_memory_space_constraint(value, pltpu.HBM)


def cost(flops, moved):
    return pl.CostEstimate(flops=int(flops), bytes_accessed=int(moved), transcendentals=0)


def on_device(q_branch, k_branch, out_gate, filters, grad_out):
    seqs, block_len, chans = q_branch.shape
    owners = lax.axis_size("ctx")
    groups = chans // GROUP
    per_device = groups // owners
    local = block_len // LANES
    length = owners * block_len
    blocks = length // LANES
    rows = length * GROUP // (2 * LANES)
    scale = 4.0 / math.sqrt(seqs * GROUP)
    size = block_len * chans * 2
    anywhere = pl.BlockSpec(memory_space=pl.ANY)
    vmem = pl.BlockSpec(memory_space=pltpu.VMEM)
    smem = pl.BlockSpec(memory_space=pltpu.SMEM)
    tail = (2, local // 2, GROUP, LANES)
    whole = (owners, per_device) + tail
    pos = lax.axis_index("ctx").astype(jnp.int32).reshape(1)
    piece = jax.ShapeDtypeStruct((per_device,) + tail, BF16)
    lag_piece = jax.ShapeDtypeStruct((per_device, blocks // owners, LANES), F32)

    def gate(left, right, after, reverse, sizes, limit, name, window="all", peers=None):
        peers = peers or tuple(range(owners))
        wide = chans if window == "all" else chans // 2
        parts = [jax.ShapeDtypeStruct((n,) + tail, BF16) for n in sizes]
        out = pl.pallas_call(
            functools.partial(
                gate_kernel,
                reverse=reverse,
                sizes=sizes,
                ordered=len(after),
                window=window,
                peers=peers,
            ),
            in_specs=[smem] + [pl.BlockSpec(memory_space=pltpu.HBM)] * 2 + [vmem] * len(after),
            out_specs=[anywhere] * (len(peers) * len(sizes)),
            out_shape=parts * len(peers),
            scratch_shapes=[
                pltpu.VMEM((block_len, wide), BF16),
                pltpu.VMEM((block_len, wide), BF16),
                pltpu.VMEM((2, local // 2, wide // GROUP, GROUP, LANES), BF16),
                pltpu.SemaphoreType.DMA((local, 2)),
                pltpu.SemaphoreType.DMA((local, len(peers) * len(sizes))),
            ],
            cost_estimate=cost(block_len * wide, 6 * block_len * wide),
            compiler_params=pltpu.CompilerParams(vmem_limit_bytes=limit << 20),
            name=name,
        )(pos, left, right, *after)
        return [out[n :: len(sizes)] for n in range(len(sizes))]

    def swap(values):
        out = [values[0]]
        for k in range(1, owners):
            out.append(lax.ppermute(values[k], "ctx", [(i, i ^ k) for i in range(owners)]))
        return out

    sizes = (8, 8) if per_device == 16 else (per_device,)
    if owners == 4:
        (far,) = gate(
            in_hbm(grad_out), in_hbm(out_gate), (), False, (per_device,), 12, "gate_far", "far", (2, 3)
        )
        far_send = far
        far = [lax.ppermute(v, "ctx", [(i, i ^ k) for i in range(4)]) for k, v in zip((2, 3), far)]
        prod_send = gate(in_hbm(q_branch), in_hbm(k_branch), (), True, sizes, 12, "gate_prod")
        (near,) = gate(
            grad_out, out_gate, prod_send[0][:1], False, (per_device,), 12, "gate_near", "near", (0, 1)
        )
        grad_got = [near[0], lax.ppermute(near[1], "ctx", [(i, i ^ 1) for i in range(4)]), *far]
    else:
        (grad_send,) = gate(grad_out, out_gate, (), False, (per_device,), 56, "gate_grad")
        grad_got = swap(grad_send)
        prod_send = gate(q_branch, k_branch, grad_send[:1], True, sizes, 12, "gate_prod")
    prod_got = []
    for part in prod_send:
        if prod_got:
            part, prod_got[-1][1] = lax.optimization_barrier((part, prod_got[-1][1]))
        prod_got.append(swap(part))
    unroll = math.gcd(4, per_device)
    toeps = pl.pallas_call(
        blocks_kernel,
        in_specs=[smem, vmem],
        out_specs=[vmem] * unroll,
        out_shape=[
            jax.ShapeDtypeStruct((per_device // unroll, blocks + 1, LANES, LANES), BF16)
        ] * unroll,
        scratch_shapes=[pltpu.VMEM((per_device, blocks + 1, 1, LANES), F32)],
        cost_estimate=cost(1, 1),
        compiler_params=pltpu.CompilerParams(vmem_limit_bytes=16 << 20),
        name="blocks",
    )(pos, filters)
    conv = pl.pallas_call(
        functools.partial(conv_kernel, owners=owners, unroll=unroll),
        in_specs=[smem] + [vmem] * (unroll + owners),
        out_specs=[vmem] * owners,
        out_shape=[piece] * owners,
        scratch_shapes=[pltpu.VMEM((2, rows, LANES), BF16)] * (2 * unroll),
        cost_estimate=cost(per_device * rows * length * 4096, 2 * size + groups * length * 2),
        compiler_params=pltpu.CompilerParams(vmem_limit_bytes=16 << 20),
        name="conv",
    )(pos, *toeps, *grad_got)
    back = swap(conv)
    both = ("ctx", "ch")
    count = lax.axis_size(both)
    old = [conv[0]]
    for n, each in enumerate(sizes):
        last = n == len(sizes) - 1
        unroll = math.gcd(4, each)
        sums = jax.ShapeDtypeStruct((count, 4, LANES) if last else (blocks // owners, LANES), F32)
        old = pl.pallas_call(
            functools.partial(
                lag_kernel, owners=owners, unroll=unroll, scale=scale, first=sum(sizes[:n]), last=last
            ),
            in_specs=[smem] + [vmem] * (2 * owners) + ([vmem] * (owners + 1) if n else [anywhere]),
            out_specs=[vmem] * (owners + 1),
            out_shape=[lag_piece] * owners + [sums],
            input_output_aliases={2 * owners + 1 + k: k for k in range(owners)} if n else {},
            scratch_shapes=[pltpu.VMEM((2, 2 * rows, LANES), BF16)] * unroll
            + [pltpu.VMEM((2, rows, LANES), BF16)] * unroll
            + [
                pltpu.VMEM((unroll, owners, blocks // owners, LANES), F32),
                pltpu.VMEM((blocks // owners, LANES), F32),
            ],
            cost_estimate=cost(each * 2 * rows * length * 2048, 2 * size),
            compiler_params=pltpu.CompilerParams(vmem_limit_bytes=16 << 20),
            name="lags",
        )(pos, *grad_got, *prod_got[n], *old)
    *raw, spread = old
    total = lax.all_to_all(spread, both, 0, 0, tiled=True)
    raw = swap(raw)
    threshold = math.sqrt(WIDTH // GROUP * length)
    grad_q, grad_k, mark = pl.pallas_call(
        ungate_kernel,
        in_specs=[smem] + [anywhere] * (2 + owners),
        out_specs=[anywhere] * 2 + [vmem],
        out_shape=[jax.ShapeDtypeStruct(q_branch.shape, BF16)] * 2
        + [jax.ShapeDtypeStruct((8, LANES), F32)],
        scratch_shapes=[
            pltpu.VMEM((local, groups, GROUP, LANES), BF16),
            pltpu.VMEM((block_len, chans), BF16),
            pltpu.VMEM((block_len, chans), BF16),
            pltpu.VMEM((block_len, chans), BF16),
            pltpu.VMEM((block_len, chans), BF16),
            pltpu.SemaphoreType.DMA((local, owners + 2)),
            pltpu.SemaphoreType.DMA((local, 2)),
        ],
        cost_estimate=cost(2 * block_len * chans, 5 * size),
        compiler_params=pltpu.CompilerParams(vmem_limit_bytes=16 << 20),
        name="ungate",
    )(pos, q_branch, k_branch, *back)
    grad_filters = pl.pallas_call(
        functools.partial(clip_kernel, threshold=threshold),
        in_specs=[smem] + [vmem] * (2 + owners),
        out_specs=vmem,
        out_shape=jax.ShapeDtypeStruct((groups, length // owners), F32),
        scratch_shapes=[pltpu.VMEM((owners, per_device, blocks // owners, LANES), F32)],
        cost_estimate=cost(groups * length, groups * length * 4),
        compiler_params=pltpu.CompilerParams(vmem_limit_bytes=8 << 20),
        name="clip",
    )(pos, total, *raw, mark)
    return (grad_q, grad_k, grad_filters)


def solution(mesh):
    return jax.shard_map(
        on_device,
        mesh=mesh,
        in_specs=(
            P(None, "ctx", "ch"),
            P(None, "ctx", "ch"),
            P(None, "ctx", "ch"),
            P("ch", None),
            P(None, "ctx", "ch"),
        ),
        out_specs=(P(None, "ctx", "ch"), P(None, "ctx", "ch"), P("ch", "ctx")),
        check_vma=False,
    )
```
